32 devices in a mesh: seq: 4 (over x, core), fsdp: 8 (over z, y).
Axes of the slice: x: 2, y: 2, z: 4, core: 2. Of those that a mesh axis runs over, the one named last changes fastest.
Arguments:
- latents: bfloat16 [8, 1024, 1152], P('fsdp', 'seq'), may hold values from -6 to 6
- timesteps: int32 [8], P('fsdp'), may hold values from 0 to 999
- labels: int32 [8], P('fsdp'), may hold values from 0 to 999
- upstream: bfloat16 [8, 1024, 1152], P('fsdp', 'seq'), may hold values from -6 to 6
- time_first: float32 [256, 1152], P('fsdp'), may hold values from -0.375 to 0.375
- time_second: float32 [1152, 1152], P('fsdp'), may hold values from -0.1875 to 0.1875
- class_table: float32 [1000, 1152], P(None, 'fsdp'), may hold values from -1.25 to 1.25
- modulation: float32 [1152, 6912], P(None, 'fsdp'), may hold values from -0.1875 to 0.1875
- attend_in: float32 [1152, 3456], P('fsdp'), may hold values from -0.1875 to 0.1875
- attend_out: float32 [1152, 1152], P('fsdp'), may hold values from -2 to 2
- expand: float32 [1152, 4608], P('fsdp'), may hold values from -0.1875 to 0.1875
- contract: float32 [4608, 1152], P('fsdp'), may hold values from -0.09375 to 0.09375
- biases: float32 [18432], P('fsdp'), may hold values from -1.25 to 1.25
- moment_time_first: float32 [256, 1152], P('fsdp'), may hold values from -0.00012207031 to 0.00012207031
- moment_time_second: float32 [1152, 1152], P('fsdp'), may hold values from -0.00012207031 to 0.00012207031
- moment_class_table: float32 [1000, 1152], P(None, 'fsdp'), may hold values from -0.00012207031 to 0.00012207031
- moment_modulation: float32 [1152, 6912], P(None, 'fsdp'), may hold values from -0.00012207031 to 0.00012207031
- moment_attend_in: float32 [1152, 3456], P('fsdp'), may hold values from -0.00012207031 to 0.00012207031
- moment_attend_out: float32 [1152, 1152], P('fsdp'), may hold values from -0.00012207031 to 0.00012207031
- moment_expand: float32 [1152, 4608], P('fsdp'), may hold values from -0.00012207031 to 0.00012207031
- moment_contract: float32 [4608, 1152], P('fsdp'), may hold values from -0.00012207031 to 0.00012207031
- moment_biases: float32 [18432], P('fsdp'), may hold values from -0.00012207031 to 0.00012207031
- square_time_first: float32 [256, 1152], P('fsdp'), may hold values from 1e-12 to 1e-10
- square_time_second: float32 [1152, 1152], P('fsdp'), may hold values from 1e-12 to 1e-10
- square_class_table: float32 [1000, 1152], P(None, 'fsdp'), may hold values from 1e-12 to 1e-10
- square_modulation: float32 [1152, 6912], P(None, 'fsdp'), may hold values from 1e-12 to 1e-10
- square_attend_in: float32 [1152, 3456], P('fsdp'), may hold values from 1e-12 to 1e-10
- square_attend_out: float32 [1152, 1152], P('fsdp'), may hold values from 1e-12 to 1e-10
- square_expand: float32 [1152, 4608], P('fsdp'), may hold values from 1e-12 to 1e-10
- square_contract: float32 [4608, 1152], P('fsdp'), may hold values from 1e-12 to 1e-10
- square_biases: float32 [18432], P('fsdp'), may hold values from 1e-12 to 1e-10
Outputs:
- output: bfloat16 [8, 1024, 1152], P('fsdp', 'seq')
- input_gradient: float32 [8, 1024, 1152], P('fsdp', 'seq')
- condition_gradient: float32 [8, 1152], P('fsdp')
- norm_before: float32 [], replicated
- gradient_time_first: float32 [256, 1152], P('fsdp')
- gradient_time_second: float32 [1152, 1152], P('fsdp')
- gradient_class_table: float32 [1000, 1152], P(None, 'fsdp')
- gradient_modulation: float32 [1152, 6912], P(None, 'fsdp')
- gradient_attend_in: float32 [1152, 3456], P('fsdp')
- gradient_attend_out: float32 [1152, 1152], P('fsdp')
- gradient_expand: float32 [1152, 4608], P('fsdp')
- gradient_contract: float32 [4608, 1152], P('fsdp')
- gradient_biases: float32 [18432], P('fsdp')
- master_time_first: float32 [256, 1152], P('fsdp')
- master_time_second: float32 [1152, 1152], P('fsdp')
- master_class_table: float32 [1000, 1152], P(None, 'fsdp')
- master_modulation: float32 [1152, 6912], P(None, 'fsdp')
- master_attend_in: float32 [1152, 3456], P('fsdp')
- master_attend_out: float32 [1152, 1152], P('fsdp')
- master_expand: float32 [1152, 4608], P('fsdp')
- master_contract: float32 [4608, 1152], P('fsdp')
- master_biases: float32 [18432], P('fsdp')
- moment_next_time_first: float32 [256, 1152], P('fsdp')
- moment_next_time_second: float32 [1152, 1152], P('fsdp')
- moment_next_class_table: float32 [1000, 1152], P(None, 'fsdp')
- moment_next_modulation: float32 [1152, 6912], P(None, 'fsdp')
- moment_next_attend_in: float32 [1152, 3456], P('fsdp')
- moment_next_attend_out: float32 [1152, 1152], P('fsdp')
- moment_next_expand: float32 [1152, 4608], P('fsdp')
- moment_next_contract: float32 [4608, 1152], P('fsdp')
- moment_next_biases: float32 [18432], P('fsdp')
- square_next_time_first: float32 [256, 1152], P('fsdp')
- square_next_time_second: float32 [1152, 1152], P('fsdp')
- square_next_class_table: float32 [1000, 1152], P(None, 'fsdp')
- square_next_modulation: float32 [1152, 6912], P(None, 'fsdp')
- square_next_attend_in: float32 [1152, 3456], P('fsdp')
- square_next_attend_out: float32 [1152, 1152], P('fsdp')
- square_next_expand: float32 [1152, 4608], P('fsdp')
- square_next_contract: float32 [4608, 1152], P('fsdp')
- square_next_biases: float32 [18432], P('fsdp')
The draws below stay inside these ranges and needn't reach their ends.
All inputs are finite; a program needn't handle non-finite values.
Results may differ from the reference program's by a relative error of at most 0.012.
The reference program's roundings to bfloat16 on the way count: a program that leaves them out, or rounds other values in their place, can miss the bound.
Values may be sent and summed in bfloat16 or wider, within the bound.
A program may use at most 384 MiB of HBM per device.

```python
import math
from functools import partial
import jax
import jax.numpy as jnp
from jax import lax

D = 1152
H = 16
HD = 72
FF = 4608
FREQ = 256
NCLS = 1000
L = 1024
STEP = 10
LAT = 8


def touch_ends(values, rng, smallest, top_value):
    index_at = [jax.random.randint(jax.random.fold_in(rng, axis), (), 0, length) for axis, length in enumerate(values.shape)]
    longest = values.shape.index(max(values.shape))
    next_to = index_at[:longest] + [(index_at[longest] + 1) % values.shape[longest]] + index_at[longest + 1:]
    return values.at[tuple(index_at)].set(smallest).at[tuple(next_to)].set(top_value)


def steps_of(rng, shape, cuts, least, high):
    def one(axis_at, parts):
        draws = jax.random.uniform(jax.random.fold_in(jax.random.fold_in(rng, 6), axis_at), (parts,), jnp.float32, least / len(cuts), high / len(cuts))
        return jnp.repeat(jnp.exp(draws), shape[axis_at] // parts).reshape((-1,) + (1,) * (len(shape) - axis_at - 1))

    gain = one(*cuts[0])
    for cut in cuts[1:]:
        gain = gain * one(*cut)
    return gain


def noise(rng, shape, scale, reach, shards=(), kind=jnp.bfloat16):
    array = jax.random.normal(rng, shape, jnp.float32) * scale
    if len(shards) > 0:
        array = steps_of(rng, shape, shards, -0.22, 0.18) * array
    return jnp.clip(array, min=-reach, max=reach).astype(kind)


def setup_inputs(seed: int = 0) -> dict:
    streams_of = jax.random.split(jax.random.key(seed), 32)
    latents = noise(streams_of[0], (LAT, L, D), 1.0, 6.0, ((0, 8), (1, 4)))
    timesteps = touch_ends(jax.random.randint(streams_of[1], (LAT,), 0, 1000), jax.random.fold_in(streams_of[1], 1), 0, 999).astype(jnp.int32)
    labels = touch_ends(jax.random.randint(streams_of[2], (LAT,), 0, NCLS), jax.random.fold_in(streams_of[2], 1), 0, NCLS - 1).astype(jnp.int32)
    upstream = noise(streams_of[3], (LAT, L, D), 1.0, 6.0, ((0, 8), (1, 4)))
    time_first = noise(streams_of[4], (FREQ, D), FREQ ** -0.5, 0.375, ((0, 8),), jnp.float32)
    time_second = noise(streams_of[5], (D, D), D ** -0.5, 0.1875, ((0, 8),), jnp.float32)
    class_table = noise(streams_of[6], (NCLS, D), 0.2, 1.25, ((1, 8),), jnp.float32)
    modulation = noise(streams_of[7], (D, 6 * D), D ** -0.5, 0.1875, ((1, 8),), jnp.float32)
    attend_in = noise(streams_of[8], (D, 3 * D), D ** -0.5, 0.1875, ((0, 8),), jnp.float32)
    attend_out = noise(streams_of[9], (D, D), (max(D // 128, 1)) ** -0.5, 2.0, ((0, 8),), jnp.float32)
    expand = noise(streams_of[10], (D, FF), D ** -0.5, 0.1875, ((0, 8),), jnp.float32)
    contract = noise(streams_of[11], (FF, D), FF ** -0.5, 0.09375, ((0, 8),), jnp.float32)
    biases = noise(streams_of[12], (12 * D + FF,), 0.2, 1.25, ((0, 8),), jnp.float32)
    moment_time_first = noise(streams_of[13], (FREQ, D), 0.00002, 0.00012207031, ((0, 8),), jnp.float32)
    moment_time_second = noise(streams_of[14], (D, D), 0.00002, 0.00012207031, ((0, 8),), jnp.float32)
    moment_class_table = noise(streams_of[15], (NCLS, D), 0.00002, 0.00012207031, ((1, 8),), jnp.float32)
    moment_modulation = noise(streams_of[16], (D, 6 * D), 0.00002, 0.00012207031, ((1, 8),), jnp.float32)
    moment_attend_in = noise(streams_of[17], (D, 3 * D), 0.00002, 0.00012207031, ((0, 8),), jnp.float32)
    moment_attend_out = noise(streams_of[18], (D, D), 0.00002, 0.00012207031, ((0, 8),), jnp.float32)
    moment_expand = noise(streams_of[19], (D, FF), 0.00002, 0.00012207031, ((0, 8),), jnp.float32)
    moment_contract = noise(streams_of[20], (FF, D), 0.00002, 0.00012207031, ((0, 8),), jnp.float32)
    moment_biases = noise(streams_of[21], (12 * D + FF,), 0.00002, 0.00012207031, ((0, 8),), jnp.float32)
    square_time_first = jnp.clip(jnp.exp(math.log(1.000000013351432e-10) - 4.6051702 * jax.random.uniform(streams_of[22], (FREQ, D), jnp.float32) ** steps_of(streams_of[22], (FREQ, D), ((0, 8),), -0.2, 0.2)), 9.999999960041972e-13, 1.000000013351432e-10)
    square_time_second = jnp.clip(jnp.exp(math.log(1.000000013351432e-10) - 4.6051702 * jax.random.uniform(streams_of[23], (D, D), jnp.float32) ** steps_of(streams_of[23], (D, D), ((0, 8),), -0.2, 0.2)), 9.999999960041972e-13, 1.000000013351432e-10)
    square_class_table = jnp.clip(jnp.exp(math.log(1.000000013351432e-10) - 4.6051702 * jax.random.uniform(streams_of[24], (NCLS, D), jnp.float32) ** steps_of(streams_of[24], (NCLS, D), ((1, 8),), -0.2, 0.2)), 9.999999960041972e-13, 1.000000013351432e-10)
    square_modulation = jnp.clip(jnp.exp(math.log(1.000000013351432e-10) - 4.6051702 * jax.random.uniform(streams_of[25], (D, 6 * D), jnp.float32) ** steps_of(streams_of[25], (D, 6 * D), ((1, 8),), -0.2, 0.2)), 9.999999960041972e-13, 1.000000013351432e-10)
    square_attend_in = jnp.clip(jnp.exp(math.log(1.000000013351432e-10) - 4.6051702 * jax.random.uniform(streams_of[26], (D, 3 * D), jnp.float32) ** steps_of(streams_of[26], (D, 3 * D), ((0, 8),), -0.2, 0.2)), 9.999999960041972e-13, 1.000000013351432e-10)
    square_attend_out = jnp.clip(jnp.exp(math.log(1.000000013351432e-10) - 4.6051702 * jax.random.uniform(streams_of[27], (D, D), jnp.float32) ** steps_of(streams_of[27], (D, D), ((0, 8),), -0.2, 0.2)), 9.999999960041972e-13, 1.000000013351432e-10)
    square_expand = jnp.clip(jnp.exp(math.log(1.000000013351432e-10) - 4.6051702 * jax.random.uniform(streams_of[28], (D, FF), jnp.float32) ** steps_of(streams_of[28], (D, FF), ((0, 8),), -0.2, 0.2)), 9.999999960041972e-13, 1.000000013351432e-10)
    square_contract = jnp.clip(jnp.exp(math.log(1.000000013351432e-10) - 4.6051702 * jax.random.uniform(streams_of[29], (FF, D), jnp.float32) ** steps_of(streams_of[29], (FF, D), ((0, 8),), -0.2, 0.2)), 9.999999960041972e-13, 1.000000013351432e-10)
    square_biases = jnp.clip(jnp.exp(math.log(1.000000013351432e-10) - 4.6051702 * jax.random.uniform(streams_of[30], (12 * D + FF,), jnp.float32) ** steps_of(streams_of[30], (12 * D + FF,), ((0, 8),), -0.2, 0.2)), 9.999999960041972e-13, 1.000000013351432e-10)
    return {"latents": latents, "timesteps": timesteps, "labels": labels, "upstream": upstream, "time_first": time_first, "time_second": time_second, "class_table": class_table, "modulation": modulation, "attend_in": attend_in, "attend_out": attend_out, "expand": expand, "contract": contract, "biases": biases, "moment_time_first": moment_time_first, "moment_time_second": moment_time_second, "moment_class_table": moment_class_table, "moment_modulation": moment_modulation, "moment_attend_in": moment_attend_in, "moment_attend_out": moment_attend_out, "moment_expand": moment_expand, "moment_contract": moment_contract, "moment_biases": moment_biases, "square_time_first": square_time_first, "square_time_second": square_time_second, "square_class_table": square_class_table, "square_modulation": square_modulation, "square_attend_in": square_attend_in, "square_attend_out": square_attend_out, "square_expand": square_expand, "square_contract": square_contract, "square_biases": square_biases}


HIGH = lax.Precision.HIGHEST
norm_eps = 1e-06
beta_one = 0.9
beta_two = 0.999
learn_rate = 0.04
weight_decay = 0.01
adam_eps = 1e-08
clip_limit = 1.0

@jax.custom_vjp
def low(v):
    return lax.optimization_barrier(v.astype(jnp.bfloat16)).astype(jnp.float32)

@jax.custom_vjp
def low_back(v):
    return v

def low_keep(v):
    return (low(v), None)

def low_pass(kept, grad):
    return (grad,)

def back_keep(v):
    return (v, None)

def back_low(kept, grad):
    return (low(grad),)
low.defvjp(low_keep, low_pass)
low_back.defvjp(back_keep, back_low)

def layer_norm(value):
    centre = value - lax.optimization_barrier(jnp.mean(value, axis=-1, keepdims=True))
    spread = lax.optimization_barrier(jnp.mean(centre * centre, axis=-1, keepdims=True))
    return centre * lax.rsqrt(spread + norm_eps)

def time_features(timesteps):
    half = FREQ // 2
    freqs = jnp.exp(-math.log(10000.0) * jnp.arange(half, dtype=jnp.float32) / half)
    angles = timesteps.astype(jnp.float32)[:, None] * freqs[None, :]
    return jnp.concatenate([jnp.cos(angles), jnp.sin(angles)], axis=-1)

def split_biases(biases):
    widths = [D, D, 6 * D, D, D, D, FF, D]
    pieces = []
    start = 0
    for width in widths:
        pieces.append(biases[start:start + width])
        start = start + width
    return pieces

def attend_one(heads):
    score_scale = 1.0 / math.sqrt(HD)
    query = heads[:, 0]
    keys = heads[:, 1]
    values = heads[:, 2]
    scores = low_back(jnp.einsum('qhd,khd->hqk', query, keys, precision=HIGH) * score_scale)
    top = lax.optimization_barrier(jnp.max(scores, axis=-1, keepdims=True))
    expo = jnp.exp(scores - top)
    probs = expo / lax.optimization_barrier(jnp.sum(expo, axis=-1, keepdims=True))
    mixed = jnp.einsum('hqk,khd->qhd', low(probs), values, precision=HIGH)
    return mixed.reshape(L, D)

def block_group(weights, group):
    attend_in, attend_out, expand, contract, qkv_bias, b_out, b_up, b_down = weights
    inputs, mod_values = group
    shift1, scale1, gate1, shift2, scale2, gate2 = jnp.split(mod_values[:, None, :], 6, axis=-1)
    h_attn = low(layer_norm(inputs) * (1.0 + scale1) + shift1)
    qkv = jnp.einsum('btd,de->bte', h_attn, attend_in, precision=HIGH) + qkv_bias
    qkv = low(low_back(qkv))
    heads = qkv.reshape(qkv.shape[0], L, 3, H, HD)
    mixed = lax.map(jax.checkpoint(attend_one), heads)
    mixed = low(low_back(mixed))
    attn_out = low_back(jnp.einsum('btd,de->bte', mixed, attend_out, precision=HIGH) + b_out)
    middle = inputs + gate1 * attn_out
    h_mlp = low(layer_norm(middle) * (1.0 + scale2) + shift2)
    pre_act = low_back(jnp.einsum('btd,df->btf', h_mlp, expand, precision=HIGH) + b_up)
    act = low(jax.nn.gelu(pre_act, approximate=True))
    mlp_out = low_back(jnp.einsum('btf,fd->btd', act, contract, precision=HIGH) + b_down)
    return middle + gate2 * mlp_out

def forward(params, inputs, shift_zero, features, onehot):
    time_first, time_second, class_table, modulation, attend_in, attend_out, expand, contract, biases = [low(param) for param in params]
    b_t1, b_t2, b_mod, b_q, b_v, b_out, b_up, b_down = split_biases(biases)
    hidden_time = jnp.dot(low(features), time_first, precision=HIGH) + b_t1
    act_time = low(jax.nn.silu(hidden_time))
    cond = jnp.dot(act_time, time_second, precision=HIGH) + b_t2 + jnp.dot(onehot, class_table, precision=HIGH) + shift_zero
    cond_act = low(jax.nn.silu(cond))
    mod_values = jnp.dot(cond_act, modulation, precision=HIGH) + b_mod
    qkv_bias = jnp.concatenate([b_q, jnp.zeros((D,), jnp.float32), b_v])
    count = math.gcd(LAT, max(1, 4096 // L))
    groups = (inputs.reshape(LAT // count, count, L, D), mod_values.reshape(LAT // count, count, 6 * D))
    weights = (attend_in, attend_out, expand, contract, qkv_bias, b_out, b_up, b_down)
    outputs = lax.map(jax.checkpoint(partial(block_group, weights)), groups)
    return outputs.reshape(LAT, L, D)

def adam_step(weight, moment, square, gradient, factor):
    clipped = gradient * factor
    moment_next = beta_one * moment + (1.0 - beta_one) * clipped
    square_next = beta_two * square + (1.0 - beta_two) * clipped * clipped
    moment_hat = moment_next / (1.0 - beta_one ** STEP)
    square_hat = square_next / (1.0 - beta_two ** STEP)
    master = weight - learn_rate * (moment_hat / (jnp.sqrt(square_hat) + adam_eps) + weight_decay * weight)
    return (master, moment_next, square_next)

def reference(latents, timesteps, labels, upstream, time_first, time_second, class_table, modulation, attend_in, attend_out, expand, contract, biases, moment_time_first, moment_time_second, moment_class_table, moment_modulation, moment_attend_in, moment_attend_out, moment_expand, moment_contract, moment_biases, square_time_first, square_time_second, square_class_table, square_modulation, square_attend_in, square_attend_out, square_expand, square_contract, square_biases):
    params = (time_first, time_second, class_table, modulation, attend_in, attend_out, expand, contract, biases)
    moments = (moment_time_first, moment_time_second, moment_class_table, moment_modulation, moment_attend_in, moment_attend_out, moment_expand, moment_contract, moment_biases)
    squares = (square_time_first, square_time_second, square_class_table, square_modulation, square_attend_in, square_attend_out, square_expand, square_contract, square_biases)
    features = time_features(timesteps)
    onehot = (labels[:, None] == jnp.arange(NCLS, dtype=jnp.int32)[None, :]).astype(jnp.float32)

    def run(param_tuple, inputs, shift_zero):
        return forward(param_tuple, inputs, shift_zero, features, onehot)
    output, pullback = jax.vjp(run, params, latents.astype(jnp.float32), jnp.zeros((LAT, D), jnp.float32))
    grads, input_gradient, condition_gradient = pullback(upstream.astype(jnp.float32))
    total = jnp.sum(grads[0] * grads[0])
    for index in range(1, 9):
        total = total + jnp.sum(grads[index] * grads[index])
    norm_before = jnp.sqrt(total)
    factor = clip_limit / jnp.maximum(norm_before, clip_limit)
    results = [adam_step(params[index], moments[index], squares[index], grads[index], factor) for index in range(9)]
    return (output.astype(jnp.bfloat16), input_gradient, condition_gradient, norm_before, grads[0], grads[1], grads[2], grads[3], grads[4], grads[5], grads[6], grads[7], grads[8], results[0][0], results[1][0], results[2][0], results[3][0], results[4][0], results[5][0], results[6][0], results[7][0], results[8][0], results[0][1], results[1][1], results[2][1], results[3][1], results[4][1], results[5][1], results[6][1], results[7][1], results[8][1], results[0][2], results[1][2], results[2][2], results[3][2], results[4][2], results[5][2], results[6][2], results[7][2], results[8][2])
```

```python
from functools import partial
import math

import jax
import jax.numpy as jnp
from jax import lax
from jax.sharding import PartitionSpec as P

H = 16
HD = 72
FREQ = 256
NCLS = 1000
STEP = 10


HIGH = lax.Precision.HIGHEST
LOW = jnp.bfloat16
norm_eps = 1e-06
beta_one = 0.9
beta_two = 0.999
learn_rate = 0.04
weight_decay = 0.01
adam_eps = 1e-08
clip_limit = 1.0


def layer_norm(value):
    centre = value - jnp.mean(value, axis=-1, keepdims=True)
    spread = jnp.mean(centre * centre, axis=-1, keepdims=True)
    inverse = lax.rsqrt(spread + norm_eps)
    return centre * inverse, inverse


def layer_norm_back(norm, inverse, grad):
    first = jnp.mean(grad, axis=-1, keepdims=True)
    second = jnp.mean(grad * norm, axis=-1, keepdims=True)
    return inverse * (grad - first - norm * second)


def silu_parts(value):
    gate = jax.nn.sigmoid(value)
    return value * gate, gate * (1.0 + value * (1.0 - gate))


def time_features(timesteps):
    half = FREQ // 2
    freqs = jnp.exp(-math.log(10000.0) * jnp.arange(half, dtype=jnp.float32) / half)
    angles = timesteps.astype(jnp.float32)[:, None] * freqs[None, :]
    return jnp.concatenate([jnp.cos(angles), jnp.sin(angles)], axis=-1)


def split_biases(biases, width, hidden):
    widths = [width, width, 6 * width, width, width, width, hidden, width]
    pieces = []
    start = 0
    for length in widths:
        pieces.append(biases[start : start + length])
        start = start + length
    return pieces


def high_dot(left, right):
    return jnp.dot(left, right, precision=HIGH, preferred_element_type=jnp.float32)


def mixed_dot(form, left, right):
    return jnp.einsum(form, left, right, preferred_element_type=jnp.float32)


SWAP_Y = [(i, i ^ 1) for i in range(8)]
SWAP_Z1 = [(i, i ^ 2) for i in range(8)]
SWAP_Z2 = [(i, i ^ 4) for i in range(8)]
Z_UP = [(i, i + 2) for i in range(6)]
Z_DOWN = [(i + 2, i) for i in range(6)]
SWAP_CORE = [(i, i ^ 1) for i in range(4)]
SWAP_X = [(i, i ^ 2) for i in range(4)]


def pick(array, index, axis=0):
    return lax.dynamic_index_in_dim(array, index, axis, keepdims=False)


def place(array, block, *index):
    starts = tuple(index) + (0,) * (array.ndim - len(index))
    return lax.dynamic_update_slice(array, block[(None,) * len(index)], starts)


def gather_rows(block):
    count = lax.axis_size("fsdp")
    if count != 8:
        return lax.all_gather(block, "fsdp", axis=0, tiled=True)
    me = lax.axis_index("fsdp")
    z, y = me // 2, me % 2
    hop = partial(lax.ppermute, axis_name="fsdp")
    up1, down1 = hop(block, perm=Z_UP), hop(block, perm=Z_DOWN)
    mate0 = hop(block, perm=SWAP_Y)
    one = jnp.where(z == 0, down1, up1)
    mate1 = hop(one, perm=SWAP_Y)
    up2, down2 = hop(up1, perm=Z_UP), hop(down1, perm=Z_DOWN)
    two = jnp.where(z < 2, down2, up2)
    mate2 = hop(two, perm=SWAP_Y)
    up3, down3 = hop(up2, perm=Z_UP), hop(down2, perm=Z_DOWN)
    three = jnp.where(z == 0, down3, jnp.where(z == 3, up3, down1))
    mate3 = hop(three, perm=SWAP_Y)
    at1 = jnp.where(z == 0, 1, z - 1)
    at2 = jnp.where(z < 2, z + 2, z - 2)
    at3 = jnp.where(z == 0, 3, jnp.where(z == 3, 0, z + 1))
    whole = jnp.zeros((4, 2) + block.shape, block.dtype)
    for at, own, mate in ((z, block, mate0), (at1, one, mate1), (at2, two, mate2), (at3, three, mate3)):
        whole = place(whole, own, at, y)
        whole = place(whole, mate, at, 1 - y)
    return whole.reshape((8 * block.shape[0],) + block.shape[1:])


def scatter_rows(whole):
    count = lax.axis_size("fsdp")
    if count != 8:
        return lax.psum_scatter(whole, "fsdp", scatter_dimension=0, tiled=True)
    me = lax.axis_index("fsdp")
    z, y = me // 2, me % 2
    hop = partial(lax.ppermute, axis_name="fsdp")
    parts = whole.reshape((4, 2, whole.shape[0] // 8) + whole.shape[1:])
    got = hop(pick(parts, 1 - y, 1).astype(LOW), perm=SWAP_Y)
    acc = pick(parts, y, 1) + got.astype(jnp.float32)
    rise = pick(acc, jnp.minimum(z + 3, 3))
    fall = pick(acc, jnp.maximum(z - 3, 0))
    for step in (2, 1, 0):
        rise_in = hop(rise.astype(LOW), perm=Z_UP).astype(jnp.float32)
        fall_in = hop(fall.astype(LOW), perm=Z_DOWN).astype(jnp.float32)
        if step:
            rise = pick(acc, jnp.minimum(z + step, 3)) + rise_in
            fall = pick(acc, jnp.maximum(z - step, 0)) + fall_in
    return pick(acc, z) + (rise_in + fall_in)


def small_gather(block):
    count = lax.axis_size("fsdp")
    if count != 8:
        return lax.all_gather(block, "fsdp", axis=0)
    me = lax.axis_index("fsdp")
    whole = block[None]
    for bit, perm in ((1, SWAP_Y), (2, SWAP_Z1), (4, SWAP_Z2)):
        other = lax.ppermute(whole, "fsdp", perm)
        low = (me & bit) == 0
        whole = jnp.concatenate([jnp.where(low, whole, other), jnp.where(low, other, whole)], axis=0)
    return whole


def small_sum(block):
    count = lax.axis_size("fsdp")
    if count != 8:
        return lax.psum(block, "fsdp")
    for perm in (SWAP_Y, SWAP_Z1, SWAP_Z2):
        block = block + lax.ppermute(block, "fsdp", perm)
    return block


def seq_sum(block):
    count = lax.axis_size("seq")
    if count != 4:
        return lax.psum(block, "seq")
    for perm in (SWAP_CORE, SWAP_X):
        block = block + lax.ppermute(block, "seq", perm)
    return block


def seq_gather(block):
    count = lax.axis_size("seq")
    if count != 4:
        return lax.all_gather(block, "seq", axis=0)
    me = lax.axis_index("seq")
    hop = partial(lax.ppermute, axis_name="seq")
    across = hop(block, perm=SWAP_X)
    mate = hop(block, perm=SWAP_CORE)
    last = hop(across, perm=SWAP_CORE)
    whole = jnp.zeros((4,) + block.shape, block.dtype)
    for at, part in ((me, block), (me ^ 1, mate), (me ^ 2, across), (me ^ 3, last)):
        whole = place(whole, part, at)
    return whole


def seq_scatter(parts):
    count = lax.axis_size("seq")
    if count != 4:
        return lax.psum_scatter(parts, "seq", scatter_dimension=0, tiled=False)
    me = lax.axis_index("seq")
    x, core = me // 2, me % 2
    hop = partial(lax.ppermute, axis_name="seq")
    parts = parts.reshape((2, 2) + parts.shape[1:])
    got = hop(pick(parts, 1 - core, 1).astype(LOW), perm=SWAP_CORE)
    acc = pick(parts, core, 1) + got.astype(jnp.float32)
    got = hop(pick(acc, 1 - x).astype(LOW), perm=SWAP_X)
    return pick(acc, x) + got.astype(jnp.float32)


def attend(query, keys, values):
    score_scale = 1.0 / math.sqrt(keys.shape[-1])
    scores = mixed_dot("qhd,khd->hqk", query, keys) * score_scale
    top = jnp.max(scores, axis=-1, keepdims=True)
    expo = jnp.exp(scores - top)
    total = jnp.sum(expo, axis=-1, keepdims=True)
    probs = (expo / total).astype(LOW)
    mixed = mixed_dot("hqk,khd->qhd", probs, values)
    return mixed.astype(LOW), (top + jnp.log(total))[..., 0]


def attend_back(query, keys, values, d_mixed, log_total):
    length, heads_here, head_dim = query.shape
    block = min(512, length)
    count = length // block
    score_scale = 1.0 / math.sqrt(head_dim)

    def back_block(carry, pieces):
        d_keys, d_values = carry
        query_block, d_block, log_block = pieces
        scores = mixed_dot("qhd,khd->hqk", query_block, keys) * score_scale
        probs = jnp.exp(scores - log_block[..., None])
        d_probs = mixed_dot("qhd,khd->hqk", d_block, values)
        delta = jnp.sum(probs * d_probs, axis=-1, keepdims=True)
        d_scores = (probs * (d_probs - delta)).astype(LOW)
        d_query = mixed_dot("hqk,khd->qhd", d_scores, keys) * score_scale
        d_keys = d_keys + mixed_dot("hqk,qhd->khd", d_scores, query_block) * score_scale
        d_values = d_values + mixed_dot("hqk,qhd->khd", probs.astype(LOW), d_block)
        return ((d_keys, d_values), d_query)

    empty = jnp.zeros((length, heads_here, head_dim), jnp.float32)
    blocked = (count, block, heads_here, head_dim)
    logs = log_total.reshape(heads_here, count, block).transpose(1, 0, 2)
    (d_keys, d_values), d_query = lax.scan(
        back_block, (empty, empty), (query.reshape(blocked), d_mixed.reshape(blocked), logs)
    )
    flat = (length, heads_here * head_dim)
    return jnp.concatenate(
        [d_query.reshape(flat), d_keys.reshape(flat), d_values.reshape(flat)], axis=1
    ).astype(LOW)


def adam_step(weight, moment, square, gradient, factor):
    clipped = gradient * factor
    moment_next = beta_one * moment + (1.0 - beta_one) * clipped
    square_next = beta_two * square + (1.0 - beta_two) * clipped * clipped
    moment_hat = moment_next / (1.0 - beta_one**STEP)
    square_hat = square_next / (1.0 - beta_two**STEP)
    master = weight - learn_rate * (
        moment_hat / (jnp.sqrt(square_hat) + adam_eps) + weight_decay * weight
    )
    return (master, moment_next, square_next)


def per_device(latents, timesteps, labels, upstream, *state):
    params, moments, squares = state[:9], state[9:18], state[18:]
    time_first, time_second, class_table, modulation, attend_in, attend_out, expand, contract, biases = params
    lat_dev, tok_rows, width = latents.shape
    assert lat_dev == 1
    hidden = expand.shape[1]
    ranks = lax.axis_size("seq")
    owners = lax.axis_size("fsdp")
    rank = lax.axis_index("seq")
    owner = lax.axis_index("fsdp")
    heads_here = H // ranks
    span = heads_here * HD
    length = ranks * tok_rows
    rows = width // owners
    unit = hidden // (owners * ranks)
    hid_here = owners * unit
    mod_here = 6 * width // owners
    first_rows = FREQ // owners

    def mine(array, axis, parts, index):
        size = array.shape[axis] // parts
        return lax.dynamic_slice_in_dim(array, index * size, size, axis)

    w_in = gather_rows(pick(attend_in.reshape(rows, 3, ranks, span), rank, 2).astype(LOW).reshape(rows, 3 * span))
    w_out_part = gather_rows(mine(attend_out, 1, ranks, rank).astype(LOW))
    w_up = gather_rows(
        pick(expand.reshape(rows, owners, ranks, unit), rank, 2).astype(LOW).reshape(rows, hid_here)
    )
    w_down = gather_rows(mine(contract, 0, ranks, rank).astype(LOW))
    inputs_low = seq_gather(latents[0]).reshape(length, width)
    d_out_low = seq_gather(upstream[0]).reshape(length, width)
    w_out = seq_gather(w_out_part).transpose(1, 0, 2).reshape(width, width)

    note = jnp.concatenate(
        [biases.astype(LOW).astype(jnp.float32), timesteps.astype(jnp.float32), labels.astype(jnp.float32)]
    )
    notes = small_gather(note)
    share = biases.shape[0]
    all_bias = notes[:, :share].reshape(owners * share)
    all_steps = notes[:, share]
    all_labels = notes[:, share + 1].astype(jnp.int32)
    b_t1, b_t2, b_mod, b_q, b_v, b_out, b_up, b_down = split_biases(all_bias, width, hidden)
    features = time_features(all_steps).astype(LOW)
    my_features = mine(features, 1, owners, owner)
    hidden_time = small_sum(mixed_dot("bf,fd->bd", my_features, time_first.astype(LOW))) + b_t1
    act_time_f, silu_time_slope = silu_parts(hidden_time)
    act_time = act_time_f.astype(LOW)
    my_act_time = mine(act_time, 1, owners, owner)
    onehot = (all_labels[:, None] == jnp.arange(NCLS, dtype=jnp.int32)[None, :]).astype(LOW)
    class_part = mixed_dot("bc,cd->bd", onehot, class_table.astype(LOW))
    cond_part = mixed_dot("bd,de->be", my_act_time, time_second.astype(LOW))
    class_wide = lax.dynamic_update_slice(jnp.zeros_like(cond_part), class_part, (0, owner * rows))
    cond = small_sum(cond_part + class_wide) + b_t2
    cond_act_f, silu_cond_slope = silu_parts(cond)
    cond_act = cond_act_f.astype(LOW)
    modulation_low = modulation.astype(LOW)
    mod_part = mixed_dot("bd,de->be", cond_act, modulation_low) + mine(b_mod, 0, owners, owner)
    mod_values = pick(small_gather(mod_part), owner, 1).reshape(6, 1, width)
    shift1, scale1, gate1, shift2, scale2, gate2 = [mod_values[index] for index in range(6)]

    inputs = inputs_low.astype(jnp.float32)
    norm_one, _ = layer_norm(inputs)
    h_attn = (norm_one * (1.0 + scale1) + shift1).astype(LOW)
    my_b_q, my_b_v = mine(b_q, 0, ranks, rank), mine(b_v, 0, ranks, rank)
    qkv_bias = jnp.concatenate([my_b_q, jnp.zeros_like(my_b_q), my_b_v])
    qkv = (mixed_dot("td,de->te", h_attn, w_in) + qkv_bias).astype(LOW)
    head_shape = (length, heads_here, HD)
    query, keys, values = [qkv[:, part * span : (part + 1) * span].reshape(head_shape) for part in range(3)]
    mixed_heads, log_total = attend(query, keys, values)
    mixed = seq_gather(mixed_heads.reshape(length, span)).transpose(1, 0, 2).reshape(length, width)
    attn_out = mixed_dot("td,de->te", mixed, w_out) + b_out
    middle = inputs + gate1 * attn_out
    norm_two, inverse_two = layer_norm(middle)
    h_mlp = (norm_two * (1.0 + scale2) + shift2).astype(LOW)

    my_b_up = pick(b_up.reshape(owners, ranks, unit), rank, 1).reshape(hid_here)
    pre_act = mixed_dot("td,df->tf", h_mlp, w_up) + my_b_up
    act_f, gelu_pull = jax.vjp(partial(jax.nn.gelu, approximate=True), pre_act)
    act = act_f.astype(LOW)
    mlp_part = mixed_dot("tf,fd->td", act, w_down)
    d_out = d_out_low.astype(jnp.float32)
    d_mlp = (d_out * gate2).astype(LOW)
    d_act = mixed_dot("td,fd->tf", d_mlp, w_down)
    d_pre = gelu_pull(d_act)[0].astype(LOW)
    d_hmlp_part = mixed_dot("tf,df->td", d_pre, w_up)
    d_hmlp = seq_scatter(d_hmlp_part.reshape(ranks, tok_rows, width))
    g_down = scatter_rows(mixed_dot("tf,td->fd", act, d_mlp))
    g_up = scatter_rows(mixed_dot("td,tf->df", h_mlp, d_pre))
    gb_up = jnp.sum(d_pre.astype(jnp.float32), axis=0)
    gb_down = jnp.sum(d_mlp.astype(jnp.float32), axis=0)

    own = lambda array: mine(array, 0, ranks, rank)
    my_attn_out, my_middle, my_norm_two, my_inverse_two = own(attn_out), own(middle), own(norm_two), own(inverse_two)
    my_d_out = upstream[0].astype(jnp.float32)
    mlp_out = seq_scatter(mlp_part.reshape(ranks, tok_rows, width)) + b_down
    output = (my_middle + gate2 * mlp_out).astype(LOW)
    d_gate2 = jnp.sum(my_d_out * mlp_out, axis=0)
    d_shift2 = jnp.sum(d_hmlp, axis=0)
    d_scale2 = jnp.sum(d_hmlp * my_norm_two, axis=0)
    d_middle = my_d_out + layer_norm_back(my_norm_two, my_inverse_two, d_hmlp * (1.0 + scale2))
    d_gate1 = jnp.sum(d_middle * my_attn_out, axis=0)
    my_d_attn = (d_middle * gate1).astype(LOW)
    d_attn = seq_gather(my_d_attn).reshape(length, width)
    d_mixed = mixed_dot("te,de->td", d_attn, mine(w_out, 0, ranks, rank)).astype(LOW)
    g_out = scatter_rows(mixed_dot("td,te->de", mixed, mine(d_attn, 1, ranks, rank)))
    d_qkv = attend_back(query, keys, values, d_mixed.reshape(head_shape), log_total)
    g_in = scatter_rows(mixed_dot("td,te->de", h_attn, d_qkv))
    d_hattn = seq_scatter(mixed_dot("te,de->td", d_qkv, w_in).reshape(ranks, tok_rows, width))
    my_inputs = latents[0].astype(jnp.float32)
    my_norm_one, my_inverse_one = layer_norm(my_inputs)
    d_shift1 = jnp.sum(d_hattn, axis=0)
    d_scale1 = jnp.sum(d_hattn * my_norm_one, axis=0)
    input_gradient = d_middle + layer_norm_back(my_norm_one, my_inverse_one, d_hattn * (1.0 + scale1))

    my_d_mod = jnp.concatenate([d_shift1, d_scale1, d_gate1, d_shift2, d_scale2, d_gate2])
    d_mod = small_gather(seq_sum(my_d_mod))
    gb_qv = jnp.sum(d_qkv.astype(jnp.float32), axis=0)
    wide = lambda part, size: lax.dynamic_update_slice(jnp.zeros((size,), jnp.float32), part, (rank * part.shape[0],))
    gb_up_wide = lax.dynamic_update_slice(
        jnp.zeros((owners, ranks, unit), jnp.float32), gb_up.reshape(owners, 1, unit), (0, rank, 0)
    ).reshape(hidden)
    gb_tail = jnp.concatenate(
        [
            wide(gb_qv[:span], width),
            wide(gb_qv[2 * span :], width),
            jnp.sum(my_d_attn.astype(jnp.float32), axis=0),
            gb_up_wide,
            jnp.where(rank == 0, gb_down, 0.0),
        ]
    )
    gb_tail = small_sum(seq_sum(gb_tail))
    my_d_mod_all = mine(d_mod, 1, owners, owner)
    d_cond_act = small_sum(high_dot(my_d_mod_all, modulation_low.astype(jnp.float32).T))
    d_cond = d_cond_act * silu_cond_slope
    my_d_cond = mine(d_cond, 1, owners, owner)
    d_time_part = high_dot(d_cond, time_second.astype(LOW).astype(jnp.float32).T)
    d_time_part = d_time_part * mine(silu_time_slope, 1, owners, owner)
    d_hidden_time = small_gather(d_time_part).transpose(1, 0, 2).reshape(owners, width)
    grad_mod = high_dot(cond_act.astype(jnp.float32).T, my_d_mod_all)
    grad_class = high_dot(onehot.astype(jnp.float32).T, my_d_cond)
    grad_second = high_dot(my_act_time.astype(jnp.float32).T, d_cond)
    grad_first = high_dot(my_features.astype(jnp.float32).T, d_hidden_time)
    all_grad_bias = jnp.concatenate(
        [jnp.sum(d_hidden_time, axis=0), jnp.sum(d_cond, axis=0), jnp.sum(d_mod, axis=0), gb_tail]
    )
    grad_bias = mine(all_grad_bias, 0, owners, owner)
    condition_gradient = lax.dynamic_slice_in_dim(d_cond, owner, 1, 0)

    grad_in = seq_gather(g_in.astype(LOW)).astype(jnp.float32).reshape(ranks, rows, 3, span)
    grad_in = grad_in.transpose(1, 2, 0, 3).reshape(rows, 3 * width)
    grad_out = seq_gather(g_out.astype(LOW)).astype(jnp.float32).transpose(1, 0, 2).reshape(rows, width)
    grad_up = seq_gather(g_up.astype(LOW)).astype(jnp.float32).reshape(ranks, rows, owners, unit)
    grad_up = grad_up.transpose(1, 2, 0, 3).reshape(rows, hidden)
    grad_down = seq_gather(g_down.astype(LOW)).astype(jnp.float32).reshape(contract.shape)
    gradients = (grad_first, grad_second, grad_class, grad_mod, grad_in, grad_out, grad_up, grad_down, grad_bias)
    local_sum = sum(jnp.sum(gradient * gradient) for gradient in gradients)
    norm_before = jnp.sqrt(small_sum(local_sum))
    factor = clip_limit / jnp.maximum(norm_before, clip_limit)
    results = [
        adam_step(params[index], moments[index], squares[index], gradients[index], factor)
        for index in range(9)
    ]
    return (
        (output[None], input_gradient[None], condition_gradient, norm_before)
        + gradients
        + tuple(result[0] for result in results)
        + tuple(result[1] for result in results)
        + tuple(result[2] for result in results)
    )


def solution(mesh):
    tokens = P("fsdp", "seq", None)
    rows, columns = P("fsdp", None), P(None, "fsdp")
    weights = (rows, rows, columns, columns, rows, rows, rows, rows, P("fsdp"))
    return jax.shard_map(
        per_device,
        mesh=mesh,
        in_specs=(tokens, P("fsdp"), P("fsdp"), tokens) + weights * 3,
        out_specs=(tokens, tokens, rows, P()) + weights * 4,
        check_vma=False,
    )
```

```python
from functools import partial
import math

import jax
import jax.numpy as jnp
from jax import lax
from jax.experimental import pallas as pl
from jax.experimental.pallas import tpu as pltpu
from jax.sharding import PartitionSpec as P

H = 16
HD = 72
FREQ = 256
NCLS = 1000
STEP = 10


HIGH = lax.Precision.HIGHEST
LOW = jnp.bfloat16
norm_eps = 1e-06
beta_one = 0.9
beta_two = 0.999
learn_rate = 0.04
weight_decay = 0.01
adam_eps = 1e-08
clip_limit = 1.0


def layer_norm(value):
    centre = value - jnp.mean(value, axis=-1, keepdims=True)
    spread = jnp.mean(centre * centre, axis=-1, keepdims=True)
    inverse = lax.rsqrt(spread + norm_eps)
    return centre * inverse, inverse


def layer_norm_back(norm, inverse, grad):
    first = jnp.mean(grad, axis=-1, keepdims=True)
    second = jnp.mean(grad * norm, axis=-1, keepdims=True)
    return inverse * (grad - first - norm * second)


def silu_parts(value):
    gate = jax.nn.sigmoid(value)
    return value * gate, gate * (1.0 + value * (1.0 - gate))


def time_features(timesteps):
    half = FREQ // 2
    freqs = jnp.exp(-math.log(10000.0) * jnp.arange(half, dtype=jnp.float32) / half)
    angles = timesteps.astype(jnp.float32)[:, None] * freqs[None, :]
    return jnp.concatenate([jnp.cos(angles), jnp.sin(angles)], axis=-1)


def split_biases(biases, width, hidden):
    widths = [width, width, 6 * width, width, width, width, hidden, width]
    pieces = []
    start = 0
    for length in widths:
        pieces.append(biases[start : start + length])
        start = start + length
    return pieces


def high_dot(left, right):
    return jnp.dot(left, right, precision=HIGH, preferred_element_type=jnp.float32)


def mixed_dot(form, left, right):
    return jnp.einsum(form, left, right, preferred_element_type=jnp.float32)


def pick(array, index, axis=0):
    return lax.dynamic_index_in_dim(array, index, axis, keepdims=False)


def mine(array, axis, parts, index):
    size = array.shape[axis] // parts
    return lax.dynamic_slice_in_dim(array, index * size, size, axis)


HBM = pl.BlockSpec(memory_space=pl.ANY)
VMEM = pl.BlockSpec(memory_space=pltpu.VMEM)
DMA = pltpu.SemaphoreType.DMA
F32 = jnp.float32


def fast():
    return lax.axis_size("fsdp") == 8 and lax.axis_size("seq") == 4


def places():
    owner, rank = lax.axis_index("fsdp"), lax.axis_index("seq")
    return owner, rank, lax.div(owner, 2), lax.rem(owner, 2), lax.div(rank, 2), lax.rem(rank, 2)


def remote(src, dst, sent, landed, **where):
    return pltpu.make_async_remote_copy(
        src_ref=src, dst_ref=dst, send_sem=sent, recv_sem=landed, device_id=where, device_id_type=pl.DeviceIdType.MESH
    )


def arrived(dst, landed, **where):
    remote(dst, dst, landed, landed, **where).wait_recv()


def greet(over_owners, over_ranks):
    owner, rank, *_ = places()
    barrier = pltpu.get_barrier_semaphore()
    count = 0
    if over_owners:
        for step in range(1, 8):
            pl.semaphore_signal(
                barrier, inc=1, device_id={"fsdp": lax.rem(owner + step, 8)}, device_id_type=pl.DeviceIdType.MESH
            )
        count += 7
    if over_ranks:
        for step in range(1, 4):
            pl.semaphore_signal(
                barrier, inc=1, device_id={"seq": lax.rem(rank + step, 4)}, device_id_type=pl.DeviceIdType.MESH
            )
        count += 3
    pl.semaphore_wait(barrier, count)


def run_all(parts):
    parts = list(parts)
    while parts:
        for part in list(parts):
            try:
                next(part)
            except StopIteration:
                parts.remove(part)


class Sends:
    def __init__(self):
        self.live = []

    def start(self, copy, when=None):
        self.live.append((copy, when))
        if when is None:
            copy.start()
        else:
            pl.when(when)(copy.start)

    def finish(self):
        for copy, when in self.live:
            wait = copy.wait_send if hasattr(copy, "wait_send") else copy.wait
            if when is None:
                wait()
            else:
                pl.when(when)(wait)


def gather_owners(src, out, sems):
    own_sem, sent, landed = sems
    owner, rank, z, y, x, core = places()
    mate = owner + 1 - 2 * y
    sends = Sends()
    local = pltpu.make_async_copy(src, out.at[owner], own_sem)
    local.start()
    sends.start(remote(src, out.at[owner], sent.at[0, 0], landed.at[owner], fsdp=owner + 2), z < 3)
    sends.start(remote(src, out.at[owner], sent.at[0, 1], landed.at[owner], fsdp=owner - 2), z > 0)
    sends.start(remote(src, out.at[owner], sent.at[0, 2], landed.at[owner], fsdp=mate))
    yield
    for far in (1, 2, 3):
        for sign in (-1, 1):
            block = owner + sign * 2 * far
            here = (z >= far) if sign < 0 else (z + far <= 3)
            on = (z < 3) if sign < 0 else (z > 0)
            at = far if sign < 0 else 3 + far
            pl.when(here)(lambda: arrived(out.at[block], landed.at[block], fsdp=mate))
            sends.start(
                remote(out.at[block], out.at[block], sent.at[at, 0], landed.at[block], fsdp=owner - sign * 2), here & on
            )
            sends.start(remote(out.at[block], out.at[block], sent.at[at, 2], landed.at[block], fsdp=mate), here)
            yield
    for step in range(4):
        block = step * 2 + 1 - y
        arrived(out.at[block], landed.at[block], fsdp=mate)
    local.wait()
    sends.finish()


GATHER_OWNERS_SEMS = [DMA(()), DMA((7, 3)), DMA((8,))]


def gather_ranks(src, out, sems, local_copy=True):
    own_sem, sent, landed = sems
    owner, rank, z, y, x, core = places()
    mate, across, last = x * 2 + 1 - core, (1 - x) * 2 + core, (1 - x) * 2 + 1 - core
    sends = Sends()
    local = None
    if local_copy:
        local = pltpu.make_async_copy(src, out.at[rank], own_sem)
        local.start()
    sends.start(remote(src, out.at[rank], sent.at[0], landed.at[rank], seq=across))
    sends.start(remote(src, out.at[rank], sent.at[1], landed.at[rank], seq=mate))
    yield
    yield
    arrived(out.at[across], landed.at[across], seq=across)
    sends.start(remote(out.at[across], out.at[across], sent.at[2], landed.at[across], seq=mate))
    yield
    arrived(out.at[mate], landed.at[mate], seq=mate)
    arrived(out.at[last], landed.at[last], seq=mate)
    if local is not None:
        local.wait()
    sends.finish()


GATHER_RANKS_SEMS = [DMA(()), DMA((3,)), DMA((4,))]


def gather_both(src, out, sems):
    rank = lax.axis_index("seq")
    yield from gather_owners(src, out.at[rank], sems[:3])
    yield from gather_ranks(out.at[rank], out, sems[3:], local_copy=False)


def by_rows(count, body, step=16):
    def one(index, carry):
        body(pl.ds(pl.multiple_of(index * step, step), step))
        return carry

    lax.fori_loop(0, count // step, one, 0)


def scatter_ranks(parts, out, own, mail, leave, enter, sems):
    own_sem, sent, landed = sems
    owner, rank, z, y, x, core = places()
    mate, across = x * 2 + 1 - core, (1 - x) * 2 + core
    sends = Sends()
    loads = []
    for step in (1, 0):
        to = lax.rem(x + step, 2)
        loads.append(pltpu.make_async_copy(parts.at[to * 2 + core], own.at[step], own_sem.at[step]))
        loads[-1].start()
        sends.start(remote(parts.at[to * 2 + 1 - core], mail.at[step], sent.at[step], landed.at[step], seq=mate))
    yield
    loads[0].wait()
    arrived(mail.at[1], landed.at[1], seq=mate)

    def first(rows):
        leave[rows] = (own[1, rows].astype(F32) + mail[1, rows].astype(F32)).astype(LOW)

    by_rows(out.shape[0], first)
    sends.start(remote(leave, enter, sent.at[2], landed.at[2], seq=across))
    yield
    loads[1].wait()
    arrived(mail.at[0], landed.at[0], seq=mate)
    yield
    arrived(enter, landed.at[2], seq=across)

    def last(rows):
        out[rows] = own[0, rows].astype(F32) + mail[0, rows].astype(F32) + enter[rows].astype(F32)

    by_rows(out.shape[0], last)
    sends.finish()


def scatter_ranks_scratch(rows, columns):
    return [
        pltpu.VMEM((2, rows, columns), LOW),
        pltpu.VMEM((2, rows, columns), LOW),
        pltpu.VMEM((rows, columns), LOW),
        pltpu.VMEM((rows, columns), LOW),
        DMA((2,)),
        DMA((3,)),
        DMA((3,)),
    ]


def scatter_owners(parts, out, own, mail, rise, fall, leave, sems):
    own_sem, y_sent, y_landed, z_sent, up_landed, down_landed = sems[:6]
    owner, rank, z, y, x, core = places()
    mate = owner + 1 - 2 * y
    rows_here = own.shape[1]
    sends = Sends()
    loads = {}
    for to in (3, 0, 2, 1):
        sends.start(remote(parts.at[to * 2 + 1 - y], mail.at[to], y_sent.at[to], y_landed.at[to], fsdp=mate))
        loads[to] = pltpu.make_async_copy(parts.at[to * 2 + y], own.at[to], own_sem.at[to])
        loads[to].start()
    yield
    for to, up in ((3, True), (0, False), (2, True), (1, False), (1, True), (2, False)):
        here = (z < to) if up else (z > to)
        more = (z > 0) if up else (z < 3)
        box, box_landed = (rise, up_landed) if up else (fall, down_landed)

        def total(to=to, more=more, box=box, box_landed=box_landed):
            loads[to].wait()
            arrived(mail.at[to], y_landed.at[to], fsdp=mate)

            def start(rows):
                leave[to, rows] = (own[to, rows].astype(F32) + mail[to, rows].astype(F32)).astype(LOW)

            def add(rows):
                leave[to, rows] = (
                    own[to, rows].astype(F32) + mail[to, rows].astype(F32) + box[to, rows].astype(F32)
                ).astype(LOW)

            @pl.when(more)
            def _():
                arrived(box.at[to], box_landed.at[to], fsdp=mate)
                by_rows(rows_here, add)

            @pl.when(jnp.logical_not(more))
            def _():
                by_rows(rows_here, start)

        pl.when(here)(total)
        sends.start(
            remote(
                leave.at[to], box.at[to], z_sent.at[to], box_landed.at[to], fsdp=owner + 2 if up else owner - 2
            ),
            here,
        )
        yield
    for to in range(4):
        at_home = z == to

        @pl.when(at_home)
        def _(to=to):
            loads[to].wait()
            arrived(mail.at[to], y_landed.at[to], fsdp=mate)
            if to > 0:
                arrived(rise.at[to], up_landed.at[to], fsdp=mate)
            if to < 3:
                arrived(fall.at[to], down_landed.at[to], fsdp=mate)

            def end(rows):
                value = own[to, rows].astype(F32) + mail[to, rows].astype(F32)
                if to > 0:
                    value = value + rise[to, rows].astype(F32)
                if to < 3:
                    value = value + fall[to, rows].astype(F32)
                leave[to, rows] = value.astype(LOW)

            by_rows(rows_here, end)

    yield from gather_ranks(leave.at[z], out, sems[6:])
    sends.finish()


def scatter_owners_scratch(rows, columns):
    return [pltpu.VMEM((4, rows, columns), LOW)] * 5 + [DMA((4,))] * 6 + GATHER_RANKS_SEMS


def swap_start(sends, src_of, dst, sent, landed):
    owner = lax.axis_index("fsdp")
    for step in range(1, 8):
        to = lax.rem(owner + step, 8)
        sends.start(remote(src_of(to), dst.at[owner], sent.at[step - 1], landed.at[owner], fsdp=to))


def swap_wait(dst, landed):
    owner = lax.axis_index("fsdp")
    for step in range(1, 8):
        of = lax.rem(owner + step, 8)
        arrived(dst.at[of], landed.at[of], fsdp=of)


SWAP_SEMS = [DMA((7,)), DMA((8,))]


def low_dot(left, right, contract):
    return lax.dot_general(left, right, ((contract[:1], contract[1:]), ((), ())), preferred_element_type=F32)


def fine_dot(left, right, contract):
    high = left.astype(LOW)
    rest = left - high.astype(F32)
    return low_dot(high, right, contract) + low_dot(rest.astype(LOW), right, contract)


def stack_rows(ref):
    return jnp.concatenate([ref[index] for index in range(8)], axis=0)


def condition_forward(note, first, second, table, modulation, outs, scratch, sems):
    notes, act_out, slope_out, cond_cut, cond_out, mod = outs
    send_cut, hid_in, cond_in, bias_cut, mod_cut = scratch
    owner = lax.axis_index("fsdp")
    cut = second.shape[0]
    share = note.shape[2] - 128
    sends = Sends()
    notes[owner] = note[owner]
    swap_start(sends, lambda to: note.at[to], notes, *sems[0:2])
    yield
    swap_wait(notes, sems[1])
    rows = stack_rows(notes)
    feats = rows[:, share : share + first.shape[0]].astype(LOW)
    label = rows[:, share + first.shape[0] : share + first.shape[0] + 1]
    hidden = low_dot(feats, first[...], (1, 0))
    for to in range(8):
        send_cut[0, to] = hidden[:, to * cut : (to + 1) * cut]
        bias_cut[0, to] = rows[0:1, to * cut : (to + 1) * cut]
        bias_cut[1, to] = rows[0:1, (8 + to) * cut : (9 + to) * cut]
    hid_in[owner] = send_cut[0, owner]
    swap_start(sends, lambda to: send_cut.at[0, to], hid_in, *sems[2:4])
    yield
    classes = lax.broadcasted_iota(jnp.int32, (8, table.shape[0]), 1).astype(F32)
    onehot = (label == classes).astype(F32).astype(LOW)
    from_class = low_dot(onehot, table[...], (1, 0))
    swap_wait(hid_in, sems[3])
    hidden_cut = bias_cut[0, owner] + jnp.zeros((8, cut), F32)
    for of in range(8):
        hidden_cut = hidden_cut + hid_in[of]
    act, slope = silu_parts(hidden_cut)
    act = act.astype(LOW)
    act_out[...] = act.astype(F32)
    slope_out[...] = slope
    part = low_dot(act, second[...], (1, 0))
    for to in range(8):
        send_cut[1, to] = part[:, to * cut : (to + 1) * cut]
    cond_in[owner] = send_cut[1, owner]
    swap_start(sends, lambda to: send_cut.at[1, to], cond_in, *sems[4:6])
    yield
    swap_wait(cond_in, sems[5])
    mine_cond = bias_cut[1, owner] + from_class
    for of in range(8):
        mine_cond = mine_cond + cond_in[of]
    cond_cut[owner] = mine_cond
    swap_start(sends, lambda to: cond_cut.at[owner], cond_cut, *sems[6:8])
    yield
    swap_wait(cond_cut, sems[7])
    for of in range(8):
        cond_out[:, of * cut : (of + 1) * cut] = cond_cut[of]
    cond_act = silu_parts(cond_out[...])[0].astype(LOW)
    values = low_dot(cond_act, modulation[...], (1, 0))
    for to in range(8):
        mod_cut[to] = values[to : to + 1]
    mod[owner] = mod_cut[owner]
    swap_start(sends, lambda to: mod_cut.at[to], mod, *sems[8:10])
    yield
    swap_wait(mod, sems[9])
    sends.finish()


def condition_backward(news, second, modulation, cond_cut, time_slope, outs, scratch, sems):
    by_latent, d_cond_out, d_hid_cut, sums = outs
    rank_news, owner_news, d_cut, d_in, d_cond_cut = scratch
    owner, rank, *_ = places()
    cut = second.shape[0]
    wide = modulation.shape[1]
    sends = Sends()
    for step in range(1, 4):
        to = lax.rem(rank + step, 4)
        sends.start(remote(news, rank_news.at[rank], sems[0].at[step - 1], sems[1].at[rank], seq=to))
    yield
    for step in range(1, 4):
        of = lax.rem(rank + step, 4)
        arrived(rank_news.at[of], sems[1].at[of], seq=of)
    rank_news[rank] = news[...]
    for to in range(8):
        owner_news[to] = rank_news[0, to] + rank_news[1, to] + rank_news[2, to] + rank_news[3, to]
    by_latent[owner] = owner_news[owner]
    swap_start(sends, lambda to: owner_news.at[to], by_latent, *sems[2:4])
    yield
    swap_wait(by_latent, sems[3])
    d_mod = stack_rows(by_latent)[:, :wide]
    part = fine_dot(d_mod, modulation[...], (1, 1))
    for to in range(8):
        d_cut[to] = part[:, to * cut : (to + 1) * cut]
    d_in[owner] = d_cut[owner]
    swap_start(sends, lambda to: d_cut.at[to], d_in, *sems[4:6])
    sums[owner] = jnp.sum(d_mod, axis=0, keepdims=True)
    swap_start(sends, lambda to: sums.at[owner], sums, *sems[6:8])
    yield
    swap_wait(d_in, sems[5])
    total = d_in[0]
    for of in range(1, 8):
        total = total + d_in[of]
    d_cond_cut[owner] = total * silu_parts(cond_cut[owner])[1]
    swap_start(sends, lambda to: d_cond_cut.at[owner], d_cond_cut, *sems[8:10])
    yield
    swap_wait(d_cond_cut, sems[9])
    for of in range(8):
        d_cond_out[:, of * cut : (of + 1) * cut] = d_cond_cut[of]
    d_hid_cut[owner] = fine_dot(d_cond_out[...], second[...], (1, 1)) * time_slope[...]
    swap_start(sends, lambda to: d_hid_cut.at[owner], d_hid_cut, *sems[10:12])
    yield
    swap_wait(d_hid_cut, sems[11])
    swap_wait(sums, sems[7])
    sends.finish()


def takes(refs, *counts):
    refs = list(refs)
    groups = []
    for count in counts:
        groups.append(refs[:count])
        refs = refs[count:]
    assert not refs
    return groups


def call(kernel, number, args, in_specs, outs, out_specs, scratch, name):
    return pl.pallas_call(
        kernel,
        out_shape=outs,
        in_specs=in_specs,
        out_specs=out_specs,
        scratch_shapes=scratch,
        compiler_params=pltpu.CompilerParams(
            collective_id=number, has_side_effects=True, vmem_limit_bytes=60 * 1024 * 1024
        ),
        name=name,
    )(*args)


def shape(dims, kind):
    return jax.ShapeDtypeStruct(tuple(dims), kind)


def forward_first(w_in, w_out, tokens, note, first, second, table, modulation):
    rows, width = second.shape
    wide = modulation.shape[1]

    def kernel(*refs):
        args, outs, scratch, cond_sems, in_sems, out_sems, token_sems = takes(refs, 8, 9, 5, 10, 3, 6, 3)
        greet(True, True)
        run_all(
            [
                condition_forward(args[3], *args[4:8], outs[3:9], scratch, cond_sems),
                gather_both(args[1], outs[1], out_sems),
                gather_ranks(args[2], outs[2], token_sems),
                gather_owners(args[0], outs[0], in_sems),
            ]
        )

    return call(
        kernel,
        1,
        (w_in, w_out, tokens, note, first, second, table, modulation),
        [VMEM] * 8,
        [
            shape((8,) + w_in.shape, LOW),
            shape((4, 8) + w_out.shape, LOW),
            shape((4,) + tokens.shape, LOW),
            shape(note.shape, F32),
            shape((8, rows), F32),
            shape((8, rows), F32),
            shape((8, 8, rows), F32),
            shape((8, width), F32),
            shape((8, 1, wide), F32),
        ],
        [HBM] * 3 + [VMEM] * 6,
        [
            pltpu.VMEM((2, 8, 8, rows), F32),
            pltpu.VMEM((8, 8, rows), F32),
            pltpu.VMEM((8, 8, rows), F32),
            pltpu.VMEM((2, 8, 1, rows), F32),
            pltpu.VMEM((8, 1, wide), F32),
        ]
        + SWAP_SEMS * 5
        + GATHER_OWNERS_SEMS
        + GATHER_OWNERS_SEMS
        + GATHER_RANKS_SEMS
        + GATHER_RANKS_SEMS,
        "forward_first",
    )


def gathers(number, by_owner, by_rank, name):
    if not fast():
        return [lax.all_gather(block, "fsdp", axis=0) for block in by_owner] + [
            lax.all_gather(block, "seq", axis=0) for block in by_rank
        ]
    many, few = len(by_owner), len(by_rank)

    def kernel(*refs):
        groups = takes(refs, many + few, many + few, *[3] * (many + few))
        args, outs, sems = groups[0], groups[1], groups[2:]
        greet(many > 0, few > 0)
        run_all(
            [gather_owners(args[at], outs[at], sems[at]) for at in range(many)]
            + [gather_ranks(args[at], outs[at], sems[at]) for at in range(many, many + few)]
        )

    blocks = list(by_owner) + list(by_rank)
    return call(
        kernel,
        number,
        blocks,
        [VMEM] * len(blocks),
        [shape((8 if at < many else 4,) + block.shape, block.dtype) for at, block in enumerate(blocks)],
        [HBM] * len(blocks),
        GATHER_OWNERS_SEMS * many + GATHER_RANKS_SEMS * few,
        name,
    )


def rank_sums(number, blocks, name):
    if not fast():
        return [lax.psum_scatter(block.astype(F32), "seq", scatter_dimension=0, tiled=False) for block in blocks]
    many = len(blocks)

    def kernel(*refs):
        groups = takes(refs, many, many, *[7] * many)
        greet(False, True)
        run_all(
            [
                scatter_ranks(groups[0][at], groups[1][at], *groups[2 + at][:4], groups[2 + at][4:])
                for at in range(many)
            ]
        )

    scratch = []
    for block in blocks:
        scratch += scatter_ranks_scratch(*block.shape[1:])
    return call(
        kernel,
        number,
        blocks,
        [HBM] * many,
        [shape(block.shape[1:], F32) for block in blocks],
        [VMEM] * many,
        scratch,
        name,
    )


def backward_last(blocks, news, second, modulation, cond_cut, time_slope):
    many = len(blocks)
    rows, width = second.shape

    def kernel(*refs):
        groups = takes(refs, many + 5, many + 4, 5, 12, *[14] * many)
        args, outs, scratch, sems = groups[:4]
        greet(True, True)
        run_all(
            [condition_backward(*args[many:], outs[many:], scratch, sems)]
            + [
                scatter_owners(args[at], outs[at], *groups[4 + at][:5], groups[4 + at][5:])
                for at in range(many)
            ]
        )

    scratch = [
        pltpu.VMEM((4,) + news.shape, F32),
        pltpu.VMEM(news.shape, F32),
        pltpu.VMEM((8, 8, rows), F32),
        pltpu.VMEM((8, 8, rows), F32),
        pltpu.VMEM((8, 8, rows), F32),
        DMA((3,)),
        DMA((4,)),
    ] + SWAP_SEMS * 5
    for block in blocks:
        scratch += scatter_owners_scratch(*block.shape[1:])
    return call(
        kernel,
        8,
        tuple(blocks) + (news, second, modulation, cond_cut, time_slope),
        [HBM] * many + [VMEM] * 5,
        [shape((4,) + block.shape[1:], LOW) for block in blocks]
        + [
            shape(news.shape, F32),
            shape((8, width), F32),
            shape((8, 8, rows), F32),
            shape((8, 1, modulation.shape[1]), F32),
        ],
        [HBM] * many + [VMEM] * 4,
        scratch,
        "backward_last",
    )


def sum_owners(number, value, name):
    if not fast():
        return lax.psum(value, "fsdp")

    def kernel(src, out, boxes, *sems):
        owner = lax.axis_index("fsdp")
        greet(True, False)
        sends = Sends()
        boxes[owner] = src[...]
        swap_start(sends, lambda to: src, boxes, *sems)
        swap_wait(boxes, sems[1])
        total = boxes[0]
        for of in range(1, 8):
            total = total + boxes[of]
        out[...] = total
        sends.finish()

    block = jnp.full((8, 128), value, F32)
    total = call(
        kernel, number, (block,), [VMEM], shape((8, 128), F32), VMEM, [pltpu.VMEM((8, 8, 128), F32)] + SWAP_SEMS, name
    )
    return total[0, 0]


def attend(query, keys, values):
    score_scale = 1.0 / math.sqrt(keys.shape[-1])
    scores = mixed_dot("qhd,khd->hqk", query, keys) * score_scale
    top = jnp.max(scores, axis=-1, keepdims=True)
    expo = jnp.exp(scores - top)
    total = jnp.sum(expo, axis=-1, keepdims=True)
    probs = (expo / total).astype(LOW)
    mixed = mixed_dot("hqk,khd->qhd", probs, values)
    return mixed.astype(LOW), (top + jnp.log(total))[..., 0]


def attend_back(query, keys, values, d_mixed, log_total):
    length, heads_here, head_dim = query.shape
    block = min(512, length)
    count = length // block
    score_scale = 1.0 / math.sqrt(head_dim)

    def back_block(carry, pieces):
        d_keys, d_values = carry
        query_block, d_block, log_block = pieces
        scores = mixed_dot("qhd,khd->hqk", query_block, keys) * score_scale
        probs = jnp.exp(scores - log_block[..., None])
        d_probs = mixed_dot("qhd,khd->hqk", d_block, values)
        delta = jnp.sum(probs * d_probs, axis=-1, keepdims=True)
        d_scores = (probs * (d_probs - delta)).astype(LOW)
        d_query = mixed_dot("hqk,khd->qhd", d_scores, keys) * score_scale
        d_keys = d_keys + mixed_dot("hqk,qhd->khd", d_scores, query_block) * score_scale
        d_values = d_values + mixed_dot("hqk,qhd->khd", probs.astype(LOW), d_block)
        return ((d_keys, d_values), d_query)

    empty = jnp.zeros((length, heads_here, head_dim), jnp.float32)
    blocked = (count, block, heads_here, head_dim)
    logs = log_total.reshape(heads_here, count, block).transpose(1, 0, 2)
    (d_keys, d_values), d_query = lax.scan(
        back_block, (empty, empty), (query.reshape(blocked), d_mixed.reshape(blocked), logs)
    )
    flat = (length, heads_here * head_dim)
    return jnp.concatenate(
        [d_query.reshape(flat), d_keys.reshape(flat), d_values.reshape(flat)], axis=1
    ).astype(LOW)


def adam_step(weight, moment, square, gradient, factor):
    clipped = gradient * factor
    moment_next = beta_one * moment + (1.0 - beta_one) * clipped
    square_next = beta_two * square + (1.0 - beta_two) * clipped * clipped
    moment_hat = moment_next / (1.0 - beta_one**STEP)
    square_hat = square_next / (1.0 - beta_two**STEP)
    master = weight - learn_rate * (
        moment_hat / (jnp.sqrt(square_hat) + adam_eps) + weight_decay * weight
    )
    return (master, moment_next, square_next)


def condition_start(latent_tokens, w_in, w_out, biases, timesteps, labels, time_first, time_second, class_table, modulation):
    owners, owner = lax.axis_size("fsdp"), lax.axis_index("fsdp")
    share = biases.shape[0]
    width = time_first.shape[1]
    first, second = time_first.astype(LOW), time_second.astype(LOW)
    table, modulation_low = class_table.astype(LOW), modulation.astype(LOW)
    units = first.shape[0]
    bias_low = biases.astype(LOW).astype(F32)
    features = time_features(timesteps).astype(LOW)
    if fast():
        note = jnp.concatenate(
            [
                jnp.broadcast_to(bias_low, (owners, share)),
                features.astype(F32).reshape(owners, units),
                jnp.broadcast_to(labels.astype(F32), (owners, 1)),
                jnp.zeros((owners, 127 - units), F32),
            ],
            axis=1,
        )[:, None]
        w_in_all, w_out_all, tokens, notes, act, slope, cond_cut, cond, mod = forward_first(
            w_in, w_out, latent_tokens, note, first, second, table, modulation_low
        )
        notes = notes[:, 0]
        all_bias = notes[:, :share].reshape(owners * share)
        my_features = notes[:, share : share + units]
        all_labels = notes[:, share + units]
        mod_values = mod.reshape(owners * mod.shape[2])
        state = (first, second, modulation_low, my_features, all_labels, act, slope, cond_cut, cond)
        return w_in_all, w_out_all, tokens, all_bias, mod_values, state
    w_in_all, w_out_part = lax.all_gather(w_in, "fsdp", axis=0), lax.all_gather(w_out, "fsdp", axis=0)
    w_out_all = lax.all_gather(w_out_part, "seq", axis=0)
    tokens = lax.all_gather(latent_tokens, "seq", axis=0)
    note = jnp.concatenate([bias_low, features[0].astype(F32), labels.astype(F32)])
    notes = lax.all_gather(note, "fsdp", axis=0)
    all_bias = notes[:, :share].reshape(owners * share)
    my_features = mine(notes[:, share:-1], 1, owners, owner)
    all_labels = notes[:, -1]
    hidden_time = lax.psum(mixed_dot("bf,fd->bd", my_features.astype(LOW), first), "fsdp") + all_bias[:width]
    act, slope = silu_parts(mine(hidden_time, 1, owners, owner))
    act = act.astype(LOW)
    onehot = (all_labels[:, None] == jnp.arange(NCLS, dtype=F32)[None, :]).astype(LOW)
    cond_part = mixed_dot("bd,de->be", act, second)
    class_part = mixed_dot("bc,cd->bd", onehot, table)
    class_wide = lax.dynamic_update_slice(jnp.zeros_like(cond_part), class_part, (0, owner * class_part.shape[1]))
    cond = lax.psum(cond_part + class_wide, "fsdp") + all_bias[width : 2 * width]
    mod_part = mixed_dot("bd,de->be", silu_parts(cond)[0].astype(LOW), modulation_low)
    mod_values = pick(lax.all_gather(mod_part, "fsdp", axis=0), owner, 1).reshape(owners * mod_part.shape[1])
    state = (first, second, modulation_low, my_features, all_labels, act.astype(F32), slope, None, cond)
    return w_in_all, w_out_all, tokens, all_bias, mod_values, state


def condition_end(state, blocks, my_d_mod, tail, share):
    first, second, modulation_low, my_features, all_labels, act, slope, cond_cut, cond = state
    owners, owner, rank = lax.axis_size("fsdp"), lax.axis_index("fsdp"), lax.axis_index("seq")
    wide, width = modulation_low.shape[1], cond.shape[1]
    if fast():
        pad = -wide % 128
        tails = jnp.concatenate([jnp.zeros((owners * share - tail.shape[0],), F32), tail]).reshape(owners, share)
        news = jnp.concatenate(
            [my_d_mod.reshape(owners, wide), jnp.zeros((owners, pad), F32), tails], axis=1
        )[:, None]
        *grads, by_latent, d_cond, d_hid, sums = backward_last(blocks, news, second, modulation_low, cond_cut, slope)
        d_mod = by_latent[:, 0, :wide]
        my_tail = jnp.sum(by_latent[:, 0, wide + pad :], axis=0)
        d_hidden = d_hid.transpose(1, 0, 2).reshape(owners, width)
        front = jnp.concatenate([jnp.sum(d_hidden, axis=0), jnp.sum(d_cond, axis=0), sums.reshape(owners * wide)])
        count = front.shape[0] // share
        grad_bias = jnp.where(
            owner < count, pick(front.reshape(count, share), jnp.minimum(owner, count - 1)), my_tail
        )
    else:
        summed = [lax.psum_scatter(block.astype(F32), "fsdp", scatter_dimension=0, tiled=False) for block in blocks]
        grads = [lax.all_gather(block.astype(LOW), "seq", axis=0) for block in summed]
        all_d_mod = lax.all_gather(lax.psum(my_d_mod, "seq"), "fsdp", axis=0)
        d_mod = mine(all_d_mod, 1, owners, owner)
        part = high_dot(d_mod, modulation_low.astype(F32).T)
        d_cond = lax.psum(part, "fsdp") * silu_parts(cond)[1]
        d_time = high_dot(d_cond, second.astype(F32).T) * slope
        d_hidden = lax.all_gather(d_time, "fsdp", axis=0).transpose(1, 0, 2).reshape(owners, width)
        tail = lax.psum(tail, ("seq", "fsdp"))
        all_bias = jnp.concatenate(
            [jnp.sum(d_hidden, axis=0), jnp.sum(d_cond, axis=0), jnp.sum(all_d_mod, axis=0), tail]
        )
        grad_bias = mine(all_bias, 0, owners, owner)
    onehot = (all_labels[:, None] == jnp.arange(NCLS, dtype=F32)[None, :]).astype(F32)
    cond_act = silu_parts(cond)[0].astype(LOW).astype(F32)
    grad_mod = high_dot(cond_act.T, d_mod)
    grad_class = high_dot(onehot.T, mine(d_cond, 1, owners, owner))
    grad_second = high_dot(act.T, d_cond)
    grad_first = high_dot(my_features.T, d_hidden)
    condition_gradient = lax.dynamic_slice_in_dim(d_cond, owner, 1, 0)
    return grads, (grad_first, grad_second, grad_class, grad_mod), grad_bias, condition_gradient


def per_device(latents, timesteps, labels, upstream, *state):
    params, moments, squares = state[:9], state[9:18], state[18:]
    time_first, time_second, class_table, modulation, attend_in, attend_out, expand, contract, biases = params
    lat_dev, tok_rows, width = latents.shape
    assert lat_dev == 1
    hidden = expand.shape[1]
    ranks = lax.axis_size("seq")
    owners = lax.axis_size("fsdp")
    rank = lax.axis_index("seq")
    heads_here = H // ranks
    span = heads_here * HD
    length = ranks * tok_rows
    rows = width // owners
    unit = hidden // (owners * ranks)
    hid_here = owners * unit

    my_in = pick(attend_in.reshape(rows, 3, ranks, span), rank, 2).astype(LOW).reshape(rows, 3 * span)
    my_out = mine(attend_out, 1, ranks, rank).astype(LOW)
    my_up = pick(expand.reshape(rows, owners, ranks, unit), rank, 2).astype(LOW).reshape(rows, hid_here)
    my_down = mine(contract, 0, ranks, rank).astype(LOW)
    w_in, w_out, tokens, all_bias, mod_values, kept = condition_start(
        latents[0], my_in, my_out, biases, timesteps, labels, time_first, time_second, class_table, modulation
    )
    w_in = w_in.reshape(width, 3 * span)
    w_out = w_out.transpose(1, 2, 0, 3).reshape(width, width)
    inputs_low = tokens.reshape(length, width)
    w_up, w_down, d_out_low = gathers(2, [my_up, my_down], [upstream[0]], "forward_second")
    w_up, w_down = w_up.reshape(width, hid_here), w_down.reshape(hid_here, width)
    d_out_low = d_out_low.reshape(length, width)

    b_t1, b_t2, b_mod, b_q, b_v, b_out, b_up, b_down = split_biases(all_bias, width, hidden)
    mod_values = (mod_values + b_mod).reshape(6, 1, width)
    shift1, scale1, gate1, shift2, scale2, gate2 = [mod_values[index] for index in range(6)]

    inputs = inputs_low.astype(F32)
    norm_one, _ = layer_norm(inputs)
    h_attn = (norm_one * (1.0 + scale1) + shift1).astype(LOW)
    my_b_q, my_b_v = mine(b_q, 0, ranks, rank), mine(b_v, 0, ranks, rank)
    qkv_bias = jnp.concatenate([my_b_q, jnp.zeros_like(my_b_q), my_b_v])
    qkv = (mixed_dot("td,de->te", h_attn, w_in) + qkv_bias).astype(LOW)
    head_shape = (length, heads_here, HD)
    query, keys, values = [qkv[:, part * span : (part + 1) * span].reshape(head_shape) for part in range(3)]
    mixed_heads, log_total = attend(query, keys, values)
    (mixed,) = gathers(3, [], [mixed_heads.reshape(length, span)], "gather_mixed")
    mixed = mixed.transpose(1, 0, 2).reshape(length, width)
    attn_out = mixed_dot("td,de->te", mixed, w_out) + b_out
    middle = inputs + gate1 * attn_out
    norm_two, inverse_two = layer_norm(middle)
    h_mlp = (norm_two * (1.0 + scale2) + shift2).astype(LOW)

    my_b_up = pick(b_up.reshape(owners, ranks, unit), rank, 1).reshape(hid_here)
    pre_act = mixed_dot("td,df->tf", h_mlp, w_up) + my_b_up
    act_f, gelu_pull = jax.vjp(partial(jax.nn.gelu, approximate=True), pre_act)
    act = act_f.astype(LOW)
    by_rank = (ranks, tok_rows, width)
    by_owner = lambda block: block.astype(LOW).reshape((owners, -1) + block.shape[1:])
    mlp_part = mixed_dot("tf,fd->td", act, w_down).astype(LOW).reshape(by_rank)
    d_out = d_out_low.astype(F32)
    d_mlp = (d_out * gate2).astype(LOW)
    d_act = mixed_dot("td,fd->tf", d_mlp, w_down)
    d_pre = gelu_pull(d_act)[0].astype(LOW)
    d_hmlp_part = mixed_dot("tf,df->td", d_pre, w_up).astype(LOW).reshape(by_rank)
    d_hmlp, mlp_sum = rank_sums(4, [d_hmlp_part, mlp_part], "sum_feed")
    g_down = by_owner(mixed_dot("tf,td->fd", act, d_mlp))
    g_up = by_owner(mixed_dot("td,tf->df", h_mlp, d_pre))
    gb_up = jnp.sum(d_pre.astype(F32), axis=0)
    gb_down = jnp.sum(d_mlp.astype(F32), axis=0)

    own = lambda array: mine(array, 0, ranks, rank)
    my_attn_out, my_middle, my_norm_two, my_inverse_two = own(attn_out), own(middle), own(norm_two), own(inverse_two)
    my_d_out = upstream[0].astype(F32)
    mlp_out = mlp_sum + b_down
    output = (my_middle + gate2 * mlp_out).astype(LOW)
    d_gate2 = jnp.sum(my_d_out * mlp_out, axis=0)
    d_shift2 = jnp.sum(d_hmlp, axis=0)
    d_scale2 = jnp.sum(d_hmlp * my_norm_two, axis=0)
    d_middle = my_d_out + layer_norm_back(my_norm_two, my_inverse_two, d_hmlp * (1.0 + scale2))
    d_gate1 = jnp.sum(d_middle * my_attn_out, axis=0)
    my_d_attn = (d_middle * gate1).astype(LOW)
    (d_attn,) = gathers(5, [], [my_d_attn], "gather_d_attn")
    d_attn = d_attn.reshape(length, width)
    d_mixed = mixed_dot("te,de->td", d_attn, mine(w_out, 0, ranks, rank)).astype(LOW)
    g_out = by_owner(mixed_dot("td,te->de", mixed, mine(d_attn, 1, ranks, rank)))
    d_qkv = attend_back(query, keys, values, d_mixed.reshape(head_shape), log_total)
    g_in = by_owner(mixed_dot("td,te->de", h_attn, d_qkv))
    d_hattn_part = mixed_dot("te,de->td", d_qkv, w_in).astype(LOW).reshape(by_rank)
    (d_hattn,) = rank_sums(6, [d_hattn_part], "sum_attend")
    my_inputs = latents[0].astype(F32)
    my_norm_one, my_inverse_one = layer_norm(my_inputs)
    d_shift1 = jnp.sum(d_hattn, axis=0)
    d_scale1 = jnp.sum(d_hattn * my_norm_one, axis=0)
    input_gradient = d_middle + layer_norm_back(my_norm_one, my_inverse_one, d_hattn * (1.0 + scale1))

    my_d_mod = jnp.concatenate([d_shift1, d_scale1, d_gate1, d_shift2, d_scale2, d_gate2])
    gb_qv = jnp.sum(d_qkv.astype(F32), axis=0)
    wide = lambda part, size: lax.dynamic_update_slice(jnp.zeros((size,), F32), part, (rank * part.shape[0],))
    gb_up_wide = lax.dynamic_update_slice(
        jnp.zeros((owners, ranks, unit), F32), gb_up.reshape(owners, 1, unit), (0, rank, 0)
    ).reshape(hidden)
    gb_tail = jnp.concatenate(
        [
            wide(gb_qv[:span], width),
            wide(gb_qv[2 * span :], width),
            jnp.sum(my_d_attn.astype(F32), axis=0),
            gb_up_wide,
            jnp.where(rank == 0, gb_down, 0.0),
        ]
    )
    grads, small_grads, grad_bias, condition_gradient = condition_end(
        kept, [g_down, g_up, g_out, g_in], my_d_mod, gb_tail, biases.shape[0]
    )
    grad_down, grad_up, grad_out, grad_in = [grad.astype(F32) for grad in grads]
    grad_in = grad_in.reshape(ranks, rows, 3, span).transpose(1, 2, 0, 3).reshape(rows, 3 * width)
    grad_out = grad_out.transpose(1, 0, 2).reshape(rows, width)
    grad_up = grad_up.reshape(ranks, rows, owners, unit).transpose(1, 2, 0, 3).reshape(rows, hidden)
    grad_down = grad_down.reshape(contract.shape)
    gradients = small_grads + (grad_in, grad_out, grad_up, grad_down, grad_bias)
    local_sum = sum(jnp.sum(gradient * gradient) for gradient in gradients)
    norm_before = jnp.sqrt(sum_owners(7, local_sum, "sum_squares"))
    factor = clip_limit / jnp.maximum(norm_before, clip_limit)
    results = [
        adam_step(params[index], moments[index], squares[index], gradients[index], factor)
        for index in range(9)
    ]
    return (
        (output[None], input_gradient[None], condition_gradient, norm_before)
        + gradients
        + tuple(result[0] for result in results)
        + tuple(result[1] for result in results)
        + tuple(result[2] for result in results)
    )


def solution(mesh):
    tokens = P("fsdp", "seq", None)
    rows, columns = P("fsdp", None), P(None, "fsdp")
    weights = (rows, rows, columns, columns, rows, rows, rows, rows, P("fsdp"))
    return jax.shard_map(
        per_device,
        mesh=mesh,
        in_specs=(tokens, P("fsdp"), P("fsdp"), tokens) + weights * 3,
        out_specs=(tokens, tokens, rows, P()) + weights * 4,
        check_vma=False,
    )
```

```python
from functools import partial
import math

import jax
import jax.numpy as jnp
from jax import lax
from jax.experimental import pallas as pl
from jax.experimental.pallas import tpu as pltpu
from jax.sharding import PartitionSpec as P

H = 16
HD = 72
FREQ = 256
NCLS = 1000
STEP = 10


HIGH = lax.Precision.HIGHEST
LOW = jnp.bfloat16
norm_eps = 1e-06
beta_one = 0.9
beta_two = 0.999
learn_rate = 0.04
weight_decay = 0.01
adam_eps = 1e-08
clip_limit = 1.0


def layer_norm(value):
    centre = value - jnp.mean(value, axis=-1, keepdims=True)
    spread = jnp.mean(centre * centre, axis=-1, keepdims=True)
    inverse = lax.rsqrt(spread + norm_eps)
    return centre * inverse, inverse


def layer_norm_back(norm, inverse, grad):
    first = jnp.mean(grad, axis=-1, keepdims=True)
    second = jnp.mean(grad * norm, axis=-1, keepdims=True)
    return inverse * (grad - first - norm * second)


def silu_parts(value):
    gate = jax.nn.sigmoid(value)
    return value * gate, gate * (1.0 + value * (1.0 - gate))


def time_features(timesteps):
    half = FREQ // 2
    freqs = jnp.exp(-math.log(10000.0) * jnp.arange(half, dtype=jnp.float32) / half)
    angles = timesteps.astype(jnp.float32)[:, None] * freqs[None, :]
    return jnp.concatenate([jnp.cos(angles), jnp.sin(angles)], axis=-1)


def split_biases(biases, width, hidden):
    widths = [width, width, 6 * width, width, width, width, hidden, width]
    pieces = []
    start = 0
    for length in widths:
        pieces.append(biases[start : start + length])
        start = start + length
    return pieces


def high_dot(left, right):
    return jnp.dot(left, right, precision=HIGH, preferred_element_type=jnp.float32)


def mixed_dot(form, left, right):
    return jnp.einsum(form, left, right, preferred_element_type=jnp.float32)


def pick(array, index, axis=0):
    return lax.dynamic_index_in_dim(array, index, axis, keepdims=False)


def mine(array, axis, parts, index):
    size = array.shape[axis] // parts
    return lax.dynamic_slice_in_dim(array, index * size, size, axis)


HBM = pl.BlockSpec(memory_space=pl.ANY)
VMEM = pl.BlockSpec(memory_space=pltpu.VMEM)
DMA = pltpu.SemaphoreType.DMA
F32 = jnp.float32


def fast():
    return lax.axis_size("fsdp") == 8 and lax.axis_size("seq") == 4


def places():
    owner, rank = lax.axis_index("fsdp"), lax.axis_index("seq")
    return owner, rank, lax.div(owner, 2), lax.rem(owner, 2), lax.div(rank, 2), lax.rem(rank, 2)


def remote(src, dst, sent, landed, **where):
    return pltpu.make_async_remote_copy(
        src_ref=src, dst_ref=dst, send_sem=sent, recv_sem=landed, device_id=where, device_id_type=pl.DeviceIdType.MESH
    )


def arrived(dst, landed, **where):
    remote(dst, dst, landed, landed, **where).wait_recv()


def greet(over_owners, over_ranks):
    owner, rank, *_ = places()
    barrier = pltpu.get_barrier_semaphore()
    count = 0
    if over_owners:
        for step in range(1, 8):
            pl.semaphore_signal(
                barrier, inc=1, device_id={"fsdp": lax.rem(owner + step, 8)}, device_id_type=pl.DeviceIdType.MESH
            )
        count += 7
    if over_ranks:
        for step in range(1, 4):
            pl.semaphore_signal(
                barrier, inc=1, device_id={"seq": lax.rem(rank + step, 4)}, device_id_type=pl.DeviceIdType.MESH
            )
        count += 3
    pl.semaphore_wait(barrier, count)


def run_all(parts):
    parts = list(parts)
    while parts:
        for part in list(parts):
            try:
                next(part)
            except StopIteration:
                parts.remove(part)


class Sends:
    def __init__(self):
        self.live = []

    def start(self, copy, when=None):
        self.live.append((copy, when))
        if when is None:
            copy.start()
        else:
            pl.when(when)(copy.start)

    def finish(self):
        for copy, when in self.live:
            wait = copy.wait_send if hasattr(copy, "wait_send") else copy.wait
            if when is None:
                wait()
            else:
                pl.when(when)(wait)


def gather_owners(src, out, sems):
    own_sem, sent, landed = sems
    owner, rank, z, y, x, core = places()
    mate = owner + 1 - 2 * y
    sends = Sends()
    local = pltpu.make_async_copy(src, out.at[owner], own_sem)
    local.start()
    sends.start(remote(src, out.at[owner], sent.at[0, 0], landed.at[owner], fsdp=owner + 2), z < 3)
    sends.start(remote(src, out.at[owner], sent.at[0, 1], landed.at[owner], fsdp=owner - 2), z > 0)
    sends.start(remote(src, out.at[owner], sent.at[0, 2], landed.at[owner], fsdp=mate))
    yield
    for far in (1, 2, 3):
        for sign in (-1, 1):
            block = owner + sign * 2 * far
            here = (z >= far) if sign < 0 else (z + far <= 3)
            on = (z < 3) if sign < 0 else (z > 0)
            at = far if sign < 0 else 3 + far
            pl.when(here)(lambda: arrived(out.at[block], landed.at[block], fsdp=mate))
            sends.start(
                remote(out.at[block], out.at[block], sent.at[at, 0], landed.at[block], fsdp=owner - sign * 2), here & on
            )
            sends.start(remote(out.at[block], out.at[block], sent.at[at, 2], landed.at[block], fsdp=mate), here)
            yield
    for step in range(4):
        block = step * 2 + 1 - y
        arrived(out.at[block], landed.at[block], fsdp=mate)
    local.wait()
    sends.finish()


GATHER_OWNERS_SEMS = [DMA(()), DMA((7, 3)), DMA((8,))]


def gather_ranks(src, out, sems, local_copy=True):
    own_sem, sent, landed = sems
    owner, rank, z, y, x, core = places()
    mate, across, last = x * 2 + 1 - core, (1 - x) * 2 + core, (1 - x) * 2 + 1 - core
    sends = Sends()
    local = None
    if local_copy:
        local = pltpu.make_async_copy(src, out.at[rank], own_sem)
        local.start()
    sends.start(remote(src, out.at[rank], sent.at[0], landed.at[rank], seq=across))
    sends.start(remote(src, out.at[rank], sent.at[1], landed.at[rank], seq=mate))
    yield
    yield
    arrived(out.at[across], landed.at[across], seq=across)
    sends.start(remote(out.at[across], out.at[across], sent.at[2], landed.at[across], seq=mate))
    yield
    arrived(out.at[mate], landed.at[mate], seq=mate)
    arrived(out.at[last], landed.at[last], seq=mate)
    if local is not None:
        local.wait()
    sends.finish()


GATHER_RANKS_SEMS = [DMA(()), DMA((3,)), DMA((4,))]


def by_rows(count, body, step=16):
    def one(index, carry):
        body(pl.ds(pl.multiple_of(index * step, step), step))
        return carry

    lax.fori_loop(0, count // step, one, 0)


def scatter_ranks(parts, out, own, mail, leave, enter, sems):
    own_sem, sent, landed = sems
    owner, rank, z, y, x, core = places()
    mate, across = x * 2 + 1 - core, (1 - x) * 2 + core
    sends = Sends()
    loads = []
    for step in (1, 0):
        to = lax.rem(x + step, 2)
        loads.append(pltpu.make_async_copy(parts.at[to * 2 + core], own.at[step], own_sem.at[step]))
        loads[-1].start()
        sends.start(remote(parts.at[to * 2 + 1 - core], mail.at[step], sent.at[step], landed.at[step], seq=mate))
    yield
    loads[0].wait()
    arrived(mail.at[1], landed.at[1], seq=mate)

    def first(rows):
        leave[rows] = (own[1, rows].astype(F32) + mail[1, rows].astype(F32)).astype(LOW)

    by_rows(out.shape[0], first)
    sends.start(remote(leave, enter, sent.at[2], landed.at[2], seq=across))
    yield
    loads[1].wait()
    arrived(mail.at[0], landed.at[0], seq=mate)
    yield
    arrived(enter, landed.at[2], seq=across)

    def last(rows):
        out[rows] = own[0, rows].astype(F32) + mail[0, rows].astype(F32) + enter[rows].astype(F32)

    by_rows(out.shape[0], last)
    sends.finish()


def scatter_ranks_scratch(rows, columns):
    return [
        pltpu.VMEM((2, rows, columns), LOW),
        pltpu.VMEM((2, rows, columns), LOW),
        pltpu.VMEM((rows, columns), LOW),
        pltpu.VMEM((rows, columns), LOW),
        DMA((2,)),
        DMA((3,)),
        DMA((3,)),
    ]


def scatter_owners(parts, out, own, mail, rise, fall, leave, sems):
    own_sem, y_sent, y_landed, z_sent, up_landed, down_landed = sems[:6]
    owner, rank, z, y, x, core = places()
    mate = owner + 1 - 2 * y
    rows_here = own.shape[1]
    sends = Sends()
    loads = {}
    for to in (3, 0, 2, 1):
        sends.start(remote(parts.at[to * 2 + 1 - y], mail.at[to], y_sent.at[to], y_landed.at[to], fsdp=mate))
        loads[to] = pltpu.make_async_copy(parts.at[to * 2 + y], own.at[to], own_sem.at[to])
        loads[to].start()
        yield
    for to, up in ((3, True), (0, False), (2, True), (1, False), (1, True), (2, False)):
        here = (z < to) if up else (z > to)
        more = (z > 0) if up else (z < 3)
        box, box_landed = (rise, up_landed) if up else (fall, down_landed)

        def total(to=to, more=more, box=box, box_landed=box_landed):
            loads[to].wait()
            arrived(mail.at[to], y_landed.at[to], fsdp=mate)

            def start(rows):
                leave[to, rows] = (own[to, rows].astype(F32) + mail[to, rows].astype(F32)).astype(LOW)

            def add(rows):
                leave[to, rows] = (
                    own[to, rows].astype(F32) + mail[to, rows].astype(F32) + box[to, rows].astype(F32)
                ).astype(LOW)

            @pl.when(more)
            def _():
                arrived(box.at[to], box_landed.at[to], fsdp=mate)
                by_rows(rows_here, add)

            @pl.when(jnp.logical_not(more))
            def _():
                by_rows(rows_here, start)

        pl.when(here)(total)
        sends.start(
            remote(
                leave.at[to], box.at[to], z_sent.at[to], box_landed.at[to], fsdp=owner + 2 if up else owner - 2
            ),
            here,
        )
        yield
    for to in range(4):
        at_home = z == to

        @pl.when(at_home)
        def _(to=to):
            loads[to].wait()
            arrived(mail.at[to], y_landed.at[to], fsdp=mate)
            if to > 0:
                arrived(rise.at[to], up_landed.at[to], fsdp=mate)
            if to < 3:
                arrived(fall.at[to], down_landed.at[to], fsdp=mate)

            def end(rows):
                value = own[to, rows].astype(F32) + mail[to, rows].astype(F32)
                if to > 0:
                    value = value + rise[to, rows].astype(F32)
                if to < 3:
                    value = value + fall[to, rows].astype(F32)
                leave[to, rows] = value.astype(LOW)

            by_rows(rows_here, end)

    yield from gather_ranks(leave.at[z], out, sems[6:])
    sends.finish()


def scatter_owners_scratch(rows, columns):
    return [pltpu.VMEM((4, rows, columns), LOW)] * 5 + [DMA((4,))] * 6 + GATHER_RANKS_SEMS


def swap_start(sends, src_of, dst, sent, landed):
    owner = lax.axis_index("fsdp")
    for step in range(1, 8):
        to = lax.rem(owner + step, 8)
        sends.start(remote(src_of(to), dst.at[owner], sent.at[step - 1], landed.at[owner], fsdp=to))


def swap_wait(dst, landed):
    owner = lax.axis_index("fsdp")
    for step in range(1, 8):
        of = lax.rem(owner + step, 8)
        arrived(dst.at[of], landed.at[of], fsdp=of)


SWAP_SEMS = [DMA((7,)), DMA((8,))]


def low_dot(left, right, contract):
    return lax.dot_general(left, right, ((contract[:1], contract[1:]), ((), ())), preferred_element_type=F32)


def fine_dot(left, right, contract):
    high = left.astype(LOW)
    rest = left - high.astype(F32)
    return low_dot(high, right, contract) + low_dot(rest.astype(LOW), right, contract)


def stack_rows(ref):
    return jnp.concatenate([ref[index] for index in range(8)], axis=0)


def condition_forward(note, first, second, table, modulation, outs, scratch, sems):
    notes, act_out, slope_out, cond_cut, cond_out, mod = outs
    send_cut, hid_in, cond_in, bias_cut, mod_cut = scratch
    owner = lax.axis_index("fsdp")
    cut = second.shape[0]
    share = note.shape[2] - 128
    sends = Sends()
    notes[owner] = note[owner]
    swap_start(sends, lambda to: note.at[to], notes, *sems[0:2])
    yield
    swap_wait(notes, sems[1])
    rows = stack_rows(notes)
    feats = rows[:, share : share + first.shape[0]].astype(LOW)
    label = rows[:, share + first.shape[0] : share + first.shape[0] + 1]
    hidden = low_dot(feats, first[...], (1, 0))
    for to in range(8):
        send_cut[0, to] = hidden[:, to * cut : (to + 1) * cut]
        bias_cut[0, to] = rows[0:1, to * cut : (to + 1) * cut]
        bias_cut[1, to] = rows[0:1, (8 + to) * cut : (9 + to) * cut]
    hid_in[owner] = send_cut[0, owner]
    swap_start(sends, lambda to: send_cut.at[0, to], hid_in, *sems[2:4])
    yield
    classes = lax.broadcasted_iota(jnp.int32, (8, table.shape[0]), 1).astype(F32)
    onehot = (label == classes).astype(F32).astype(LOW)
    from_class = low_dot(onehot, table[...], (1, 0))
    swap_wait(hid_in, sems[3])
    hidden_cut = bias_cut[0, owner] + jnp.zeros((8, cut), F32)
    for of in range(8):
        hidden_cut = hidden_cut + hid_in[of]
    act, slope = silu_parts(hidden_cut)
    act = act.astype(LOW)
    act_out[...] = act.astype(F32)
    slope_out[...] = slope
    part = low_dot(act, second[...], (1, 0))
    for to in range(8):
        send_cut[1, to] = part[:, to * cut : (to + 1) * cut]
    cond_in[owner] = send_cut[1, owner]
    swap_start(sends, lambda to: send_cut.at[1, to], cond_in, *sems[4:6])
    yield
    swap_wait(cond_in, sems[5])
    mine_cond = bias_cut[1, owner] + from_class
    for of in range(8):
        mine_cond = mine_cond + cond_in[of]
    cond_cut[owner] = mine_cond
    swap_start(sends, lambda to: cond_cut.at[owner], cond_cut, *sems[6:8])
    yield
    swap_wait(cond_cut, sems[7])
    for of in range(8):
        cond_out[:, of * cut : (of + 1) * cut] = cond_cut[of]
    cond_act = silu_parts(cond_out[...])[0].astype(LOW)
    values = low_dot(cond_act, modulation[...], (1, 0))
    for to in range(8):
        mod_cut[to] = values[to : to + 1]
    mod[owner] = mod_cut[owner]
    swap_start(sends, lambda to: mod_cut.at[to], mod, *sems[8:10])
    yield
    swap_wait(mod, sems[9])
    sends.finish()


def condition_backward(news, second, modulation, cond_cut, time_slope, outs, scratch, sems):
    by_latent, d_cond_out, d_hid_cut, sums = outs
    rank_news, owner_news, d_cut, d_in, d_cond_cut = scratch
    owner, rank, *_ = places()
    cut = second.shape[0]
    wide = modulation.shape[1]
    sends = Sends()
    for step in range(1, 4):
        to = lax.rem(rank + step, 4)
        sends.start(remote(news, rank_news.at[rank], sems[0].at[step - 1], sems[1].at[rank], seq=to))
    yield
    for step in range(1, 4):
        of = lax.rem(rank + step, 4)
        arrived(rank_news.at[of], sems[1].at[of], seq=of)
    rank_news[rank] = news[...]
    for to in range(8):
        owner_news[to] = rank_news[0, to] + rank_news[1, to] + rank_news[2, to] + rank_news[3, to]
    by_latent[owner] = owner_news[owner]
    swap_start(sends, lambda to: owner_news.at[to], by_latent, *sems[2:4])
    yield
    swap_wait(by_latent, sems[3])
    d_mod = stack_rows(by_latent)[:, :wide]
    part = fine_dot(d_mod, modulation[...], (1, 1))
    for to in range(8):
        d_cut[to] = part[:, to * cut : (to + 1) * cut]
    d_in[owner] = d_cut[owner]
    swap_start(sends, lambda to: d_cut.at[to], d_in, *sems[4:6])
    sums[owner] = jnp.sum(d_mod, axis=0, keepdims=True)
    swap_start(sends, lambda to: sums.at[owner], sums, *sems[6:8])
    yield
    swap_wait(d_in, sems[5])
    total = d_in[0]
    for of in range(1, 8):
        total = total + d_in[of]
    d_cond_cut[owner] = total * silu_parts(cond_cut[owner])[1]
    swap_start(sends, lambda to: d_cond_cut.at[owner], d_cond_cut, *sems[8:10])
    yield
    swap_wait(d_cond_cut, sems[9])
    for of in range(8):
        d_cond_out[:, of * cut : (of + 1) * cut] = d_cond_cut[of]
    d_hid_cut[owner] = fine_dot(d_cond_out[...], second[...], (1, 1)) * time_slope[...]
    swap_start(sends, lambda to: d_hid_cut.at[owner], d_hid_cut, *sems[10:12])
    yield
    swap_wait(d_hid_cut, sems[11])
    swap_wait(sums, sems[7])
    sends.finish()


def takes(refs, *counts):
    refs = list(refs)
    groups = []
    for count in counts:
        groups.append(refs[:count])
        refs = refs[count:]
    assert not refs
    return groups


def call(kernel, number, args, in_specs, outs, out_specs, scratch, name):
    return pl.pallas_call(
        kernel,
        out_shape=outs,
        in_specs=in_specs,
        out_specs=out_specs,
        scratch_shapes=scratch,
        compiler_params=pltpu.CompilerParams(
            collective_id=number, has_side_effects=True, vmem_limit_bytes=60 * 1024 * 1024
        ),
        name=name,
    )(*args)


def shape(dims, kind):
    return jax.ShapeDtypeStruct(tuple(dims), kind)


def forward_first(w_io, tokens, note, first, second, table, modulation):
    rows, width = second.shape
    wide = modulation.shape[1]

    def kernel(*refs):
        args, outs, scratch, cond_sems, io_sems, token_sems = takes(refs, 7, 8, 5, 10, 3, 3)
        greet(True, True)
        run_all(
            [
                condition_forward(args[2], *args[3:7], outs[2:8], scratch, cond_sems),
                gather_ranks(args[1], outs[1], token_sems),
                gather_owners(args[0], outs[0], io_sems),
            ]
        )

    return call(
        kernel,
        1,
        (w_io, tokens, note, first, second, table, modulation),
        [VMEM] * 7,
        [
            shape((8,) + w_io.shape, LOW),
            shape((4,) + tokens.shape, LOW),
            shape(note.shape, F32),
            shape((8, rows), F32),
            shape((8, rows), F32),
            shape((8, 8, rows), F32),
            shape((8, width), F32),
            shape((8, 1, wide), F32),
        ],
        [HBM] * 2 + [VMEM] * 6,
        [
            pltpu.VMEM((2, 8, 8, rows), F32),
            pltpu.VMEM((8, 8, rows), F32),
            pltpu.VMEM((8, 8, rows), F32),
            pltpu.VMEM((2, 8, 1, rows), F32),
            pltpu.VMEM((8, 1, wide), F32),
        ]
        + SWAP_SEMS * 5
        + GATHER_OWNERS_SEMS
        + GATHER_RANKS_SEMS,
        "forward_first",
    )


QUERIES = 256


def block_of(index, size=QUERIES):
    return pl.ds(pl.multiple_of(index * size, size), size)


def attend_heads(qkv, mixed, logs, head_rows, heads):
    length = qkv.shape[0]
    span = heads * HD
    scale = 1.0 / math.sqrt(HD)
    for head in range(heads):
        for part in range(3):
            start = part * span + head * HD
            head_rows[part] = qkv[:, start : start + HD]

        def block(index, carry):
            query = head_rows[0, block_of(index)]
            scores = low_dot(head_rows[1], query, (1, 1)) * scale
            top = jnp.max(scores, axis=0, keepdims=True)
            expo = jnp.exp(scores - top)
            total = jnp.sum(expo, axis=0, keepdims=True)
            probs = (expo * (1.0 / total)).astype(LOW)
            mixed[block_of(index), head * HD : (head + 1) * HD] = low_dot(head_rows[2], probs, (0, 0)).T.astype(LOW)
            logs[head, index] = top + jnp.log(total)
            return carry

        lax.fori_loop(0, length // QUERIES, block, 0)
        yield


def attend_heads_back(qkv, logs, d_mixed, d_qkv, head_rows, d_head, d_keys, d_values, heads):
    length = qkv.shape[0]
    span = heads * HD
    scale = 1.0 / math.sqrt(HD)
    for head in range(heads):
        lanes = slice(head * HD, (head + 1) * HD)
        for part in range(3):
            start = part * span + head * HD
            head_rows[part] = qkv[:, start : start + HD]
        d_head[...] = d_mixed[:, lanes]
        d_keys[...] = jnp.zeros_like(d_keys)
        d_values[...] = jnp.zeros_like(d_values)

        def block(index, carry):
            query, d_block = head_rows[0, block_of(index)], d_head[block_of(index)]
            scores = low_dot(head_rows[1], query, (1, 1)) * scale
            probs = jnp.exp(scores - logs[head, index])
            d_probs = low_dot(head_rows[2], d_block, (1, 1))
            delta = jnp.sum(probs * d_probs, axis=0, keepdims=True)
            d_scores = (probs * (d_probs - delta)).astype(LOW)
            d_keys[...] += low_dot(d_scores, query, (1, 0))
            d_values[...] += low_dot(probs.astype(LOW), d_block, (1, 0))
            d_query = low_dot(head_rows[1], d_scores, (0, 0)).T * scale
            d_qkv[block_of(index), lanes] = d_query.astype(LOW)
            return carry

        lax.fori_loop(0, length // QUERIES, block, 0)
        d_qkv[:, span + head * HD : span + (head + 1) * HD] = (d_keys[...] * scale).astype(LOW)
        d_qkv[:, 2 * span + head * HD : 2 * span + (head + 1) * HD] = d_values[...].astype(LOW)
        yield


def forward_attention(qkv, w_up, w_down, upstream, w_out):
    length = qkv.shape[0]
    heads = qkv.shape[1] // (3 * HD)
    span = heads * HD

    def kernel(*refs):
        args, outs, scratch, up_sems, down_sems, token_sems, out_sems, mixed_sems = takes(refs, 5, 6, 2, 3, 3, 3, 3, 3)
        mixed_here, head_rows = scratch
        greet(True, True)

        def attention():
            yield from attend_heads(args[0], mixed_here, outs[5], head_rows, heads)
            yield from gather_ranks(mixed_here, outs[4], mixed_sems)

        run_all(
            [
                gather_owners(args[1], outs[0], up_sems),
                gather_owners(args[2], outs[1], down_sems),
                gather_ranks(args[4], outs[3], out_sems),
                attention(),
                gather_ranks(args[3], outs[2], token_sems),
            ]
        )

    return call(
        kernel,
        2,
        (qkv, w_up, w_down, upstream, w_out),
        [VMEM] * 5,
        [
            shape((8,) + w_up.shape, LOW),
            shape((8,) + w_down.shape, LOW),
            shape((4,) + upstream.shape, LOW),
            shape((4,) + w_out.shape, LOW),
            shape((4, length, span), LOW),
            shape((heads, length // QUERIES, 1, QUERIES), F32),
        ],
        [HBM] * 5 + [VMEM],
        [pltpu.VMEM((length, span), LOW), pltpu.VMEM((3, length, HD), LOW)]
        + GATHER_OWNERS_SEMS * 2
        + GATHER_RANKS_SEMS * 3,
        "forward_attention",
    )


def gathers(number, by_owner, by_rank, name):
    if not fast():
        return [lax.all_gather(block, "fsdp", axis=0) for block in by_owner] + [
            lax.all_gather(block, "seq", axis=0) for block in by_rank
        ]
    many, few = len(by_owner), len(by_rank)

    def kernel(*refs):
        groups = takes(refs, many + few, many + few, *[3] * (many + few))
        args, outs, sems = groups[0], groups[1], groups[2:]
        greet(many > 0, few > 0)
        run_all(
            [gather_owners(args[at], outs[at], sems[at]) for at in range(many)]
            + [gather_ranks(args[at], outs[at], sems[at]) for at in range(many, many + few)]
        )

    blocks = list(by_owner) + list(by_rank)
    return call(
        kernel,
        number,
        blocks,
        [VMEM] * len(blocks),
        [shape((8 if at < many else 4,) + block.shape, block.dtype) for at, block in enumerate(blocks)],
        [HBM] * len(blocks),
        GATHER_OWNERS_SEMS * many + GATHER_RANKS_SEMS * few,
        name,
    )


def rank_sums(number, blocks, name):
    if not fast():
        return [lax.psum_scatter(block.astype(F32), "seq", scatter_dimension=0, tiled=False) for block in blocks]
    many = len(blocks)

    def kernel(*refs):
        groups = takes(refs, many, many, *[7] * many)
        greet(False, True)
        run_all(
            [
                scatter_ranks(groups[0][at], groups[1][at], *groups[2 + at][:4], groups[2 + at][4:])
                for at in range(many)
            ]
        )

    scratch = []
    for block in blocks:
        scratch += scatter_ranks_scratch(*block.shape[1:])
    return call(
        kernel,
        number,
        blocks,
        [HBM] * many,
        [shape(block.shape[1:], F32) for block in blocks],
        [VMEM] * many,
        scratch,
        name,
    )


def row_cuts(rows):
    half = (rows // 2 + 15) // 16 * 16
    return [(0, half), (half, rows - half)]


def scatter_items(parts, outs, scratch):
    items, at = [], 0
    for part, out in zip(parts, outs):
        for start, count in row_cuts(part.shape[1]):
            rows = pl.ds(start, count)
            refs = scratch[at]
            items.append(scatter_owners(part.at[:, rows], out.at[:, rows], *refs[:5], refs[5:]))
            at += 1
    return items


def scatter_items_scratch(blocks):
    scratch = []
    for block in blocks:
        for _, count in row_cuts(block.shape[1]):
            scratch += scatter_owners_scratch(count, block.shape[2])
    return scratch


def backward_attention(g_up, g_down, my_d_attn, mlp_part, qkv, w_out, logs, units):
    length = qkv.shape[0]
    heads = qkv.shape[1] // (3 * HD)
    span = heads * HD
    rows, width = my_d_attn.shape

    def kernel(*refs):
        groups = takes(refs, 7, 5, 7, 7, 3, *[14] * 4)
        args, outs, scratch, sum_scratch, token_sems = groups[:5]
        d_mixed, head_rows, d_head, d_keys, d_values, up_all, _ = scratch
        greet(True, True)

        def attention():
            yield from gather_ranks(args[2], outs[2], token_sems)
            for part in range(4):
                d_mixed[part * rows : (part + 1) * rows] = low_dot(outs[2][part], args[5][...], (1, 1)).astype(LOW)
            yield
            yield from attend_heads_back(
                args[4], args[6], d_mixed, outs[4], head_rows, d_head, d_keys, d_values, heads
            )

        run_all(
            scatter_items(args[:2], (up_all, outs[1]), groups[5:])
            + [attention(), scatter_ranks(args[3], outs[3], *sum_scratch[:4], sum_scratch[4:])]
        )
        owners = up_all.shape[2] // units

        def assemble(at):
            for part in range(4):
                for owner in range(owners):
                    to = (owner * 4 + part) * units
                    outs[0][at, to : to + units] = up_all[part, at, owner * units : (owner + 1) * units]

        by_rows(up_all.shape[1], assemble)

    return call(
        kernel,
        9,
        (g_up, g_down, my_d_attn, mlp_part, qkv, w_out, logs),
        [HBM, HBM, VMEM, HBM, VMEM, VMEM, VMEM],
        [
            shape((g_up.shape[1], 4 * g_up.shape[2]), LOW),
            shape((4,) + g_down.shape[1:], LOW),
            shape((4,) + my_d_attn.shape, LOW),
            shape(my_d_attn.shape, F32),
            shape(qkv.shape, LOW),
        ],
        [VMEM, HBM, VMEM, VMEM, VMEM],
        [
            pltpu.VMEM((length, span), LOW),
            pltpu.VMEM((3, length, HD), LOW),
            pltpu.VMEM((length, HD), LOW),
            pltpu.VMEM((length, HD), F32),
            pltpu.VMEM((length, HD), F32),
            pltpu.VMEM((4,) + g_up.shape[1:], LOW),
            pltpu.VMEM((8, 128), F32),
        ]
        + scatter_ranks_scratch(rows, width)
        + GATHER_RANKS_SEMS
        + scatter_items_scratch([g_up, g_down]),
        "backward_attention",
    )


def backward_last(g_io, news, second, modulation, cond_cut, time_slope):
    rows, width = second.shape
    span = g_io.shape[2] // 4

    def kernel(*refs):
        groups = takes(refs, 6, 6, 5, 12, 1, *[14] * 2)
        args, outs, scratch, sems, (io_all,) = groups[:5]
        greet(True, True)
        run_all(
            [condition_backward(*args[1:], outs[2:], scratch, sems)] + scatter_items(args[:1], (io_all,), groups[5:])
        )

        def assemble(at):
            for part in range(4):
                for block in range(3):
                    to = (block * 4 + part) * span
                    outs[0][at, to : to + span] = io_all[part, at, block * span : (block + 1) * span]
                outs[1][at, part * span : (part + 1) * span] = io_all[part, at, 3 * span :]

        by_rows(rows, assemble)

    return call(
        kernel,
        8,
        (g_io, news, second, modulation, cond_cut, time_slope),
        [HBM] + [VMEM] * 5,
        [
            shape((rows, 12 * span), LOW),
            shape((rows, 4 * span), LOW),
            shape(news.shape, F32),
            shape((8, width), F32),
            shape((8, 8, rows), F32),
            shape((8, 1, modulation.shape[1]), F32),
        ],
        [VMEM] * 6,
        [
            pltpu.VMEM((4,) + news.shape, F32),
            pltpu.VMEM(news.shape, F32),
            pltpu.VMEM((8, 8, rows), F32),
            pltpu.VMEM((8, 8, rows), F32),
            pltpu.VMEM((8, 8, rows), F32),
            DMA((3,)),
            DMA((4,)),
        ]
        + SWAP_SEMS * 5
        + [pltpu.VMEM((4,) + g_io.shape[1:], LOW)]
        + scatter_items_scratch([g_io]),
        "backward_last",
    )


def pick_weights(attend_in, attend_out, expand, rank, span, units):
    rows = attend_in.shape[0]
    owners = expand.shape[1] // (4 * units)
    if not fast():
        w_in = pick(attend_in.reshape(rows, 3, 4, span), rank, 2).astype(LOW).reshape(rows, 3 * span)
        w_up = pick(expand.reshape(rows, owners, 4, units), rank, 2).astype(LOW).reshape(rows, owners * units)
        return jnp.concatenate([w_in, mine(attend_out, 1, 4, rank).astype(LOW)], axis=1), w_up

    def kernel(in_ref, out_ref, up_ref, io, up):
        here = lax.axis_index("seq")
        for part in range(4):

            @pl.when(here == part)
            def _(part=part):
                def one(at):
                    for block in range(3):
                        start = (block * 4 + part) * span
                        io[at, block * span : (block + 1) * span] = in_ref[at, start : start + span].astype(LOW)
                    io[at, 3 * span :] = out_ref[at, part * span : (part + 1) * span].astype(LOW)
                    for owner in range(owners):
                        start = (owner * 4 + part) * units
                        up[at, owner * units : (owner + 1) * units] = up_ref[at, start : start + units].astype(LOW)

                by_rows(rows, one)

    return pl.pallas_call(
        kernel,
        out_shape=[shape((rows, 4 * span), LOW), shape((rows, owners * units), LOW)],
        in_specs=[VMEM] * 3,
        out_specs=[VMEM] * 2,
        compiler_params=pltpu.CompilerParams(vmem_limit_bytes=32 * 1024 * 1024),
        name="pick_weights",
    )(attend_in, attend_out, expand)


def sum_owners(number, value, name):
    if not fast():
        return lax.psum(value, "fsdp")

    def kernel(src, out, boxes, *sems):
        owner = lax.axis_index("fsdp")
        greet(True, False)
        sends = Sends()
        boxes[owner] = src[...]
        swap_start(sends, lambda to: src, boxes, *sems)
        swap_wait(boxes, sems[1])
        total = boxes[0]
        for of in range(1, 8):
            total = total + boxes[of]
        out[...] = total
        sends.finish()

    block = jnp.full((8, 128), value, F32)
    total = call(
        kernel, number, (block,), [VMEM], shape((8, 128), F32), VMEM, [pltpu.VMEM((8, 8, 128), F32)] + SWAP_SEMS, name
    )
    return total[0, 0]


def attend(query, keys, values):
    score_scale = 1.0 / math.sqrt(keys.shape[-1])
    scores = mixed_dot("qhd,khd->hqk", query, keys) * score_scale
    top = jnp.max(scores, axis=-1, keepdims=True)
    expo = jnp.exp(scores - top)
    total = jnp.sum(expo, axis=-1, keepdims=True)
    probs = (expo / total).astype(LOW)
    mixed = mixed_dot("hqk,khd->qhd", probs, values)
    return mixed.astype(LOW), (top + jnp.log(total))[..., 0]


def attend_back(query, keys, values, d_mixed, log_total):
    length, heads_here, head_dim = query.shape
    block = min(512, length)
    count = length // block
    score_scale = 1.0 / math.sqrt(head_dim)

    def back_block(carry, pieces):
        d_keys, d_values = carry
        query_block, d_block, log_block = pieces
        scores = mixed_dot("qhd,khd->hqk", query_block, keys) * score_scale
        probs = jnp.exp(scores - log_block[..., None])
        d_probs = mixed_dot("qhd,khd->hqk", d_block, values)
        delta = jnp.sum(probs * d_probs, axis=-1, keepdims=True)
        d_scores = (probs * (d_probs - delta)).astype(LOW)
        d_query = mixed_dot("hqk,khd->qhd", d_scores, keys) * score_scale
        d_keys = d_keys + mixed_dot("hqk,qhd->khd", d_scores, query_block) * score_scale
        d_values = d_values + mixed_dot("hqk,qhd->khd", probs.astype(LOW), d_block)
        return ((d_keys, d_values), d_query)

    empty = jnp.zeros((length, heads_here, head_dim), jnp.float32)
    blocked = (count, block, heads_here, head_dim)
    logs = log_total.reshape(heads_here, count, block).transpose(1, 0, 2)
    (d_keys, d_values), d_query = lax.scan(
        back_block, (empty, empty), (query.reshape(blocked), d_mixed.reshape(blocked), logs)
    )
    flat = (length, heads_here * head_dim)
    return jnp.concatenate(
        [d_query.reshape(flat), d_keys.reshape(flat), d_values.reshape(flat)], axis=1
    ).astype(LOW)


def adam_step(weight, moment, square, gradient, factor):
    clipped = gradient * factor
    moment_next = beta_one * moment + (1.0 - beta_one) * clipped
    square_next = beta_two * square + (1.0 - beta_two) * clipped * clipped
    moment_hat = moment_next / (1.0 - beta_one**STEP)
    square_hat = square_next / (1.0 - beta_two**STEP)
    master = weight - learn_rate * (
        moment_hat / (jnp.sqrt(square_hat) + adam_eps) + weight_decay * weight
    )
    return (master, moment_next, square_next)


def condition_start(latent_tokens, w_io, biases, timesteps, labels, time_first, time_second, class_table, modulation):
    owners, owner = lax.axis_size("fsdp"), lax.axis_index("fsdp")
    share = biases.shape[0]
    width = time_first.shape[1]
    first, second = time_first.astype(LOW), time_second.astype(LOW)
    table, modulation_low = class_table.astype(LOW), modulation.astype(LOW)
    units = first.shape[0]
    bias_low = biases.astype(LOW).astype(F32)
    features = time_features(timesteps).astype(LOW)
    if fast():
        note = jnp.concatenate(
            [
                jnp.broadcast_to(bias_low, (owners, share)),
                features.astype(F32).reshape(owners, units),
                jnp.broadcast_to(labels.astype(F32), (owners, 1)),
                jnp.zeros((owners, 127 - units), F32),
            ],
            axis=1,
        )[:, None]
        w_io_all, tokens, notes, act, slope, cond_cut, cond, mod = forward_first(
            w_io, latent_tokens, note, first, second, table, modulation_low
        )
        notes = notes[:, 0]
        all_bias = notes[:, :share].reshape(owners * share)
        my_features = notes[:, share : share + units]
        all_labels = notes[:, share + units]
        mod_values = mod.reshape(owners * mod.shape[2])
        state = (first, second, modulation_low, my_features, all_labels, act, slope, cond_cut, cond)
        return w_io_all, tokens, all_bias, mod_values, state
    w_io_all = lax.all_gather(w_io, "fsdp", axis=0)
    tokens = lax.all_gather(latent_tokens, "seq", axis=0)
    note = jnp.concatenate([bias_low, features[0].astype(F32), labels.astype(F32)])
    notes = lax.all_gather(note, "fsdp", axis=0)
    all_bias = notes[:, :share].reshape(owners * share)
    my_features = mine(notes[:, share:-1], 1, owners, owner)
    all_labels = notes[:, -1]
    hidden_time = lax.psum(mixed_dot("bf,fd->bd", my_features.astype(LOW), first), "fsdp") + all_bias[:width]
    act, slope = silu_parts(mine(hidden_time, 1, owners, owner))
    act = act.astype(LOW)
    onehot = (all_labels[:, None] == jnp.arange(NCLS, dtype=F32)[None, :]).astype(LOW)
    cond_part = mixed_dot("bd,de->be", act, second)
    class_part = mixed_dot("bc,cd->bd", onehot, table)
    class_wide = lax.dynamic_update_slice(jnp.zeros_like(cond_part), class_part, (0, owner * class_part.shape[1]))
    cond = lax.psum(cond_part + class_wide, "fsdp") + all_bias[width : 2 * width]
    mod_part = mixed_dot("bd,de->be", silu_parts(cond)[0].astype(LOW), modulation_low)
    mod_values = pick(lax.all_gather(mod_part, "fsdp", axis=0), owner, 1).reshape(owners * mod_part.shape[1])
    state = (first, second, modulation_low, my_features, all_labels, act.astype(F32), slope, None, cond)
    return w_io_all, tokens, all_bias, mod_values, state


def owner_sums(blocks):
    summed = [lax.psum_scatter(block.astype(F32), "fsdp", scatter_dimension=0, tiled=False) for block in blocks]
    return [lax.all_gather(block.astype(LOW), "seq", axis=0) for block in summed]


def condition_end(state, g_io, my_d_mod, tail, share):
    first, second, modulation_low, my_features, all_labels, act, slope, cond_cut, cond = state
    owners, owner, rank = lax.axis_size("fsdp"), lax.axis_index("fsdp"), lax.axis_index("seq")
    wide, width = modulation_low.shape[1], cond.shape[1]
    if fast():
        pad = -wide % 128
        tails = jnp.concatenate([jnp.zeros((owners * share - tail.shape[0],), F32), tail]).reshape(owners, share)
        news = jnp.concatenate(
            [my_d_mod.reshape(owners, wide), jnp.zeros((owners, pad), F32), tails], axis=1
        )[:, None]
        grad_in, grad_out, by_latent, d_cond, d_hid, sums = backward_last(g_io, news, second, modulation_low, cond_cut, slope)
        d_mod = by_latent[:, 0, :wide]
        my_tail = jnp.sum(by_latent[:, 0, wide + pad :], axis=0)
        d_hidden = d_hid.transpose(1, 0, 2).reshape(owners, width)
        front = jnp.concatenate([jnp.sum(d_hidden, axis=0), jnp.sum(d_cond, axis=0), sums.reshape(owners * wide)])
        count = front.shape[0] // share
        grad_bias = jnp.where(
            owner < count, pick(front.reshape(count, share), jnp.minimum(owner, count - 1)), my_tail
        )
    else:
        (grad_io,) = owner_sums([g_io])
        rows, span = grad_io.shape[1], grad_io.shape[2] // 4
        grad_in = grad_io[:, :, : 3 * span].reshape(4, rows, 3, span).transpose(1, 2, 0, 3).reshape(rows, 12 * span)
        grad_out = grad_io[:, :, 3 * span :].transpose(1, 0, 2).reshape(rows, 4 * span)
        all_d_mod = lax.all_gather(lax.psum(my_d_mod, "seq"), "fsdp", axis=0)
        d_mod = mine(all_d_mod, 1, owners, owner)
        part = high_dot(d_mod, modulation_low.astype(F32).T)
        d_cond = lax.psum(part, "fsdp") * silu_parts(cond)[1]
        d_time = high_dot(d_cond, second.astype(F32).T) * slope
        d_hidden = lax.all_gather(d_time, "fsdp", axis=0).transpose(1, 0, 2).reshape(owners, width)
        tail = lax.psum(tail, ("seq", "fsdp"))
        all_bias = jnp.concatenate(
            [jnp.sum(d_hidden, axis=0), jnp.sum(d_cond, axis=0), jnp.sum(all_d_mod, axis=0), tail]
        )
        grad_bias = mine(all_bias, 0, owners, owner)
    onehot = (all_labels[:, None] == jnp.arange(NCLS, dtype=F32)[None, :]).astype(F32)
    cond_act = silu_parts(cond)[0].astype(LOW).astype(F32)
    grad_mod = high_dot(cond_act.T, d_mod)
    grad_class = high_dot(onehot.T, mine(d_cond, 1, owners, owner))
    grad_second = high_dot(act.T, d_cond)
    grad_first = high_dot(my_features.T, d_hidden)
    condition_gradient = lax.dynamic_slice_in_dim(d_cond, owner, 1, 0)
    return grad_in, grad_out, (grad_first, grad_second, grad_class, grad_mod), grad_bias, condition_gradient


def per_device(latents, timesteps, labels, upstream, *state):
    params, moments, squares = state[:9], state[9:18], state[18:]
    time_first, time_second, class_table, modulation, attend_in, attend_out, expand, contract, biases = params
    lat_dev, tok_rows, width = latents.shape
    assert lat_dev == 1
    hidden = expand.shape[1]
    ranks = lax.axis_size("seq")
    owners = lax.axis_size("fsdp")
    rank = lax.axis_index("seq")
    heads_here = H // ranks
    span = heads_here * HD
    length = ranks * tok_rows
    rows = width // owners
    unit = hidden // (owners * ranks)
    hid_here = owners * unit

    my_io, my_up = pick_weights(attend_in, attend_out, expand, rank, span, unit)
    my_down = mine(contract, 0, ranks, rank).astype(LOW)
    w_io, tokens, all_bias, mod_values, kept = condition_start(
        latents[0], my_io, biases, timesteps, labels, time_first, time_second, class_table, modulation
    )
    w_io = w_io.reshape(width, 4 * span)
    w_in = w_io[:, : 3 * span]
    inputs_low = tokens.reshape(length, width)

    b_t1, b_t2, b_mod, b_q, b_v, b_out, b_up, b_down = split_biases(all_bias, width, hidden)
    mod_values = (mod_values + b_mod).reshape(6, 1, width)
    shift1, scale1, gate1, shift2, scale2, gate2 = [mod_values[index] for index in range(6)]

    inputs = inputs_low.astype(F32)
    norm_one, _ = layer_norm(inputs)
    h_attn = (norm_one * (1.0 + scale1) + shift1).astype(LOW)
    my_b_q, my_b_v = mine(b_q, 0, ranks, rank), mine(b_v, 0, ranks, rank)
    qkv_bias = jnp.concatenate([my_b_q, jnp.zeros_like(my_b_q), my_b_v])
    qkv = (mixed_dot("td,de->te", h_attn, w_in) + qkv_bias).astype(LOW)
    head_shape = (length, heads_here, HD)
    if fast():
        w_up, w_down, d_out_low, w_out, mixed, logs = forward_attention(
            qkv, my_up, my_down, upstream[0], w_io[:, 3 * span :]
        )
    else:
        query, keys, values = [qkv[:, part * span : (part + 1) * span].reshape(head_shape) for part in range(3)]
        mixed_heads, logs = attend(query, keys, values)
        w_up, w_down, d_out_low, w_out, mixed = gathers(
            2, [my_up, my_down], [upstream[0], w_io[:, 3 * span :], mixed_heads.reshape(length, span)], "gathers"
        )
    w_up, w_down = w_up.reshape(width, hid_here), w_down.reshape(hid_here, width)
    d_out_low = d_out_low.reshape(length, width)
    w_out = w_out.transpose(1, 0, 2).reshape(width, width)
    mixed = mixed.transpose(1, 0, 2).reshape(length, width)
    attn_out = mixed_dot("td,de->te", mixed, w_out) + b_out
    middle = inputs + gate1 * attn_out
    norm_two, inverse_two = layer_norm(middle)
    h_mlp = (norm_two * (1.0 + scale2) + shift2).astype(LOW)

    my_b_up = pick(b_up.reshape(owners, ranks, unit), rank, 1).reshape(hid_here)
    pre_act = mixed_dot("td,df->tf", h_mlp, w_up) + my_b_up
    act_f, gelu_pull = jax.vjp(partial(jax.nn.gelu, approximate=True), pre_act)
    act = act_f.astype(LOW)
    by_rank = (ranks, tok_rows, width)
    by_owner = lambda block: block.astype(LOW).reshape((owners, -1) + block.shape[1:])
    mlp_part = mixed_dot("tf,fd->td", act, w_down).astype(LOW).reshape(by_rank)
    d_out = d_out_low.astype(F32)
    d_mlp = (d_out * gate2).astype(LOW)
    d_act = mixed_dot("td,fd->tf", d_mlp, w_down)
    d_pre = gelu_pull(d_act)[0].astype(LOW)
    d_hmlp_part = mixed_dot("tf,df->td", d_pre, w_up).astype(LOW).reshape(by_rank)
    (d_hmlp,) = rank_sums(4, [d_hmlp_part], "sum_feed")
    g_down = by_owner(mixed_dot("tf,td->fd", act, d_mlp))
    g_up = by_owner(mixed_dot("td,tf->df", h_mlp, d_pre))
    gb_up = jnp.sum(d_pre.astype(F32), axis=0)
    gb_down = jnp.sum(d_mlp.astype(F32), axis=0)

    own = lambda array: mine(array, 0, ranks, rank)
    my_attn_out, my_middle, my_norm_two, my_inverse_two = own(attn_out), own(middle), own(norm_two), own(inverse_two)
    my_d_out = upstream[0].astype(F32)
    d_shift2 = jnp.sum(d_hmlp, axis=0)
    d_scale2 = jnp.sum(d_hmlp * my_norm_two, axis=0)
    d_middle = my_d_out + layer_norm_back(my_norm_two, my_inverse_two, d_hmlp * (1.0 + scale2))
    d_gate1 = jnp.sum(d_middle * my_attn_out, axis=0)
    my_d_attn = (d_middle * gate1).astype(LOW)
    my_w_out = mine(w_out, 0, ranks, rank)
    if fast():
        grad_up, grad_down, d_attn, mlp_sum, d_qkv = backward_attention(
            g_up, g_down, my_d_attn, mlp_part, qkv, my_w_out, logs, unit
        )
        d_attn = d_attn.reshape(length, width)
    else:
        (mlp_sum,) = rank_sums(5, [mlp_part], "sums")
        (d_attn,) = gathers(5, [], [my_d_attn], "gathers")
        d_attn = d_attn.reshape(length, width)
        d_mixed = mixed_dot("te,de->td", d_attn, my_w_out).astype(LOW)
        d_qkv = attend_back(query, keys, values, d_mixed.reshape(head_shape), logs)
        grad_up, grad_down = owner_sums([g_up, g_down])
        grad_up = grad_up.reshape(ranks, rows, owners, unit).transpose(1, 2, 0, 3).reshape(rows, hidden)
    mlp_out = mlp_sum + b_down
    output = (my_middle + gate2 * mlp_out).astype(LOW)
    d_gate2 = jnp.sum(my_d_out * mlp_out, axis=0)
    g_io = by_owner(
        jnp.concatenate(
            [
                mixed_dot("td,te->de", h_attn, d_qkv).astype(LOW),
                mixed_dot("td,te->de", mixed, mine(d_attn, 1, ranks, rank)).astype(LOW),
            ],
            axis=1,
        )
    )
    d_hattn_part = mixed_dot("te,de->td", d_qkv, w_in).astype(LOW).reshape(by_rank)
    (d_hattn,) = rank_sums(6, [d_hattn_part], "sum_attend")
    my_inputs = latents[0].astype(F32)
    my_norm_one, my_inverse_one = layer_norm(my_inputs)
    d_shift1 = jnp.sum(d_hattn, axis=0)
    d_scale1 = jnp.sum(d_hattn * my_norm_one, axis=0)
    input_gradient = d_middle + layer_norm_back(my_norm_one, my_inverse_one, d_hattn * (1.0 + scale1))

    my_d_mod = jnp.concatenate([d_shift1, d_scale1, d_gate1, d_shift2, d_scale2, d_gate2])
    gb_qv = jnp.sum(d_qkv.astype(F32), axis=0)
    wide = lambda part, size: lax.dynamic_update_slice(jnp.zeros((size,), F32), part, (rank * part.shape[0],))
    gb_up_wide = lax.dynamic_update_slice(
        jnp.zeros((owners, ranks, unit), F32), gb_up.reshape(owners, 1, unit), (0, rank, 0)
    ).reshape(hidden)
    gb_tail = jnp.concatenate(
        [
            wide(gb_qv[:span], width),
            wide(gb_qv[2 * span :], width),
            jnp.sum(my_d_attn.astype(F32), axis=0),
            gb_up_wide,
            jnp.where(rank == 0, gb_down, 0.0),
        ]
    )
    grad_in, grad_out, small_grads, grad_bias, condition_gradient = condition_end(
        kept, g_io, my_d_mod, gb_tail, biases.shape[0]
    )
    grad_in, grad_out, grad_up, grad_down = [grad.astype(F32) for grad in (grad_in, grad_out, grad_up, grad_down)]
    grad_down = grad_down.reshape(contract.shape)
    gradients = small_grads + (grad_in, grad_out, grad_up, grad_down, grad_bias)
    local_sum = sum(jnp.sum(gradient * gradient) for gradient in gradients)
    norm_before = jnp.sqrt(sum_owners(7, local_sum, "sum_squares"))
    factor = clip_limit / jnp.maximum(norm_before, clip_limit)
    results = [
        adam_step(params[index], moments[index], squares[index], gradients[index], factor)
        for index in range(9)
    ]
    return (
        (output[None], input_gradient[None], condition_gradient, norm_before)
        + gradients
        + tuple(result[0] for result in results)
        + tuple(result[1] for result in results)
        + tuple(result[2] for result in results)
    )


def solution(mesh):
    tokens = P("fsdp", "seq", None)
    rows, columns = P("fsdp", None), P(None, "fsdp")
    weights = (rows, rows, columns, columns, rows, rows, rows, rows, P("fsdp"))
    return jax.shard_map(
        per_device,
        mesh=mesh,
        in_specs=(tokens, P("fsdp"), P("fsdp"), tokens) + weights * 3,
        out_specs=(tokens, tokens, rows, P()) + weights * 4,
        check_vma=False,
    )
```

```python
from functools import partial
import math

import jax
import jax.numpy as jnp
from jax import lax
from jax.experimental import pallas as pl
from jax.experimental.pallas import tpu as pltpu
from jax.sharding import PartitionSpec as P

H = 16
HD = 72
FREQ = 256
NCLS = 1000
STEP = 10


HIGH = lax.Precision.HIGHEST
LOW = jnp.bfloat16
norm_eps = 1e-06
beta_one = 0.9
beta_two = 0.999
learn_rate = 0.04
weight_decay = 0.01
adam_eps = 1e-08
clip_limit = 1.0


def layer_norm(value):
    centre = value - jnp.mean(value, axis=-1, keepdims=True)
    spread = jnp.mean(centre * centre, axis=-1, keepdims=True)
    inverse = lax.rsqrt(spread + norm_eps)
    return centre * inverse, inverse


def layer_norm_back(norm, inverse, grad):
    first = jnp.mean(grad, axis=-1, keepdims=True)
    second = jnp.mean(grad * norm, axis=-1, keepdims=True)
    return inverse * (grad - first - norm * second)


def silu_parts(value):
    gate = jax.nn.sigmoid(value)
    return value * gate, gate * (1.0 + value * (1.0 - gate))


def time_features(timesteps):
    half = FREQ // 2
    freqs = jnp.exp(-math.log(10000.0) * jnp.arange(half, dtype=jnp.float32) / half)
    angles = timesteps.astype(jnp.float32)[:, None] * freqs[None, :]
    return jnp.concatenate([jnp.cos(angles), jnp.sin(angles)], axis=-1)


def split_biases(biases, width, hidden):
    widths = [width, width, 6 * width, width, width, width, hidden, width]
    pieces = []
    start = 0
    for length in widths:
        pieces.append(biases[start : start + length])
        start = start + length
    return pieces


def high_dot(left, right):
    return jnp.dot(left, right, precision=HIGH, preferred_element_type=jnp.float32)


def mixed_dot(form, left, right):
    return jnp.einsum(form, left, right, preferred_element_type=jnp.float32)


def pick(array, index, axis=0):
    return lax.dynamic_index_in_dim(array, index, axis, keepdims=False)


def mine(array, axis, parts, index):
    size = array.shape[axis] // parts
    return lax.dynamic_slice_in_dim(array, index * size, size, axis)


HBM = pl.BlockSpec(memory_space=pl.ANY)
VMEM = pl.BlockSpec(memory_space=pltpu.VMEM)
DMA = pltpu.SemaphoreType.DMA
F32 = jnp.float32


def fast():
    return lax.axis_size("fsdp") == 8 and lax.axis_size("seq") == 4


def places():
    owner, rank = lax.axis_index("fsdp"), lax.axis_index("seq")
    return owner, rank, lax.div(owner, 2), lax.rem(owner, 2), lax.div(rank, 2), lax.rem(rank, 2)


def remote(src, dst, sent, landed, **where):
    return pltpu.make_async_remote_copy(
        src_ref=src, dst_ref=dst, send_sem=sent, recv_sem=landed, device_id=where, device_id_type=pl.DeviceIdType.MESH
    )


def arrived(dst, landed, **where):
    remote(dst, dst, landed, landed, **where).wait_recv()


def greet(over_owners, over_ranks):
    owner, rank, *_ = places()
    barrier = pltpu.get_barrier_semaphore()
    count = 0
    if over_owners:
        for step in range(1, 8):
            pl.semaphore_signal(
                barrier, inc=1, device_id={"fsdp": lax.rem(owner + step, 8)}, device_id_type=pl.DeviceIdType.MESH
            )
        count += 7
    if over_ranks:
        for step in range(1, 4):
            pl.semaphore_signal(
                barrier, inc=1, device_id={"seq": lax.rem(rank + step, 4)}, device_id_type=pl.DeviceIdType.MESH
            )
        count += 3
    pl.semaphore_wait(barrier, count)


def run_all(parts):
    parts = list(parts)
    while parts:
        for part in list(parts):
            try:
                next(part)
            except StopIteration:
                parts.remove(part)


class Sends:
    def __init__(self):
        self.live = []

    def start(self, copy, when=None):
        self.live.append((copy, when))
        if when is None:
            copy.start()
        else:
            pl.when(when)(copy.start)

    def finish(self):
        for copy, when in self.live:
            wait = copy.wait_send if hasattr(copy, "wait_send") else copy.wait
            if when is None:
                wait()
            else:
                pl.when(when)(wait)


def gather_owners(src, out, sems):
    own_sem, sent, landed = sems
    owner, rank, z, y, x, core = places()
    mate = owner + 1 - 2 * y
    sends = Sends()
    local = pltpu.make_async_copy(src, out.at[owner], own_sem)
    local.start()
    sends.start(remote(src, out.at[owner], sent.at[0, 0], landed.at[owner], fsdp=owner + 2), z < 3)
    sends.start(remote(src, out.at[owner], sent.at[0, 1], landed.at[owner], fsdp=owner - 2), z > 0)
    sends.start(remote(src, out.at[owner], sent.at[0, 2], landed.at[owner], fsdp=mate))
    yield
    for far in (1, 2, 3):
        for sign in (-1, 1):
            block = owner + sign * 2 * far
            here = (z >= far) if sign < 0 else (z + far <= 3)
            on = (z < 3) if sign < 0 else (z > 0)
            at = far if sign < 0 else 3 + far
            pl.when(here)(lambda: arrived(out.at[block], landed.at[block], fsdp=mate))
            sends.start(
                remote(out.at[block], out.at[block], sent.at[at, 0], landed.at[block], fsdp=owner - sign * 2), here & on
            )
            sends.start(remote(out.at[block], out.at[block], sent.at[at, 2], landed.at[block], fsdp=mate), here)
        yield
    for step in range(4):
        block = step * 2 + 1 - y
        arrived(out.at[block], landed.at[block], fsdp=mate)
    local.wait()
    sends.finish()


GATHER_OWNERS_SEMS = [DMA(()), DMA((7, 3)), DMA((8,))]


def gather_ranks(src, out, sems, local_copy=True):
    own_sem, sent, landed = sems
    owner, rank, z, y, x, core = places()
    mate, across, last = x * 2 + 1 - core, (1 - x) * 2 + core, (1 - x) * 2 + 1 - core
    sends = Sends()
    local = None
    if local_copy:
        local = pltpu.make_async_copy(src, out.at[rank], own_sem)
        local.start()
    sends.start(remote(src, out.at[rank], sent.at[0], landed.at[rank], seq=across))
    sends.start(remote(src, out.at[rank], sent.at[1], landed.at[rank], seq=mate))
    yield
    yield
    arrived(out.at[across], landed.at[across], seq=across)
    sends.start(remote(out.at[across], out.at[across], sent.at[2], landed.at[across], seq=mate))
    yield
    arrived(out.at[mate], landed.at[mate], seq=mate)
    arrived(out.at[last], landed.at[last], seq=mate)
    if local is not None:
        local.wait()
    sends.finish()


GATHER_RANKS_SEMS = [DMA(()), DMA((3,)), DMA((4,))]


def by_rows(count, body, step=16):
    def one(index, carry):
        body(pl.ds(pl.multiple_of(index * step, step), step))
        return carry

    lax.fori_loop(0, count // step, one, 0)


def scatter_ranks(parts, out, own, mail, leave, enter, sems):
    own_sem, sent, landed = sems
    owner, rank, z, y, x, core = places()
    mate, across = x * 2 + 1 - core, (1 - x) * 2 + core
    sends = Sends()
    loads = []
    for step in (1, 0):
        to = lax.rem(x + step, 2)
        loads.append(pltpu.make_async_copy(parts.at[to * 2 + core], own.at[step], own_sem.at[step]))
        loads[-1].start()
        sends.start(remote(parts.at[to * 2 + 1 - core], mail.at[step], sent.at[step], landed.at[step], seq=mate))
    yield
    loads[0].wait()
    arrived(mail.at[1], landed.at[1], seq=mate)

    def first(rows):
        leave[rows] = (own[1, rows].astype(F32) + mail[1, rows].astype(F32)).astype(LOW)

    by_rows(out.shape[0], first)
    sends.start(remote(leave, enter, sent.at[2], landed.at[2], seq=across))
    yield
    loads[1].wait()
    arrived(mail.at[0], landed.at[0], seq=mate)
    yield
    arrived(enter, landed.at[2], seq=across)

    def last(rows):
        out[rows] = own[0, rows].astype(F32) + mail[0, rows].astype(F32) + enter[rows].astype(F32)

    by_rows(out.shape[0], last)
    sends.finish()


def scatter_ranks_scratch(rows, columns):
    return [
        pltpu.VMEM((2, rows, columns), LOW),
        pltpu.VMEM((2, rows, columns), LOW),
        pltpu.VMEM((rows, columns), LOW),
        pltpu.VMEM((rows, columns), LOW),
        DMA((2,)),
        DMA((3,)),
        DMA((3,)),
    ]


def scatter_owners(parts, out, own, mail, rise, fall, leave, sems):
    own_sem, y_sent, y_landed, z_sent, up_landed, down_landed = sems[:6]
    owner, rank, z, y, x, core = places()
    mate = owner + 1 - 2 * y
    rows_here = own.shape[1]
    sends = Sends()
    loads = {}
    for to in (3, 0, 2, 1):
        sends.start(remote(parts.at[to * 2 + 1 - y], mail.at[to], y_sent.at[to], y_landed.at[to], fsdp=mate))
        loads[to] = pltpu.make_async_copy(parts.at[to * 2 + y], own.at[to], own_sem.at[to])
        loads[to].start()
        yield
    for to, up in ((3, True), (0, False), (2, True), (1, False), (1, True), (2, False)):
        here = (z < to) if up else (z > to)
        more = (z > 0) if up else (z < 3)
        box, box_landed = (rise, up_landed) if up else (fall, down_landed)

        def total(to=to, more=more, box=box, box_landed=box_landed):
            loads[to].wait()
            arrived(mail.at[to], y_landed.at[to], fsdp=mate)

            def start(rows):
                leave[to, rows] = (own[to, rows].astype(F32) + mail[to, rows].astype(F32)).astype(LOW)

            def add(rows):
                leave[to, rows] = (
                    own[to, rows].astype(F32) + mail[to, rows].astype(F32) + box[to, rows].astype(F32)
                ).astype(LOW)

            @pl.when(more)
            def _():
                arrived(box.at[to], box_landed.at[to], fsdp=mate)
                by_rows(rows_here, add)

            @pl.when(jnp.logical_not(more))
            def _():
                by_rows(rows_here, start)

        pl.when(here)(total)
        sends.start(
            remote(
                leave.at[to], box.at[to], z_sent.at[to], box_landed.at[to], fsdp=owner + 2 if up else owner - 2
            ),
            here,
        )
        yield
    for to in range(4):
        at_home = z == to

        @pl.when(at_home)
        def _(to=to):
            loads[to].wait()
            arrived(mail.at[to], y_landed.at[to], fsdp=mate)
            if to > 0:
                arrived(rise.at[to], up_landed.at[to], fsdp=mate)
            if to < 3:
                arrived(fall.at[to], down_landed.at[to], fsdp=mate)

            def end(rows):
                value = own[to, rows].astype(F32) + mail[to, rows].astype(F32)
                if to > 0:
                    value = value + rise[to, rows].astype(F32)
                if to < 3:
                    value = value + fall[to, rows].astype(F32)
                leave[to, rows] = value.astype(LOW)

            by_rows(rows_here, end)

    yield from gather_ranks(leave.at[z], out, sems[6:])
    sends.finish()


def scatter_owners_scratch(rows, columns):
    return [pltpu.VMEM((4, rows, columns), LOW)] * 5 + [DMA((4,))] * 6 + GATHER_RANKS_SEMS


def swap_start(sends, src_of, dst, sent, landed):
    owner = lax.axis_index("fsdp")
    for step in range(1, 8):
        to = lax.rem(owner + step, 8)
        sends.start(remote(src_of(to), dst.at[owner], sent.at[step - 1], landed.at[owner], fsdp=to))


def swap_wait(dst, landed):
    owner = lax.axis_index("fsdp")
    for step in range(1, 8):
        of = lax.rem(owner + step, 8)
        arrived(dst.at[of], landed.at[of], fsdp=of)


SWAP_SEMS = [DMA((7,)), DMA((8,))]


def low_dot(left, right, contract):
    return lax.dot_general(left, right, ((contract[:1], contract[1:]), ((), ())), preferred_element_type=F32)


def fine_dot(left, right, contract):
    high = left.astype(LOW)
    rest = left - high.astype(F32)
    return low_dot(high, right, contract) + low_dot(rest.astype(LOW), right, contract)


def stack_rows(ref):
    return jnp.concatenate([ref[index] for index in range(8)], axis=0)


def condition_forward(note, first, second, table, modulation, outs, scratch, sems):
    notes, act_out, slope_out, cond_cut, cond_out, mod = outs
    send_cut, hid_in, cond_in, bias_cut, mod_cut = scratch
    owner = lax.axis_index("fsdp")
    cut = second.shape[0]
    share = note.shape[2] - 128
    sends = Sends()
    notes[owner] = note[owner]
    swap_start(sends, lambda to: note.at[to], notes, *sems[0:2])
    yield
    swap_wait(notes, sems[1])
    rows = stack_rows(notes)
    feats = rows[:, share : share + first.shape[0]].astype(LOW)
    label = rows[:, share + first.shape[0] : share + first.shape[0] + 1]
    hidden = low_dot(feats, first[...], (1, 0))
    for to in range(8):
        send_cut[0, to] = hidden[:, to * cut : (to + 1) * cut]
        bias_cut[0, to] = rows[0:1, to * cut : (to + 1) * cut]
        bias_cut[1, to] = rows[0:1, (8 + to) * cut : (9 + to) * cut]
    hid_in[owner] = send_cut[0, owner]
    swap_start(sends, lambda to: send_cut.at[0, to], hid_in, *sems[2:4])
    yield
    classes = lax.broadcasted_iota(jnp.int32, (8, table.shape[0]), 1).astype(F32)
    onehot = (label == classes).astype(F32).astype(LOW)
    from_class = low_dot(onehot, table[...], (1, 0))
    swap_wait(hid_in, sems[3])
    hidden_cut = bias_cut[0, owner] + jnp.zeros((8, cut), F32)
    for of in range(8):
        hidden_cut = hidden_cut + hid_in[of]
    act, slope = silu_parts(hidden_cut)
    act = act.astype(LOW)
    act_out[...] = act.astype(F32)
    slope_out[...] = slope
    part = low_dot(act, second[...], (1, 0))
    for to in range(8):
        send_cut[1, to] = part[:, to * cut : (to + 1) * cut]
    cond_in[owner] = send_cut[1, owner]
    swap_start(sends, lambda to: send_cut.at[1, to], cond_in, *sems[4:6])
    yield
    swap_wait(cond_in, sems[5])
    mine_cond = bias_cut[1, owner] + from_class
    for of in range(8):
        mine_cond = mine_cond + cond_in[of]
    cond_cut[owner] = mine_cond
    swap_start(sends, lambda to: cond_cut.at[owner], cond_cut, *sems[6:8])
    yield
    swap_wait(cond_cut, sems[7])
    for of in range(8):
        cond_out[:, of * cut : (of + 1) * cut] = cond_cut[of]
    cond_act = silu_parts(cond_out[...])[0].astype(LOW)
    values = low_dot(cond_act, modulation[...], (1, 0))
    for to in range(8):
        mod_cut[to] = values[to : to + 1]
    mod[owner] = mod_cut[owner]
    swap_start(sends, lambda to: mod_cut.at[to], mod, *sems[8:10])
    yield
    swap_wait(mod, sems[9])
    sends.finish()


def condition_backward(news, second, modulation, cond_cut, time_slope, outs, scratch, sems):
    by_latent, d_cond_out, d_hid_cut, sums = outs
    rank_news, owner_news, d_cut, d_in, d_cond_cut = scratch
    owner, rank, *_ = places()
    cut = second.shape[0]
    wide = modulation.shape[1]
    sends = Sends()
    for step in range(1, 4):
        to = lax.rem(rank + step, 4)
        sends.start(remote(news, rank_news.at[rank], sems[0].at[step - 1], sems[1].at[rank], seq=to))
    yield
    for step in range(1, 4):
        of = lax.rem(rank + step, 4)
        arrived(rank_news.at[of], sems[1].at[of], seq=of)
    rank_news[rank] = news[...]
    for to in range(8):
        owner_news[to] = rank_news[0, to] + rank_news[1, to] + rank_news[2, to] + rank_news[3, to]
    by_latent[owner] = owner_news[owner]
    swap_start(sends, lambda to: owner_news.at[to], by_latent, *sems[2:4])
    yield
    swap_wait(by_latent, sems[3])
    d_mod = stack_rows(by_latent)[:, :wide]
    part = fine_dot(d_mod, modulation[...], (1, 1))
    for to in range(8):
        d_cut[to] = part[:, to * cut : (to + 1) * cut]
    d_in[owner] = d_cut[owner]
    swap_start(sends, lambda to: d_cut.at[to], d_in, *sems[4:6])
    sums[owner] = jnp.sum(d_mod, axis=0, keepdims=True)
    swap_start(sends, lambda to: sums.at[owner], sums, *sems[6:8])
    yield
    swap_wait(d_in, sems[5])
    total = d_in[0]
    for of in range(1, 8):
        total = total + d_in[of]
    d_cond_cut[owner] = total * silu_parts(cond_cut[owner])[1]
    swap_start(sends, lambda to: d_cond_cut.at[owner], d_cond_cut, *sems[8:10])
    yield
    swap_wait(d_cond_cut, sems[9])
    for of in range(8):
        d_cond_out[:, of * cut : (of + 1) * cut] = d_cond_cut[of]
    d_hid_cut[owner] = fine_dot(d_cond_out[...], second[...], (1, 1)) * time_slope[...]
    swap_start(sends, lambda to: d_hid_cut.at[owner], d_hid_cut, *sems[10:12])
    yield
    swap_wait(d_hid_cut, sems[11])
    swap_wait(sums, sems[7])
    sends.finish()


def takes(refs, *counts):
    refs = list(refs)
    groups = []
    for count in counts:
        groups.append(refs[:count])
        refs = refs[count:]
    assert not refs
    return groups


def call(kernel, number, args, in_specs, outs, out_specs, scratch, name, room):
    return pl.pallas_call(
        kernel,
        out_shape=outs,
        in_specs=in_specs,
        out_specs=out_specs,
        scratch_shapes=scratch,
        compiler_params=pltpu.CompilerParams(
            collective_id=number, has_side_effects=True, vmem_limit_bytes=room * 1024 * 1024
        ),
        name=name,
    )(*args)


def shape(dims, kind):
    return jax.ShapeDtypeStruct(tuple(dims), kind)


def forward_first(w_io, tokens, note, first, second, table, modulation):
    rows, width = second.shape
    wide = modulation.shape[1]

    def kernel(*refs):
        args, outs, scratch, cond_sems, io_sems, token_sems = takes(refs, 7, 8, 5, 10, 3, 3)
        greet(True, True)
        run_all(
            [
                condition_forward(args[2], *args[3:7], outs[2:8], scratch, cond_sems),
                gather_ranks(args[1], outs[1], token_sems),
                gather_owners(args[0], outs[0], io_sems),
            ]
        )

    return call(
        kernel,
        1,
        (w_io, tokens, note, first, second, table, modulation),
        [VMEM] * 7,
        [
            shape((8,) + w_io.shape, LOW),
            shape((4,) + tokens.shape, LOW),
            shape(note.shape, F32),
            shape((8, rows), F32),
            shape((8, rows), F32),
            shape((8, 8, rows), F32),
            shape((8, width), F32),
            shape((8, 1, wide), F32),
        ],
        [HBM] * 2 + [VMEM] * 6,
        [
            pltpu.VMEM((2, 8, 8, rows), F32),
            pltpu.VMEM((8, 8, rows), F32),
            pltpu.VMEM((8, 8, rows), F32),
            pltpu.VMEM((2, 8, 1, rows), F32),
            pltpu.VMEM((8, 1, wide), F32),
        ]
        + SWAP_SEMS * 5
        + GATHER_OWNERS_SEMS
        + GATHER_RANKS_SEMS,
        "forward_first",
        20,
    )


QUERIES = 256


def block_of(index, size=QUERIES):
    return pl.ds(pl.multiple_of(index * size, size), size)


def attend_heads(qkv, mixed, logs, head_rows, heads):
    length = qkv.shape[0]
    span = heads * HD
    scale = 1.0 / math.sqrt(HD)
    for head in range(heads):
        for part in range(3):
            start = part * span + head * HD
            head_rows[part] = qkv[:, start : start + HD]

        def block(index, carry):
            query = head_rows[0, block_of(index)]
            scores = low_dot(head_rows[1], query, (1, 1)) * scale
            top = jnp.max(scores, axis=0, keepdims=True)
            expo = jnp.exp(scores - top)
            total = jnp.sum(expo, axis=0, keepdims=True)
            probs = (expo * (1.0 / total)).astype(LOW)
            mixed[block_of(index), head * HD : (head + 1) * HD] = low_dot(head_rows[2], probs, (0, 0)).T.astype(LOW)
            logs[head, index] = top + jnp.log(total)
            return carry

        lax.fori_loop(0, length // QUERIES, block, 0)
        yield


def attend_heads_back(qkv, logs, d_mixed, d_qkv, head_rows, d_head, d_keys, d_values, heads):
    length = qkv.shape[0]
    span = heads * HD
    scale = 1.0 / math.sqrt(HD)
    for head in range(heads):
        lanes = slice(head * HD, (head + 1) * HD)
        for part in range(3):
            start = part * span + head * HD
            head_rows[part] = qkv[:, start : start + HD]
        d_head[...] = d_mixed[:, lanes]
        d_keys[...] = jnp.zeros_like(d_keys)
        d_values[...] = jnp.zeros_like(d_values)

        def block(index, carry):
            query, d_block = head_rows[0, block_of(index)], d_head[block_of(index)]
            scores = low_dot(head_rows[1], query, (1, 1)) * scale
            probs = jnp.exp(scores - logs[head, index])
            d_probs = low_dot(head_rows[2], d_block, (1, 1))
            delta = jnp.sum(probs * d_probs, axis=0, keepdims=True)
            d_scores = (probs * (d_probs - delta)).astype(LOW)
            d_keys[...] += low_dot(d_scores, query, (1, 0))
            d_values[...] += low_dot(probs.astype(LOW), d_block, (1, 0))
            d_query = low_dot(head_rows[1], d_scores, (0, 0)).T * scale
            d_qkv[block_of(index), lanes] = d_query.astype(LOW)
            return carry

        lax.fori_loop(0, length // QUERIES, block, 0)
        d_qkv[:, span + head * HD : span + (head + 1) * HD] = (d_keys[...] * scale).astype(LOW)
        d_qkv[:, 2 * span + head * HD : 2 * span + (head + 1) * HD] = d_values[...].astype(LOW)
        yield


def beside(blocks, out):
    columns = blocks.shape[2]

    def one(at):
        for part in range(4):
            out[at, part * columns : (part + 1) * columns] = blocks[part, at]

    by_rows(out.shape[0], one)


def forward_attention(qkv, w_up, w_down, upstream, w_io):
    length = qkv.shape[0]
    heads = qkv.shape[1] // (3 * HD)
    span = heads * HD
    width = w_io.shape[0]

    def kernel(*refs):
        args, outs, scratch, up_sems, down_sems, token_sems, out_sems, mixed_sems = takes(refs, 5, 6, 5, 3, 3, 3, 3, 3)
        mixed_here, head_rows, mixed_all, out_here, out_all = scratch
        greet(True, True)

        def attention():
            steps = attend_heads(args[0], mixed_here, outs[5], head_rows, heads)
            for index, _ in enumerate(steps):
                if 0 < index < heads - 1:
                    yield
            yield from gather_ranks(mixed_here, mixed_all, mixed_sems)

        def out_weight():
            out_here[...] = args[4][:, 3 * span :]
            yield from gather_ranks(out_here, out_all, out_sems)
            beside(out_all, outs[3])

        run_all(
            [
                gather_owners(args[1], outs[0], up_sems),
                gather_owners(args[2], outs[1], down_sems),
                out_weight(),
                attention(),
                gather_ranks(args[3], outs[2], token_sems),
            ]
        )
        beside(mixed_all, outs[4])

    return call(
        kernel,
        2,
        (qkv, w_up, w_down, upstream, w_io),
        [VMEM] * 5,
        [
            shape((8,) + w_up.shape, LOW),
            shape((8,) + w_down.shape, LOW),
            shape((4,) + upstream.shape, LOW),
            shape((width, 4 * span), LOW),
            shape((length, 4 * span), LOW),
            shape((heads, length // QUERIES, 1, QUERIES), F32),
        ],
        [HBM] * 3 + [VMEM] * 3,
        [
            pltpu.VMEM((length, span), LOW),
            pltpu.VMEM((3, length, HD), LOW),
            pltpu.VMEM((4, length, span), LOW),
            pltpu.VMEM((width, span), LOW),
            pltpu.VMEM((4, width, span), LOW),
        ]
        + GATHER_OWNERS_SEMS * 2
        + GATHER_RANKS_SEMS * 3,
        "forward_attention",
        40,
    )


def gathers(number, by_owner, by_rank, name):
    if not fast():
        return [lax.all_gather(block, "fsdp", axis=0) for block in by_owner] + [
            lax.all_gather(block, "seq", axis=0) for block in by_rank
        ]
    many, few = len(by_owner), len(by_rank)

    def kernel(*refs):
        groups = takes(refs, many + few, many + few, *[3] * (many + few))
        args, outs, sems = groups[0], groups[1], groups[2:]
        greet(many > 0, few > 0)
        run_all(
            [gather_owners(args[at], outs[at], sems[at]) for at in range(many)]
            + [gather_ranks(args[at], outs[at], sems[at]) for at in range(many, many + few)]
        )

    blocks = list(by_owner) + list(by_rank)
    return call(
        kernel,
        number,
        blocks,
        [VMEM] * len(blocks),
        [shape((8 if at < many else 4,) + block.shape, block.dtype) for at, block in enumerate(blocks)],
        [HBM] * len(blocks),
        GATHER_OWNERS_SEMS * many + GATHER_RANKS_SEMS * few,
        name,
        16,
    )


def rank_sums(number, blocks, name):
    if not fast():
        return [lax.psum_scatter(block.astype(F32), "seq", scatter_dimension=0, tiled=False) for block in blocks]
    many = len(blocks)

    def kernel(*refs):
        groups = takes(refs, many, many, *[7] * many)
        greet(False, True)
        run_all(
            [
                scatter_ranks(groups[0][at], groups[1][at], *groups[2 + at][:4], groups[2 + at][4:])
                for at in range(many)
            ]
        )

    scratch = []
    for block in blocks:
        scratch += scatter_ranks_scratch(*block.shape[1:])
    return call(
        kernel,
        number,
        blocks,
        [HBM] * many,
        [shape(block.shape[1:], F32) for block in blocks],
        [VMEM] * many,
        scratch,
        name,
        16,
    )


def row_cuts(rows, cuts):
    step = (rows // cuts + 15) // 16 * 16
    return [(start, min(step, rows - start)) for start in range(0, rows, step)]


def together(parts, first):
    parts = list(parts)
    for _ in range(first):
        for part in parts:
            next(part)
    yield
    while parts:
        for part in list(parts):
            try:
                next(part)
            except StopIteration:
                parts.remove(part)
        yield


def scatter_items(parts, outs, scratch, cuts):
    items, at = [], 0
    for part, out in zip(parts, outs):
        for start, count in row_cuts(part.shape[1], cuts):
            rows = pl.ds(start, count)
            refs = scratch[at]
            items.append(scatter_owners(part.at[:, rows], out.at[:, rows], *refs[:5], refs[5:]))
            at += 1
    return [together(items, 4)]


def scatter_items_scratch(blocks, cuts):
    scratch = []
    for block in blocks:
        for _, count in row_cuts(block.shape[1], cuts):
            scratch += scatter_owners_scratch(count, block.shape[2])
    return scratch


def backward_attention(g_up, g_down, my_d_attn, mlp_part, qkv, w_out, logs, units):
    length = qkv.shape[0]
    heads = qkv.shape[1] // (3 * HD)
    span = heads * HD
    rows, width = my_d_attn.shape

    def kernel(*refs):
        groups = takes(refs, 7, 5, 6, 7, 3, *[14] * 6)
        args, outs, scratch, sum_scratch, token_sems = groups[:5]
        d_mixed, head_rows, d_head, d_keys, d_values, up_all = scratch
        greet(True, True)

        def attention():
            tokens = gather_ranks(args[2], outs[2], token_sems)
            next(tokens)
            yield
            for _ in tokens:
                pass
            w_rows = args[5][pl.ds(pl.multiple_of(lax.axis_index("seq") * span, 16), span)]
            for part in range(4):
                d_mixed[part * rows : (part + 1) * rows] = low_dot(outs[2][part], w_rows, (1, 1)).astype(LOW)
            yield from attend_heads_back(
                args[4], args[6], d_mixed, outs[4], head_rows, d_head, d_keys, d_values, heads
            )

        run_all(
            scatter_items(args[:2], (up_all, outs[1]), groups[5:], 3)
            + [attention(), scatter_ranks(args[3], outs[3], *sum_scratch[:4], sum_scratch[4:])]
        )
        owners = up_all.shape[2] // units

        def assemble(at):
            for part in range(4):
                for owner in range(owners):
                    to = (owner * 4 + part) * units
                    outs[0][at, to : to + units] = up_all[part, at, owner * units : (owner + 1) * units]

        by_rows(up_all.shape[1], assemble)

    return call(
        kernel,
        9,
        (g_up, g_down, my_d_attn, mlp_part, qkv, w_out, logs),
        [HBM, HBM, VMEM, HBM, VMEM, VMEM, VMEM],
        [
            shape((g_up.shape[1], 4 * g_up.shape[2]), LOW),
            shape((4,) + g_down.shape[1:], LOW),
            shape((4,) + my_d_attn.shape, LOW),
            shape(my_d_attn.shape, F32),
            shape(qkv.shape, LOW),
        ],
        [VMEM, HBM, VMEM, VMEM, VMEM],
        [
            pltpu.VMEM((length, span), LOW),
            pltpu.VMEM((3, length, HD), LOW),
            pltpu.VMEM((length, HD), LOW),
            pltpu.VMEM((length, HD), F32),
            pltpu.VMEM((length, HD), F32),
            pltpu.VMEM((4,) + g_up.shape[1:], LOW),
        ]
        + scatter_ranks_scratch(rows, width)
        + GATHER_RANKS_SEMS
        + scatter_items_scratch([g_up, g_down], 3),
        "backward_attention",
        50,
    )


def backward_last(g_in, g_out, d_tokens, tokens, scale, d_middle, news, second, modulation, cond_cut, time_slope):
    rows, width = second.shape
    span = g_out.shape[2]
    tok_rows = tokens.shape[0]
    wide = modulation.shape[1]

    def kernel(*refs):
        groups = takes(refs, 11, 7, 5, 12, 7, 5, *[14] * 4)
        args, outs, scratch, sems, sum_scratch, (in_all, out_all, d_sum, edge, news_here) = groups[:6]
        greet(True, True)

        def condition():
            yield from scatter_ranks(args[2], d_sum, *sum_scratch[:4], sum_scratch[4:])
            edge[...] = jnp.zeros_like(edge)

            def one(at):
                value = args[3][at].astype(F32)
                norm, inverse = layer_norm(value)
                grad = d_sum[at]
                edge[0] += jnp.sum(grad.reshape(2, 8, width), axis=0)
                edge[1] += jnp.sum((grad * norm).reshape(2, 8, width), axis=0)
                outs[2][at] = args[5][at] + layer_norm_back(norm, inverse, grad * (1.0 + args[4][...]))

            by_rows(tok_rows, one)
            news_here[...] = args[6][...]
            line = jnp.concatenate(
                [jnp.sum(edge[0], axis=0, keepdims=True), jnp.sum(edge[1], axis=0, keepdims=True)], axis=1
            )
            at = 0
            while at * wide < 2 * width:
                end = min((at + 1) * wide, 2 * width)
                news_here[at, :, : end - at * wide] = line[:, at * wide : end]
                at += 1
            yield from condition_backward(news_here, *args[7:], outs[3:], scratch, sems)

        run_all([condition()] + scatter_items(args[:2], (in_all, out_all), groups[6:], 2))

        def assemble(at):
            for part in range(4):
                for block in range(3):
                    to = (block * 4 + part) * span
                    outs[0][at, to : to + span] = in_all[part, at, block * span : (block + 1) * span]
                outs[1][at, part * span : (part + 1) * span] = out_all[part, at]

        by_rows(rows, assemble)

    return call(
        kernel,
        8,
        (g_in, g_out, d_tokens, tokens, scale, d_middle, news, second, modulation, cond_cut, time_slope),
        [HBM] * 3 + [VMEM] * 8,
        [
            shape((rows, 12 * span), LOW),
            shape((rows, 4 * span), LOW),
            shape(tokens.shape, F32),
            shape(news.shape, F32),
            shape((8, width), F32),
            shape((8, 8, rows), F32),
            shape((8, 1, wide), F32),
        ],
        [VMEM] * 7,
        [
            pltpu.VMEM((4,) + news.shape, F32),
            pltpu.VMEM(news.shape, F32),
            pltpu.VMEM((8, 8, rows), F32),
            pltpu.VMEM((8, 8, rows), F32),
            pltpu.VMEM((8, 8, rows), F32),
            DMA((3,)),
            DMA((4,)),
        ]
        + SWAP_SEMS * 5
        + scatter_ranks_scratch(tok_rows, width)
        + [
            pltpu.VMEM((4,) + g_in.shape[1:], LOW),
            pltpu.VMEM((4,) + g_out.shape[1:], LOW),
            pltpu.VMEM((tok_rows, width), F32),
            pltpu.VMEM((2, 8, width), F32),
            pltpu.VMEM(news.shape, F32),
        ]
        + scatter_items_scratch([g_in, g_out], 2),
        "backward_last",
        36,
    )


def pick_weights(attend_in, attend_out, expand, rank, span, units):
    rows = attend_in.shape[0]
    owners = expand.shape[1] // (4 * units)
    if not fast():
        w_in = pick(attend_in.reshape(rows, 3, 4, span), rank, 2).astype(LOW).reshape(rows, 3 * span)
        w_up = pick(expand.reshape(rows, owners, 4, units), rank, 2).astype(LOW).reshape(rows, owners * units)
        return jnp.concatenate([w_in, mine(attend_out, 1, 4, rank).astype(LOW)], axis=1), w_up

    def kernel(in_ref, out_ref, up_ref, io, up):
        here = lax.axis_index("seq")
        for part in range(4):

            @pl.when(here == part)
            def _(part=part):
                def one(at):
                    for block in range(3):
                        start = (block * 4 + part) * span
                        io[at, block * span : (block + 1) * span] = in_ref[at, start : start + span].astype(LOW)
                    io[at, 3 * span :] = out_ref[at, part * span : (part + 1) * span].astype(LOW)
                    for owner in range(owners):
                        start = (owner * 4 + part) * units
                        up[at, owner * units : (owner + 1) * units] = up_ref[at, start : start + units].astype(LOW)

                by_rows(rows, one)

    return pl.pallas_call(
        kernel,
        out_shape=[shape((rows, 4 * span), LOW), shape((rows, owners * units), LOW)],
        in_specs=[VMEM] * 3,
        out_specs=[VMEM] * 2,
        compiler_params=pltpu.CompilerParams(vmem_limit_bytes=32 * 1024 * 1024),
        name="pick_weights",
    )(attend_in, attend_out, expand)


def sum_owners(number, value, name):
    if not fast():
        return lax.psum(value, "fsdp")

    def kernel(src, out, boxes, *sems):
        owner = lax.axis_index("fsdp")
        greet(True, False)
        sends = Sends()
        boxes[owner] = src[...]
        swap_start(sends, lambda to: src, boxes, *sems)
        swap_wait(boxes, sems[1])
        total = boxes[0]
        for of in range(1, 8):
            total = total + boxes[of]
        out[...] = total
        sends.finish()

    block = jnp.full((8, 128), value, F32)
    total = call(
        kernel, number, (block,), [VMEM], shape((8, 128), F32), VMEM, [pltpu.VMEM((8, 8, 128), F32)] + SWAP_SEMS, name, 4
    )
    return total[0, 0]


def attend(query, keys, values):
    score_scale = 1.0 / math.sqrt(keys.shape[-1])
    scores = mixed_dot("qhd,khd->hqk", query, keys) * score_scale
    top = jnp.max(scores, axis=-1, keepdims=True)
    expo = jnp.exp(scores - top)
    total = jnp.sum(expo, axis=-1, keepdims=True)
    probs = (expo / total).astype(LOW)
    mixed = mixed_dot("hqk,khd->qhd", probs, values)
    return mixed.astype(LOW), (top + jnp.log(total))[..., 0]


def attend_back(query, keys, values, d_mixed, log_total):
    length, heads_here, head_dim = query.shape
    block = min(512, length)
    count = length // block
    score_scale = 1.0 / math.sqrt(head_dim)

    def back_block(carry, pieces):
        d_keys, d_values = carry
        query_block, d_block, log_block = pieces
        scores = mixed_dot("qhd,khd->hqk", query_block, keys) * score_scale
        probs = jnp.exp(scores - log_block[..., None])
        d_probs = mixed_dot("qhd,khd->hqk", d_block, values)
        delta = jnp.sum(probs * d_probs, axis=-1, keepdims=True)
        d_scores = (probs * (d_probs - delta)).astype(LOW)
        d_query = mixed_dot("hqk,khd->qhd", d_scores, keys) * score_scale
        d_keys = d_keys + mixed_dot("hqk,qhd->khd", d_scores, query_block) * score_scale
        d_values = d_values + mixed_dot("hqk,qhd->khd", probs.astype(LOW), d_block)
        return ((d_keys, d_values), d_query)

    empty = jnp.zeros((length, heads_here, head_dim), jnp.float32)
    blocked = (count, block, heads_here, head_dim)
    logs = log_total.reshape(heads_here, count, block).transpose(1, 0, 2)
    (d_keys, d_values), d_query = lax.scan(
        back_block, (empty, empty), (query.reshape(blocked), d_mixed.reshape(blocked), logs)
    )
    flat = (length, heads_here * head_dim)
    return jnp.concatenate(
        [d_query.reshape(flat), d_keys.reshape(flat), d_values.reshape(flat)], axis=1
    ).astype(LOW)


def adam_step(weight, moment, square, gradient, factor):
    clipped = gradient * factor
    moment_next = beta_one * moment + (1.0 - beta_one) * clipped
    square_next = beta_two * square + (1.0 - beta_two) * clipped * clipped
    moment_hat = moment_next / (1.0 - beta_one**STEP)
    square_hat = square_next / (1.0 - beta_two**STEP)
    master = weight - learn_rate * (
        moment_hat / (jnp.sqrt(square_hat) + adam_eps) + weight_decay * weight
    )
    return (master, moment_next, square_next)


def condition_start(latent_tokens, w_io, biases, timesteps, labels, time_first, time_second, class_table, modulation):
    owners, owner = lax.axis_size("fsdp"), lax.axis_index("fsdp")
    share = biases.shape[0]
    width = time_first.shape[1]
    first, second = time_first.astype(LOW), time_second.astype(LOW)
    table, modulation_low = class_table.astype(LOW), modulation.astype(LOW)
    units = first.shape[0]
    bias_low = biases.astype(LOW).astype(F32)
    features = time_features(timesteps).astype(LOW)
    if fast():
        note = jnp.concatenate(
            [
                jnp.broadcast_to(bias_low, (owners, share)),
                features.astype(F32).reshape(owners, units),
                jnp.broadcast_to(labels.astype(F32), (owners, 1)),
                jnp.zeros((owners, 127 - units), F32),
            ],
            axis=1,
        )[:, None]
        w_io_all, tokens, notes, act, slope, cond_cut, cond, mod = forward_first(
            w_io, latent_tokens, note, first, second, table, modulation_low
        )
        notes = notes[:, 0]
        all_bias = notes[:, :share].reshape(owners * share)
        my_features = notes[:, share : share + units]
        all_labels = notes[:, share + units]
        mod_values = mod.reshape(owners * mod.shape[2])
        state = (first, second, modulation_low, my_features, all_labels, act, slope, cond_cut, cond)
        return w_io_all, tokens, all_bias, mod_values, state
    w_io_all = lax.all_gather(w_io, "fsdp", axis=0)
    tokens = lax.all_gather(latent_tokens, "seq", axis=0)
    note = jnp.concatenate([bias_low, features[0].astype(F32), labels.astype(F32)])
    notes = lax.all_gather(note, "fsdp", axis=0)
    all_bias = notes[:, :share].reshape(owners * share)
    my_features = mine(notes[:, share:-1], 1, owners, owner)
    all_labels = notes[:, -1]
    hidden_time = lax.psum(mixed_dot("bf,fd->bd", my_features.astype(LOW), first), "fsdp") + all_bias[:width]
    act, slope = silu_parts(mine(hidden_time, 1, owners, owner))
    act = act.astype(LOW)
    onehot = (all_labels[:, None] == jnp.arange(NCLS, dtype=F32)[None, :]).astype(LOW)
    cond_part = mixed_dot("bd,de->be", act, second)
    class_part = mixed_dot("bc,cd->bd", onehot, table)
    class_wide = lax.dynamic_update_slice(jnp.zeros_like(cond_part), class_part, (0, owner * class_part.shape[1]))
    cond = lax.psum(cond_part + class_wide, "fsdp") + all_bias[width : 2 * width]
    mod_part = mixed_dot("bd,de->be", silu_parts(cond)[0].astype(LOW), modulation_low)
    mod_values = pick(lax.all_gather(mod_part, "fsdp", axis=0), owner, 1).reshape(owners * mod_part.shape[1])
    state = (first, second, modulation_low, my_features, all_labels, act.astype(F32), slope, None, cond)
    return w_io_all, tokens, all_bias, mod_values, state


def owner_sums(blocks):
    summed = [lax.psum_scatter(block.astype(F32), "fsdp", scatter_dimension=0, tiled=False) for block in blocks]
    return [lax.all_gather(block.astype(LOW), "seq", axis=0) for block in summed]


def condition_end(state, g_in, g_out, d_tokens, tokens, scale1, d_middle, d_mod_rest, tail, share):
    first, second, modulation_low, my_features, all_labels, act, slope, cond_cut, cond = state
    owners, owner, rank = lax.axis_size("fsdp"), lax.axis_index("fsdp"), lax.axis_index("seq")
    wide, width = modulation_low.shape[1], cond.shape[1]
    blank = jnp.zeros((2 * width,), F32)
    if fast():
        pad = -wide % 128
        tails = jnp.concatenate([jnp.zeros((owners * share - tail.shape[0],), F32), tail]).reshape(owners, share)
        news = jnp.concatenate(
            [jnp.concatenate([blank, d_mod_rest]).reshape(owners, wide), jnp.zeros((owners, pad), F32), tails], axis=1
        )[:, None]
        grad_in, grad_out, input_gradient, by_latent, d_cond, d_hid, sums = backward_last(
            g_in, g_out, d_tokens, tokens, scale1, d_middle, news, second, modulation_low, cond_cut, slope
        )
        d_mod = by_latent[:, 0, :wide]
        my_tail = jnp.sum(by_latent[:, 0, wide + pad :], axis=0)
        d_hidden = d_hid.transpose(1, 0, 2).reshape(owners, width)
        front = jnp.concatenate([jnp.sum(d_hidden, axis=0), jnp.sum(d_cond, axis=0), sums.reshape(owners * wide)])
        count = front.shape[0] // share
        grad_bias = jnp.where(
            owner < count, pick(front.reshape(count, share), jnp.minimum(owner, count - 1)), my_tail
        )
    else:
        (d_hattn,) = rank_sums(6, [d_tokens], "sums")
        norm, inverse = layer_norm(tokens.astype(F32))
        input_gradient = d_middle + layer_norm_back(norm, inverse, d_hattn * (1.0 + scale1))
        my_d_mod = jnp.concatenate([jnp.sum(d_hattn, axis=0), jnp.sum(d_hattn * norm, axis=0), d_mod_rest])
        grad_in, grad_out = owner_sums([g_in, g_out])
        rows, span = grad_out.shape[1], grad_out.shape[2]
        grad_in = grad_in.reshape(4, rows, 3, span).transpose(1, 2, 0, 3).reshape(rows, 12 * span)
        grad_out = grad_out.transpose(1, 0, 2).reshape(rows, 4 * span)
        all_d_mod = lax.all_gather(lax.psum(my_d_mod, "seq"), "fsdp", axis=0)
        d_mod = mine(all_d_mod, 1, owners, owner)
        part = high_dot(d_mod, modulation_low.astype(F32).T)
        d_cond = lax.psum(part, "fsdp") * silu_parts(cond)[1]
        d_time = high_dot(d_cond, second.astype(F32).T) * slope
        d_hidden = lax.all_gather(d_time, "fsdp", axis=0).transpose(1, 0, 2).reshape(owners, width)
        tail = lax.psum(tail, ("seq", "fsdp"))
        all_bias = jnp.concatenate(
            [jnp.sum(d_hidden, axis=0), jnp.sum(d_cond, axis=0), jnp.sum(all_d_mod, axis=0), tail]
        )
        grad_bias = mine(all_bias, 0, owners, owner)
    onehot = (all_labels[:, None] == jnp.arange(NCLS, dtype=F32)[None, :]).astype(F32)
    cond_act = silu_parts(cond)[0].astype(LOW).astype(F32)
    grad_mod = high_dot(cond_act.T, d_mod)
    grad_class = high_dot(onehot.T, mine(d_cond, 1, owners, owner))
    grad_second = high_dot(act.T, d_cond)
    grad_first = high_dot(my_features.T, d_hidden)
    condition_gradient = lax.dynamic_slice_in_dim(d_cond, owner, 1, 0)
    return grad_in, grad_out, input_gradient, (grad_first, grad_second, grad_class, grad_mod), grad_bias, condition_gradient


def per_device(latents, timesteps, labels, upstream, *state):
    params, moments, squares = state[:9], state[9:18], state[18:]
    time_first, time_second, class_table, modulation, attend_in, attend_out, expand, contract, biases = params
    lat_dev, tok_rows, width = latents.shape
    assert lat_dev == 1
    hidden = expand.shape[1]
    ranks = lax.axis_size("seq")
    owners = lax.axis_size("fsdp")
    rank = lax.axis_index("seq")
    heads_here = H // ranks
    span = heads_here * HD
    length = ranks * tok_rows
    rows = width // owners
    unit = hidden // (owners * ranks)
    hid_here = owners * unit

    my_io, my_up = pick_weights(attend_in, attend_out, expand, rank, span, unit)
    my_down = mine(contract, 0, ranks, rank).astype(LOW)
    w_io, tokens, all_bias, mod_values, kept = condition_start(
        latents[0], my_io, biases, timesteps, labels, time_first, time_second, class_table, modulation
    )
    w_io = w_io.reshape(width, 4 * span)
    w_in = w_io[:, : 3 * span]
    inputs_low = tokens.reshape(length, width)

    b_t1, b_t2, b_mod, b_q, b_v, b_out, b_up, b_down = split_biases(all_bias, width, hidden)
    mod_values = (mod_values + b_mod).reshape(6, 1, width)
    shift1, scale1, gate1, shift2, scale2, gate2 = [mod_values[index] for index in range(6)]

    inputs = inputs_low.astype(F32)
    norm_one, _ = layer_norm(inputs)
    h_attn = (norm_one * (1.0 + scale1) + shift1).astype(LOW)
    my_b_q, my_b_v = mine(b_q, 0, ranks, rank), mine(b_v, 0, ranks, rank)
    qkv_bias = jnp.concatenate([my_b_q, jnp.zeros_like(my_b_q), my_b_v])
    qkv = (mixed_dot("td,de->te", h_attn, w_in) + qkv_bias).astype(LOW)
    head_shape = (length, heads_here, HD)
    if fast():
        w_up, w_down, d_out_low, w_out, mixed, logs = forward_attention(
            qkv, my_up, my_down, upstream[0], w_io
        )
    else:
        query, keys, values = [qkv[:, part * span : (part + 1) * span].reshape(head_shape) for part in range(3)]
        mixed_heads, logs = attend(query, keys, values)
        w_up, w_down, d_out_low, w_out, mixed = gathers(
            2, [my_up, my_down], [upstream[0], w_io[:, 3 * span :], mixed_heads.reshape(length, span)], "gathers"
        )
        w_out = w_out.transpose(1, 0, 2).reshape(width, width)
        mixed = mixed.transpose(1, 0, 2).reshape(length, width)
    w_up, w_down = w_up.reshape(width, hid_here), w_down.reshape(hid_here, width)
    d_out_low = d_out_low.reshape(length, width)
    attn_out = mixed_dot("td,de->te", mixed, w_out) + b_out
    middle = inputs + gate1 * attn_out
    norm_two, inverse_two = layer_norm(middle)
    h_mlp = (norm_two * (1.0 + scale2) + shift2).astype(LOW)

    my_b_up = pick(b_up.reshape(owners, ranks, unit), rank, 1).reshape(hid_here)
    pre_act = mixed_dot("td,df->tf", h_mlp, w_up) + my_b_up
    act_f, gelu_pull = jax.vjp(partial(jax.nn.gelu, approximate=True), pre_act)
    act = act_f.astype(LOW)
    by_rank = (ranks, tok_rows, width)
    by_owner = lambda block: block.astype(LOW).reshape((owners, -1) + block.shape[1:])
    mlp_part = mixed_dot("tf,fd->td", act, w_down).astype(LOW).reshape(by_rank)
    d_out = d_out_low.astype(F32)
    d_mlp = (d_out * gate2).astype(LOW)
    d_act = mixed_dot("td,fd->tf", d_mlp, w_down)
    d_pre = gelu_pull(d_act)[0].astype(LOW)
    d_hmlp_part = mixed_dot("tf,df->td", d_pre, w_up).astype(LOW).reshape(by_rank)
    (d_hmlp,) = rank_sums(4, [d_hmlp_part], "sum_feed")
    g_down = by_owner(mixed_dot("tf,td->fd", act, d_mlp))
    g_up = by_owner(mixed_dot("td,tf->df", h_mlp, d_pre))
    gb_up = jnp.sum(d_pre.astype(F32), axis=0)
    gb_down = jnp.sum(d_mlp.astype(F32), axis=0)

    own = lambda array: mine(array, 0, ranks, rank)
    my_attn_out, my_middle, my_norm_two, my_inverse_two = own(attn_out), own(middle), own(norm_two), own(inverse_two)
    my_d_out = upstream[0].astype(F32)
    d_shift2 = jnp.sum(d_hmlp, axis=0)
    d_scale2 = jnp.sum(d_hmlp * my_norm_two, axis=0)
    d_middle = my_d_out + layer_norm_back(my_norm_two, my_inverse_two, d_hmlp * (1.0 + scale2))
    d_gate1 = jnp.sum(d_middle * my_attn_out, axis=0)
    my_d_attn = (d_middle * gate1).astype(LOW)
    if fast():
        grad_up, grad_down, d_attn, mlp_sum, d_qkv = backward_attention(
            g_up, g_down, my_d_attn, mlp_part, qkv, w_out, logs, unit
        )
        d_attn = d_attn.reshape(length, width)
    else:
        (mlp_sum,) = rank_sums(5, [mlp_part], "sums")
        (d_attn,) = gathers(5, [], [my_d_attn], "gathers")
        d_attn = d_attn.reshape(length, width)
        d_mixed = mixed_dot("te,de->td", d_attn, mine(w_out, 0, ranks, rank)).astype(LOW)
        d_qkv = attend_back(query, keys, values, d_mixed.reshape(head_shape), logs)
        grad_up, grad_down = owner_sums([g_up, g_down])
        grad_up = grad_up.reshape(ranks, rows, owners, unit).transpose(1, 2, 0, 3).reshape(rows, hidden)
    mlp_out = mlp_sum + b_down
    output = (my_middle + gate2 * mlp_out).astype(LOW)
    d_gate2 = jnp.sum(my_d_out * mlp_out, axis=0)
    g_in = by_owner(mixed_dot("td,te->de", h_attn, d_qkv))
    g_out = by_owner(mixed_dot("td,te->de", mixed, mine(d_attn, 1, ranks, rank)))
    d_hattn_part = mixed_dot("te,de->td", d_qkv, w_in).astype(LOW).reshape(by_rank)
    d_mod_rest = jnp.concatenate([d_gate1, d_shift2, d_scale2, d_gate2])
    gb_qv = jnp.sum(d_qkv.astype(F32), axis=0)
    wide = lambda part, size: lax.dynamic_update_slice(jnp.zeros((size,), F32), part, (rank * part.shape[0],))
    gb_up_wide = lax.dynamic_update_slice(
        jnp.zeros((owners, ranks, unit), F32), gb_up.reshape(owners, 1, unit), (0, rank, 0)
    ).reshape(hidden)
    gb_tail = jnp.concatenate(
        [
            wide(gb_qv[:span], width),
            wide(gb_qv[2 * span :], width),
            jnp.sum(my_d_attn.astype(F32), axis=0),
            gb_up_wide,
            jnp.where(rank == 0, gb_down, 0.0),
        ]
    )
    grad_in, grad_out, input_gradient, small_grads, grad_bias, condition_gradient = condition_end(
        kept, g_in, g_out, d_hattn_part, latents[0], scale1, d_middle, d_mod_rest, gb_tail, biases.shape[0]
    )
    grad_in, grad_out, grad_up, grad_down = [grad.astype(F32) for grad in (grad_in, grad_out, grad_up, grad_down)]
    grad_down = grad_down.reshape(contract.shape)
    gradients = small_grads + (grad_in, grad_out, grad_up, grad_down, grad_bias)
    local_sum = sum(jnp.sum(gradient * gradient) for gradient in gradients)
    norm_before = jnp.sqrt(sum_owners(7, local_sum, "sum_squares"))
    factor = clip_limit / jnp.maximum(norm_before, clip_limit)
    results = [
        adam_step(params[index], moments[index], squares[index], gradients[index], factor)
        for index in range(9)
    ]
    return (
        (output[None], input_gradient[None], condition_gradient, norm_before)
        + gradients
        + tuple(result[0] for result in results)
        + tuple(result[1] for result in results)
        + tuple(result[2] for result in results)
    )


def solution(mesh):
    tokens = P("fsdp", "seq", None)
    rows, columns = P("fsdp", None), P(None, "fsdp")
    weights = (rows, rows, columns, columns, rows, rows, rows, rows, P("fsdp"))
    return jax.shard_map(
        per_device,
        mesh=mesh,
        in_specs=(tokens, P("fsdp"), P("fsdp"), tokens) + weights * 3,
        out_specs=(tokens, tokens, rows, P()) + weights * 4,
        check_vma=False,
    )
```

```python
from functools import partial
import math

import jax
import jax.numpy as jnp
from jax import lax
from jax.experimental import pallas as pl
from jax.experimental.pallas import tpu as pltpu
from jax.sharding import PartitionSpec as P

H = 16
HD = 72
FREQ = 256
NCLS = 1000
STEP = 10


HIGH = lax.Precision.HIGHEST
LOW = jnp.bfloat16
norm_eps = 1e-06
beta_one = 0.9
beta_two = 0.999
learn_rate = 0.04
weight_decay = 0.01
adam_eps = 1e-08
clip_limit = 1.0


def layer_norm(value):
    centre = value - jnp.mean(value, axis=-1, keepdims=True)
    spread = jnp.mean(centre * centre, axis=-1, keepdims=True)
    inverse = lax.rsqrt(spread + norm_eps)
    return centre * inverse, inverse


def layer_norm_back(norm, inverse, grad):
    first = jnp.mean(grad, axis=-1, keepdims=True)
    second = jnp.mean(grad * norm, axis=-1, keepdims=True)
    return inverse * (grad - first - norm * second)


def silu_parts(value):
    gate = jax.nn.sigmoid(value)
    return value * gate, gate * (1.0 + value * (1.0 - gate))


def time_features(timesteps):
    half = FREQ // 2
    freqs = jnp.exp(-math.log(10000.0) * jnp.arange(half, dtype=jnp.float32) / half)
    angles = timesteps.astype(jnp.float32)[:, None] * freqs[None, :]
    return jnp.concatenate([jnp.cos(angles), jnp.sin(angles)], axis=-1)


def split_biases(biases, width, hidden):
    widths = [width, width, 6 * width, width, width, width, hidden, width]
    pieces = []
    start = 0
    for length in widths:
        pieces.append(biases[start : start + length])
        start = start + length
    return pieces


def high_dot(left, right):
    return jnp.dot(left, right, precision=HIGH, preferred_element_type=jnp.float32)


def mixed_dot(form, left, right):
    return jnp.einsum(form, left, right, preferred_element_type=jnp.float32)


def pick(array, index, axis=0):
    return lax.dynamic_index_in_dim(array, index, axis, keepdims=False)


def mine(array, axis, parts, index):
    size = array.shape[axis] // parts
    return lax.dynamic_slice_in_dim(array, index * size, size, axis)


HBM = pl.BlockSpec(memory_space=pl.ANY)
VMEM = pl.BlockSpec(memory_space=pltpu.VMEM)
DMA = pltpu.SemaphoreType.DMA
F32 = jnp.float32


def fast():
    return lax.axis_size("fsdp") == 8 and lax.axis_size("seq") == 4


def places():
    owner, rank = lax.axis_index("fsdp"), lax.axis_index("seq")
    return owner, rank, lax.div(owner, 2), lax.rem(owner, 2), lax.div(rank, 2), lax.rem(rank, 2)


def remote(src, dst, sent, landed, **where):
    return pltpu.make_async_remote_copy(
        src_ref=src, dst_ref=dst, send_sem=sent, recv_sem=landed, device_id=where, device_id_type=pl.DeviceIdType.MESH
    )


def arrived(dst, landed, **where):
    remote(dst, dst, landed, landed, **where).wait_recv()


def greet(over_owners, over_ranks):
    owner, rank, *_ = places()
    barrier = pltpu.get_barrier_semaphore()
    count = 0
    if over_owners:
        for step in range(1, 8):
            pl.semaphore_signal(
                barrier, inc=1, device_id={"fsdp": lax.rem(owner + step, 8)}, device_id_type=pl.DeviceIdType.MESH
            )
        count += 7
    if over_ranks:
        for step in range(1, 4):
            pl.semaphore_signal(
                barrier, inc=1, device_id={"seq": lax.rem(rank + step, 4)}, device_id_type=pl.DeviceIdType.MESH
            )
        count += 3
    pl.semaphore_wait(barrier, count)


def run_all(parts):
    parts = list(parts)
    while parts:
        for part in list(parts):
            try:
                next(part)
            except StopIteration:
                parts.remove(part)


class Sends:
    def __init__(self):
        self.live = []

    def start(self, copy, when=None):
        self.live.append((copy, when))
        if when is None:
            copy.start()
        else:
            pl.when(when)(copy.start)

    def finish(self):
        for copy, when in self.live:
            wait = copy.wait_send if hasattr(copy, "wait_send") else copy.wait
            if when is None:
                wait()
            else:
                pl.when(when)(wait)


def gather_owners(src, out, sems):
    own_sem, sent, landed = sems
    owner, rank, z, y, x, core = places()
    mate = owner + 1 - 2 * y
    sends = Sends()
    local = pltpu.make_async_copy(src, out.at[owner], own_sem)
    local.start()
    sends.start(remote(src, out.at[owner], sent.at[0, 0], landed.at[owner], fsdp=owner + 2), z < 3)
    sends.start(remote(src, out.at[owner], sent.at[0, 1], landed.at[owner], fsdp=owner - 2), z > 0)
    sends.start(remote(src, out.at[owner], sent.at[0, 2], landed.at[owner], fsdp=mate))
    yield
    for far in (1, 2, 3):
        for sign in (-1, 1):
            block = owner + sign * 2 * far
            here = (z >= far) if sign < 0 else (z + far <= 3)
            on = (z < 3) if sign < 0 else (z > 0)
            at = far if sign < 0 else 3 + far
            pl.when(here)(lambda: arrived(out.at[block], landed.at[block], fsdp=mate))
            sends.start(
                remote(out.at[block], out.at[block], sent.at[at, 0], landed.at[block], fsdp=owner - sign * 2), here & on
            )
            sends.start(remote(out.at[block], out.at[block], sent.at[at, 2], landed.at[block], fsdp=mate), here)
        yield
    for step in range(4):
        block = step * 2 + 1 - y
        arrived(out.at[block], landed.at[block], fsdp=mate)
    local.wait()
    sends.finish()


GATHER_OWNERS_SEMS = [DMA(()), DMA((7, 3)), DMA((8,))]


def gather_ranks(src, out, sems, local_copy=True):
    own_sem, sent, landed = sems
    owner, rank, z, y, x, core = places()
    mate, across, last = x * 2 + 1 - core, (1 - x) * 2 + core, (1 - x) * 2 + 1 - core
    sends = Sends()
    local = None
    if local_copy:
        local = pltpu.make_async_copy(src, out.at[rank], own_sem)
        local.start()
    sends.start(remote(src, out.at[rank], sent.at[0], landed.at[rank], seq=across))
    sends.start(remote(src, out.at[rank], sent.at[1], landed.at[rank], seq=mate))
    yield
    yield
    arrived(out.at[across], landed.at[across], seq=across)
    sends.start(remote(out.at[across], out.at[across], sent.at[2], landed.at[across], seq=mate))
    yield
    arrived(out.at[mate], landed.at[mate], seq=mate)
    arrived(out.at[last], landed.at[last], seq=mate)
    if local is not None:
        local.wait()
    sends.finish()


GATHER_RANKS_SEMS = [DMA(()), DMA((3,)), DMA((4,))]


def by_rows(count, body, step=16):
    def one(index, carry):
        body(pl.ds(pl.multiple_of(index * step, step), step))
        return carry

    lax.fori_loop(0, count // step, one, 0)


def scatter_ranks(parts, out, own, mail, leave, enter, sems):
    own_sem, sent, landed = sems
    owner, rank, z, y, x, core = places()
    mate, across = x * 2 + 1 - core, (1 - x) * 2 + core
    sends = Sends()
    loads = []
    for step in (1, 0):
        to = lax.rem(x + step, 2)
        loads.append(pltpu.make_async_copy(parts.at[to * 2 + core], own.at[step], own_sem.at[step]))
        loads[-1].start()
        sends.start(remote(parts.at[to * 2 + 1 - core], mail.at[step], sent.at[step], landed.at[step], seq=mate))
    yield
    loads[0].wait()
    arrived(mail.at[1], landed.at[1], seq=mate)

    def first(rows):
        leave[rows] = (own[1, rows].astype(F32) + mail[1, rows].astype(F32)).astype(LOW)

    by_rows(out.shape[0], first)
    sends.start(remote(leave, enter, sent.at[2], landed.at[2], seq=across))
    yield
    loads[1].wait()
    arrived(mail.at[0], landed.at[0], seq=mate)
    yield
    arrived(enter, landed.at[2], seq=across)

    def last(rows):
        out[rows] = own[0, rows].astype(F32) + mail[0, rows].astype(F32) + enter[rows].astype(F32)

    by_rows(out.shape[0], last)
    sends.finish()


def scatter_ranks_scratch(rows, columns):
    return [
        pltpu.VMEM((2, rows, columns), LOW),
        pltpu.VMEM((2, rows, columns), LOW),
        pltpu.VMEM((rows, columns), LOW),
        pltpu.VMEM((rows, columns), LOW),
        DMA((2,)),
        DMA((3,)),
        DMA((3,)),
    ]


def scatter_owners(parts, out, own, mail, rise, fall, leave, sems):
    own_sem, y_sent, y_landed, z_sent, up_landed, down_landed = sems[:6]
    owner, rank, z, y, x, core = places()
    mate = owner + 1 - 2 * y
    rows_here = own.shape[1]
    sends = Sends()
    loads = {}
    for to in (3, 0, 2, 1):
        sends.start(remote(parts(to * 2 + 1 - y), mail.at[to], y_sent.at[to], y_landed.at[to], fsdp=mate))
        loads[to] = pltpu.make_async_copy(parts(to * 2 + y), own.at[to], own_sem.at[to])
        loads[to].start()
        yield
    for to, up in ((3, True), (0, False), (2, True), (1, False), (1, True), (2, False)):
        here = (z < to) if up else (z > to)
        more = (z > 0) if up else (z < 3)
        box, box_landed = (rise, up_landed) if up else (fall, down_landed)

        def total(to=to, more=more, box=box, box_landed=box_landed):
            loads[to].wait()
            arrived(mail.at[to], y_landed.at[to], fsdp=mate)

            def start(rows):
                leave[to, rows] = (own[to, rows].astype(F32) + mail[to, rows].astype(F32)).astype(LOW)

            def add(rows):
                leave[to, rows] = (
                    own[to, rows].astype(F32) + mail[to, rows].astype(F32) + box[to, rows].astype(F32)
                ).astype(LOW)

            @pl.when(more)
            def _():
                arrived(box.at[to], box_landed.at[to], fsdp=mate)
                by_rows(rows_here, add)

            @pl.when(jnp.logical_not(more))
            def _():
                by_rows(rows_here, start)

        pl.when(here)(total)
        sends.start(
            remote(
                leave.at[to], box.at[to], z_sent.at[to], box_landed.at[to], fsdp=owner + 2 if up else owner - 2
            ),
            here,
        )
        yield
    for to in range(4):
        at_home = z == to

        @pl.when(at_home)
        def _(to=to):
            loads[to].wait()
            arrived(mail.at[to], y_landed.at[to], fsdp=mate)
            if to > 0:
                arrived(rise.at[to], up_landed.at[to], fsdp=mate)
            if to < 3:
                arrived(fall.at[to], down_landed.at[to], fsdp=mate)

            def end(rows):
                value = own[to, rows].astype(F32) + mail[to, rows].astype(F32)
                if to > 0:
                    value = value + rise[to, rows].astype(F32)
                if to < 3:
                    value = value + fall[to, rows].astype(F32)
                leave[to, rows] = value.astype(LOW)

            by_rows(rows_here, end)

    yield from gather_ranks(leave.at[z], out, sems[6:])
    sends.finish()


def scatter_owners_scratch(rows, columns):
    return [pltpu.VMEM((4, rows, columns), LOW)] * 5 + [DMA((4,))] * 6 + GATHER_RANKS_SEMS


def swap_start(sends, src_of, dst, sent, landed):
    owner = lax.axis_index("fsdp")
    for step in range(1, 8):
        to = lax.rem(owner + step, 8)
        sends.start(remote(src_of(to), dst.at[owner], sent.at[step - 1], landed.at[owner], fsdp=to))


def swap_wait(dst, landed):
    owner = lax.axis_index("fsdp")
    for step in range(1, 8):
        of = lax.rem(owner + step, 8)
        arrived(dst.at[of], landed.at[of], fsdp=of)


SWAP_SEMS = [DMA((7,)), DMA((8,))]


def low_dot(left, right, contract):
    return lax.dot_general(left, right, ((contract[:1], contract[1:]), ((), ())), preferred_element_type=F32)


def fine_dot(left, right, contract):
    high = left.astype(LOW)
    rest = left - high.astype(F32)
    return low_dot(high, right, contract) + low_dot(rest.astype(LOW), right, contract)


def stack_rows(ref):
    return jnp.concatenate([ref[index] for index in range(8)], axis=0)


def condition_forward(note, first, second, table, modulation, outs, scratch, sems):
    notes, act_out, slope_out, cond_cut, cond_out, mod = outs
    send_cut, hid_in, cond_in, bias_cut, mod_cut = scratch
    owner = lax.axis_index("fsdp")
    cut = second.shape[0]
    share = note.shape[2] - 128
    sends = Sends()
    notes[owner] = note[owner]
    swap_start(sends, lambda to: note.at[to], notes, *sems[0:2])
    yield
    swap_wait(notes, sems[1])
    rows = stack_rows(notes)
    feats = rows[:, share : share + first.shape[0]].astype(LOW)
    label = rows[:, share + first.shape[0] : share + first.shape[0] + 1]
    hidden = low_dot(feats, first[...], (1, 0))
    for to in range(8):
        send_cut[0, to] = hidden[:, to * cut : (to + 1) * cut]
        bias_cut[0, to] = rows[0:1, to * cut : (to + 1) * cut]
        bias_cut[1, to] = rows[0:1, (8 + to) * cut : (9 + to) * cut]
    hid_in[owner] = send_cut[0, owner]
    swap_start(sends, lambda to: send_cut.at[0, to], hid_in, *sems[2:4])
    yield
    classes = lax.broadcasted_iota(jnp.int32, (8, table.shape[1]), 1).astype(F32)
    onehot = (label == classes).astype(F32).astype(LOW)
    from_class = low_dot(onehot, table[...], (1, 1))
    swap_wait(hid_in, sems[3])
    hidden_cut = bias_cut[0, owner] + jnp.zeros((8, cut), F32)
    for of in range(8):
        hidden_cut = hidden_cut + hid_in[of]
    act, slope = silu_parts(hidden_cut)
    act = act.astype(LOW)
    act_out[...] = act.astype(F32)
    slope_out[...] = slope
    part = low_dot(act, second[...], (1, 0))
    for to in range(8):
        send_cut[1, to] = part[:, to * cut : (to + 1) * cut]
    cond_in[owner] = send_cut[1, owner]
    swap_start(sends, lambda to: send_cut.at[1, to], cond_in, *sems[4:6])
    yield
    swap_wait(cond_in, sems[5])
    mine_cond = bias_cut[1, owner] + from_class
    for of in range(8):
        mine_cond = mine_cond + cond_in[of]
    cond_cut[owner] = mine_cond
    swap_start(sends, lambda to: cond_cut.at[owner], cond_cut, *sems[6:8])
    yield
    swap_wait(cond_cut, sems[7])
    for of in range(8):
        cond_out[:, of * cut : (of + 1) * cut] = cond_cut[of]
    cond_act = silu_parts(cond_out[...])[0].astype(LOW)
    values = low_dot(cond_act, modulation[...], (1, 1))
    for to in range(8):
        mod_cut[to] = values[to : to + 1]
    mod[owner] = mod_cut[owner]
    swap_start(sends, lambda to: mod_cut.at[to], mod, *sems[8:10])
    yield
    swap_wait(mod, sems[9])
    sends.finish()


def condition_backward(news, second, modulation, cond_cut, time_slope, outs, scratch, sems):
    by_latent, d_cond_out, d_hid_cut, sums = outs
    rank_news, owner_news, d_cut, d_in, d_cond_cut = scratch
    owner, rank, *_ = places()
    cut = second.shape[0]
    wide = modulation.shape[0]
    sends = Sends()
    for step in range(1, 4):
        to = lax.rem(rank + step, 4)
        sends.start(remote(news, rank_news.at[rank], sems[0].at[step - 1], sems[1].at[rank], seq=to))
    yield
    for step in range(1, 4):
        of = lax.rem(rank + step, 4)
        arrived(rank_news.at[of], sems[1].at[of], seq=of)
    rank_news[rank] = news[...]
    for to in range(8):
        owner_news[to] = rank_news[0, to] + rank_news[1, to] + rank_news[2, to] + rank_news[3, to]
    by_latent[owner] = owner_news[owner]
    swap_start(sends, lambda to: owner_news.at[to], by_latent, *sems[2:4])
    yield
    swap_wait(by_latent, sems[3])
    d_mod = stack_rows(by_latent)[:, :wide]
    part = fine_dot(d_mod, modulation[...], (1, 0))
    for to in range(8):
        d_cut[to] = part[:, to * cut : (to + 1) * cut]
    d_in[owner] = d_cut[owner]
    swap_start(sends, lambda to: d_cut.at[to], d_in, *sems[4:6])
    sums[owner] = jnp.sum(d_mod, axis=0, keepdims=True)
    swap_start(sends, lambda to: sums.at[owner], sums, *sems[6:8])
    yield
    swap_wait(d_in, sems[5])
    total = d_in[0]
    for of in range(1, 8):
        total = total + d_in[of]
    d_cond_cut[owner] = total * silu_parts(cond_cut[owner])[1]
    swap_start(sends, lambda to: d_cond_cut.at[owner], d_cond_cut, *sems[8:10])
    yield
    swap_wait(d_cond_cut, sems[9])
    for of in range(8):
        d_cond_out[:, of * cut : (of + 1) * cut] = d_cond_cut[of]
    d_hid_cut[owner] = fine_dot(d_cond_out[...], second[...], (1, 1)) * time_slope[...]
    swap_start(sends, lambda to: d_hid_cut.at[owner], d_hid_cut, *sems[10:12])
    yield
    swap_wait(d_hid_cut, sems[11])
    swap_wait(sums, sems[7])
    sends.finish()


def takes(refs, *counts):
    refs = list(refs)
    groups = []
    for count in counts:
        groups.append(refs[:count])
        refs = refs[count:]
    assert not refs
    return groups


def call(kernel, number, args, in_specs, outs, out_specs, scratch, name, room):
    return pl.pallas_call(
        kernel,
        out_shape=outs,
        in_specs=in_specs,
        out_specs=out_specs,
        scratch_shapes=scratch,
        compiler_params=pltpu.CompilerParams(
            collective_id=number, has_side_effects=True, vmem_limit_bytes=room * 1024 * 1024
        ),
        name=name,
    )(*args)


def shape(dims, kind):
    return jax.ShapeDtypeStruct(tuple(dims), kind)


def forward_first(w_io, tokens, note, first, second, table, modulation):
    rows, width = second.shape
    wide = modulation.shape[0]

    def kernel(*refs):
        args, outs, scratch, cond_sems, io_sems, token_sems = takes(refs, 7, 8, 5, 10, 3, 3)
        greet(True, True)
        run_all(
            [
                condition_forward(args[2], *args[3:7], outs[2:8], scratch, cond_sems),
                gather_ranks(args[1], outs[1], token_sems),
                gather_owners(args[0], outs[0], io_sems),
            ]
        )

    return call(
        kernel,
        1,
        (w_io, tokens, note, first, second, table, modulation),
        [VMEM] * 7,
        [
            shape((8,) + w_io.shape, LOW),
            shape((4,) + tokens.shape, LOW),
            shape(note.shape, F32),
            shape((8, rows), F32),
            shape((8, rows), F32),
            shape((8, 8, rows), F32),
            shape((8, width), F32),
            shape((8, 1, wide), F32),
        ],
        [HBM] * 2 + [VMEM] * 6,
        [
            pltpu.VMEM((2, 8, 8, rows), F32),
            pltpu.VMEM((8, 8, rows), F32),
            pltpu.VMEM((8, 8, rows), F32),
            pltpu.VMEM((2, 8, 1, rows), F32),
            pltpu.VMEM((8, 1, wide), F32),
        ]
        + SWAP_SEMS * 5
        + GATHER_OWNERS_SEMS
        + GATHER_RANKS_SEMS,
        "forward_first",
        20,
    )


QUERIES = 256


def block_of(index, size=QUERIES):
    return pl.ds(pl.multiple_of(index * size, size), size)


def attend_heads(qkv, mixed, logs, head_rows, heads):
    length = qkv.shape[0]
    span = heads * HD
    scale = 1.0 / math.sqrt(HD)
    for head in range(heads):
        for part in range(3):
            start = part * span + head * HD
            head_rows[part] = qkv[:, start : start + HD]

        def block(index, carry):
            query = head_rows[0, block_of(index)]
            scores = low_dot(head_rows[1], query, (1, 1)) * scale
            top = jnp.max(scores, axis=0, keepdims=True)
            expo = jnp.exp(scores - top)
            total = jnp.sum(expo, axis=0, keepdims=True)
            probs = (expo * (1.0 / total)).astype(LOW)
            mixed[block_of(index), head * HD : (head + 1) * HD] = low_dot(head_rows[2], probs, (0, 0)).T.astype(LOW)
            logs[head, index] = top + jnp.log(total)
            return carry

        lax.fori_loop(0, length // QUERIES, block, 0)
        yield


def attend_heads_back(qkv, logs, d_mixed, d_qkv, head_rows, d_head, d_keys, d_values, heads):
    length = qkv.shape[0]
    span = heads * HD
    scale = 1.0 / math.sqrt(HD)
    for head in range(heads):
        lanes = slice(head * HD, (head + 1) * HD)
        for part in range(3):
            start = part * span + head * HD
            head_rows[part] = qkv[:, start : start + HD]
        d_head[...] = d_mixed[:, lanes]
        d_keys[...] = jnp.zeros_like(d_keys)
        d_values[...] = jnp.zeros_like(d_values)

        def block(index, carry):
            query, d_block = head_rows[0, block_of(index)], d_head[block_of(index)]
            scores = low_dot(head_rows[1], query, (1, 1)) * scale
            probs = jnp.exp(scores - logs[head, index])
            d_probs = low_dot(head_rows[2], d_block, (1, 1))
            delta = jnp.sum(probs * d_probs, axis=0, keepdims=True)
            d_scores = (probs * (d_probs - delta)).astype(LOW)
            d_keys[...] += low_dot(d_scores, query, (1, 0))
            d_values[...] += low_dot(probs.astype(LOW), d_block, (1, 0))
            d_query = low_dot(head_rows[1], d_scores, (0, 0)).T * scale
            d_qkv[block_of(index), lanes] = d_query.astype(LOW)
            return carry

        lax.fori_loop(0, length // QUERIES, block, 0)
        d_qkv[:, span + head * HD : span + (head + 1) * HD] = (d_keys[...] * scale).astype(LOW)
        d_qkv[:, 2 * span + head * HD : 2 * span + (head + 1) * HD] = d_values[...].astype(LOW)
        yield


def beside(blocks, out):
    columns = blocks.shape[2]

    def one(at):
        for part in range(4):
            out[at, part * columns : (part + 1) * columns] = blocks[part, at]

    by_rows(out.shape[0], one)


def forward_attention(qkv, w_up, w_down, upstream, w_io):
    length = qkv.shape[0]
    heads = qkv.shape[1] // (3 * HD)
    span = heads * HD
    width = w_io.shape[0]

    def kernel(*refs):
        args, outs, scratch, up_sems, down_sems, token_sems, out_sems, mixed_sems = takes(refs, 5, 6, 5, 3, 3, 3, 3, 3)
        mixed_here, head_rows, mixed_all, out_here, out_all = scratch
        greet(True, True)

        def attention():
            steps = attend_heads(args[0], mixed_here, outs[5], head_rows, heads)
            for index, _ in enumerate(steps):
                if 0 < index < heads - 1:
                    yield
            yield from gather_ranks(mixed_here, mixed_all, mixed_sems)

        def out_weight():
            out_here[...] = args[4][:, 3 * span :]
            yield from gather_ranks(out_here, out_all, out_sems)
            beside(out_all, outs[3])

        run_all(
            [
                gather_owners(args[1], outs[0], up_sems),
                gather_owners(args[2], outs[1], down_sems),
                out_weight(),
                attention(),
                gather_ranks(args[3], outs[2], token_sems),
            ]
        )
        beside(mixed_all, outs[4])

    return call(
        kernel,
        2,
        (qkv, w_up, w_down, upstream, w_io),
        [VMEM] * 5,
        [
            shape((8,) + w_up.shape, LOW),
            shape((8,) + w_down.shape, LOW),
            shape((4,) + upstream.shape, LOW),
            shape((width, 4 * span), LOW),
            shape((length, 4 * span), LOW),
            shape((heads, length // QUERIES, 1, QUERIES), F32),
        ],
        [HBM] * 3 + [VMEM] * 3,
        [
            pltpu.VMEM((length, span), LOW),
            pltpu.VMEM((3, length, HD), LOW),
            pltpu.VMEM((4, length, span), LOW),
            pltpu.VMEM((width, span), LOW),
            pltpu.VMEM((4, width, span), LOW),
        ]
        + GATHER_OWNERS_SEMS * 2
        + GATHER_RANKS_SEMS * 3,
        "forward_attention",
        40,
    )


def gathers(number, by_owner, by_rank, name):
    if not fast():
        return [lax.all_gather(block, "fsdp", axis=0) for block in by_owner] + [
            lax.all_gather(block, "seq", axis=0) for block in by_rank
        ]
    many, few = len(by_owner), len(by_rank)

    def kernel(*refs):
        groups = takes(refs, many + few, many + few, *[3] * (many + few))
        args, outs, sems = groups[0], groups[1], groups[2:]
        greet(many > 0, few > 0)
        run_all(
            [gather_owners(args[at], outs[at], sems[at]) for at in range(many)]
            + [gather_ranks(args[at], outs[at], sems[at]) for at in range(many, many + few)]
        )

    blocks = list(by_owner) + list(by_rank)
    return call(
        kernel,
        number,
        blocks,
        [VMEM] * len(blocks),
        [shape((8 if at < many else 4,) + block.shape, block.dtype) for at, block in enumerate(blocks)],
        [HBM] * len(blocks),
        GATHER_OWNERS_SEMS * many + GATHER_RANKS_SEMS * few,
        name,
        16,
    )


def rank_sums(number, blocks, name):
    if not fast():
        return [lax.psum_scatter(block.astype(F32), "seq", scatter_dimension=0, tiled=False) for block in blocks]
    many = len(blocks)

    def kernel(*refs):
        groups = takes(refs, many, many, *[7] * many)
        greet(False, True)
        run_all(
            [
                scatter_ranks(groups[0][at], groups[1][at], *groups[2 + at][:4], groups[2 + at][4:])
                for at in range(many)
            ]
        )

    scratch = []
    for block in blocks:
        scratch += scatter_ranks_scratch(*block.shape[1:])
    return call(
        kernel,
        number,
        blocks,
        [HBM] * many,
        [shape(block.shape[1:], F32) for block in blocks],
        [VMEM] * many,
        scratch,
        name,
        16,
    )


def columns_product(left, right, out, first=0):
    count = left.shape[1] // 128

    def one(index, carry):
        at = pl.ds(pl.multiple_of(lax.rem(index + first, count) * 128, 128), 128)
        out[at] = low_dot(left[:, at], right[...], (0, 0)).astype(LOW)
        return carry

    lax.fori_loop(0, count, one, 0)


def sum_feed(part, pairs):
    many = len(pairs)

    def kernel(*refs):
        args, outs, scratch = takes(refs, 1 + 2 * many, 1 + many, 7)
        greet(False, True)

        def products():
            for at in range(many):
                columns_product(args[1 + 2 * at], args[2 + 2 * at], outs[1 + at])
                yield

        run_all([scatter_ranks(args[0], outs[0], *scratch[:4], scratch[4:]), products()])

    return call(
        kernel,
        4,
        (part,) + tuple(array for pair in pairs for array in pair),
        [HBM] + [VMEM] * (2 * many),
        [shape(part.shape[1:], F32)] + [shape((left.shape[1], right.shape[1]), LOW) for left, right in pairs],
        [VMEM] * (1 + many),
        scatter_ranks_scratch(*part.shape[1:]),
        "sum_feed",
        36,
    )


def row_cuts(rows, cuts):
    step = (rows // cuts + 15) // 16 * 16
    return [(start, min(step, rows - start)) for start in range(0, rows, step)]


def together(parts, first):
    parts = list(parts)
    for _ in range(first):
        for part in parts:
            next(part)
    yield
    while parts:
        for part in list(parts):
            try:
                next(part)
            except StopIteration:
                parts.remove(part)
        yield


def scatter_items(parts, outs, scratch, cuts):
    items, at = [], 0
    for part, out in zip(parts, outs):
        height = out.shape[1]
        for start, count in row_cuts(height, cuts):
            refs = scratch[at]

            def block(owner, part=part, start=start, count=count):
                if len(part.shape) == 3:
                    return part.at[owner, pl.ds(start, count)]
                return part.at[pl.ds(pl.multiple_of(owner * height + start, 16), count)]

            items.append(scatter_owners(block, out.at[:, pl.ds(start, count)], *refs[:5], refs[5:]))
            at += 1
    return [together(items, 4)]


def scatter_items_scratch(shapes, cuts):
    scratch = []
    for height, columns in shapes:
        for _, count in row_cuts(height, cuts):
            scratch += scatter_owners_scratch(count, columns)
    return scratch


def backward_attention(g_up, g_down, my_d_attn, mlp_part, qkv, w_out, logs, units):
    length = qkv.shape[0]
    heads = qkv.shape[1] // (3 * HD)
    span = heads * HD
    rows, width = my_d_attn.shape

    def kernel(*refs):
        groups = takes(refs, 7, 6, 6, 7, 3, *[14] * 6)
        args, outs, scratch, sum_scratch, token_sems = groups[:5]
        d_mixed, head_rows, d_head, d_keys, d_values, up_all = scratch
        greet(True, True)

        def attention():
            tokens = gather_ranks(args[2], outs[2], token_sems)
            next(tokens)
            yield
            for _ in tokens:
                pass
            w_rows = args[5][pl.ds(pl.multiple_of(lax.axis_index("seq") * span, 16), span)]
            for part in range(4):
                d_mixed[part * rows : (part + 1) * rows] = low_dot(outs[2][part], w_rows, (1, 1)).astype(LOW)
            yield from attend_heads_back(
                args[4], args[6], d_mixed, outs[4], head_rows, d_head, d_keys, d_values, heads
            )

        run_all(
            scatter_items(args[:2], (up_all, outs[1]), groups[5:], 3)
            + [attention(), scatter_ranks(args[3], outs[3], *sum_scratch[:4], sum_scratch[4:])]
        )
        owners = up_all.shape[2] // units
        outs[5][...] = jnp.zeros_like(outs[5])

        def assemble(at):
            for part in range(4):
                for owner in range(owners):
                    to = (owner * 4 + part) * units
                    outs[0][at, to : to + units] = up_all[part, at, owner * units : (owner + 1) * units]
            add_squares(outs[0][at], outs[5])

        by_rows(up_all.shape[1], assemble)

    return call(
        kernel,
        9,
        (g_up, g_down, my_d_attn, mlp_part, qkv, w_out, logs),
        [HBM, HBM, VMEM, HBM, VMEM, VMEM, VMEM],
        [
            shape((g_up.shape[1], 4 * g_up.shape[2]), LOW),
            shape((4,) + g_down.shape[1:], LOW),
            shape((4,) + my_d_attn.shape, LOW),
            shape(my_d_attn.shape, F32),
            shape(qkv.shape, LOW),
            shape((1, 4 * g_up.shape[2]), F32),
        ],
        [VMEM, HBM, VMEM, VMEM, VMEM, VMEM],
        [
            pltpu.VMEM((length, span), LOW),
            pltpu.VMEM((3, length, HD), LOW),
            pltpu.VMEM((length, HD), LOW),
            pltpu.VMEM((length, HD), F32),
            pltpu.VMEM((length, HD), F32),
            pltpu.VMEM((4,) + g_up.shape[1:], LOW),
        ]
        + scatter_ranks_scratch(rows, width)
        + GATHER_RANKS_SEMS
        + scatter_items_scratch([g_up.shape[1:], g_down.shape[1:]], 3),
        "backward_attention",
        50,
    )


def add_squares(values, box):
    values = values.astype(F32)
    box[...] += jnp.sum(values * values, axis=0, keepdims=True)


def backward_last(h_attn, d_qkv, mixed, d_part, d_tokens, tokens, scale, d_middle, news, second, modulation, cond_cut, time_slope):
    rows, width = second.shape
    span = d_part.shape[1]
    tok_rows = tokens.shape[0]
    wide = modulation.shape[0]

    def kernel(*refs):
        groups = takes(refs, 13, 9, 5, 12, 7, 7, *[14] * 4)
        args, outs, scratch, sems, sum_scratch = groups[:5]
        in_all, out_all, d_sum, edge, news_here, g_in, g_out = groups[5]
        squares, outs = outs[7:], outs[:7]
        products, args = args[:4], args[2:]
        greet(True, True)

        def condition():
            yield from scatter_ranks(args[2], d_sum, *sum_scratch[:4], sum_scratch[4:])
            edge[...] = jnp.zeros_like(edge)

            def one(at):
                value = args[3][at].astype(F32)
                norm, inverse = layer_norm(value)
                grad = d_sum[at]
                edge[0] += jnp.sum(grad.reshape(2, 8, width), axis=0)
                edge[1] += jnp.sum((grad * norm).reshape(2, 8, width), axis=0)
                outs[2][at] = args[5][at] + layer_norm_back(norm, inverse, grad * (1.0 + args[4][...]))

            by_rows(tok_rows, one)
            news_here[...] = args[6][...]
            line = jnp.concatenate(
                [jnp.sum(edge[0], axis=0, keepdims=True), jnp.sum(edge[1], axis=0, keepdims=True)], axis=1
            )
            at = 0
            while at * wide < 2 * width:
                end = min((at + 1) * wide, 2 * width)
                news_here[at, :, : end - at * wide] = line[:, at * wide : end]
                at += 1
            yield from condition_backward(news_here, *args[7:], outs[3:], scratch, sems)

        def gradients():
            columns_product(products[2], products[3], g_out, 5)
            yield
            columns_product(products[0], products[1], g_in, 5)
            yield from scatter_items((g_in, g_out), (in_all, out_all), groups[6:], 2)[0]

        run_all([condition(), gradients()])
        for box in squares:
            box[...] = jnp.zeros_like(box)

        def assemble(at):
            for part in range(4):
                for block in range(3):
                    to = (block * 4 + part) * span
                    outs[0][at, to : to + span] = in_all[part, at, block * span : (block + 1) * span]
                outs[1][at, part * span : (part + 1) * span] = out_all[part, at]
            add_squares(outs[0][at], squares[0])
            add_squares(outs[1][at], squares[1])

        by_rows(rows, assemble)

    return call(
        kernel,
        8,
        (h_attn, d_qkv, mixed, d_part, d_tokens, tokens, scale, d_middle, news, second, modulation, cond_cut, time_slope),
        [VMEM] * 4 + [HBM] + [VMEM] * 8,
        [
            shape((rows, 12 * span), LOW),
            shape((rows, 4 * span), LOW),
            shape(tokens.shape, F32),
            shape(news.shape, F32),
            shape((8, width), F32),
            shape((8, 8, rows), F32),
            shape((8, 1, wide), F32),
            shape((1, 12 * span), F32),
            shape((1, 4 * span), F32),
        ],
        [VMEM] * 9,
        [
            pltpu.VMEM((4,) + news.shape, F32),
            pltpu.VMEM(news.shape, F32),
            pltpu.VMEM((8, 8, rows), F32),
            pltpu.VMEM((8, 8, rows), F32),
            pltpu.VMEM((8, 8, rows), F32),
            DMA((3,)),
            DMA((4,)),
        ]
        + SWAP_SEMS * 5
        + scatter_ranks_scratch(tok_rows, width)
        + [
            pltpu.VMEM((4, rows, 3 * span), LOW),
            pltpu.VMEM((4, rows, span), LOW),
            pltpu.VMEM((tok_rows, width), F32),
            pltpu.VMEM((2, 8, width), F32),
            pltpu.VMEM(news.shape, F32),
            pltpu.VMEM((width, 3 * span), LOW),
            pltpu.VMEM((width, span), LOW),
        ]
        + scatter_items_scratch([(rows, 3 * span), (rows, span)], 2),
        "backward_last",
        52,
    )


def pick_weights(attend_in, attend_out, expand, rank, span, units):
    rows = attend_in.shape[0]
    owners = expand.shape[1] // (4 * units)
    if not fast():
        w_in = pick(attend_in.reshape(rows, 3, 4, span), rank, 2).astype(LOW).reshape(rows, 3 * span)
        w_up = pick(expand.reshape(rows, owners, 4, units), rank, 2).astype(LOW).reshape(rows, owners * units)
        return jnp.concatenate([w_in, mine(attend_out, 1, 4, rank).astype(LOW)], axis=1), w_up

    def kernel(in_ref, out_ref, up_ref, io, up):
        here = lax.axis_index("seq")
        for part in range(4):

            @pl.when(here == part)
            def _(part=part):
                def one(at):
                    for block in range(3):
                        start = (block * 4 + part) * span
                        io[at, block * span : (block + 1) * span] = in_ref[at, start : start + span].astype(LOW)
                    io[at, 3 * span :] = out_ref[at, part * span : (part + 1) * span].astype(LOW)
                    for owner in range(owners):
                        start = (owner * 4 + part) * units
                        up[at, owner * units : (owner + 1) * units] = up_ref[at, start : start + units].astype(LOW)

                by_rows(rows, one)

    return pl.pallas_call(
        kernel,
        out_shape=[shape((rows, 4 * span), LOW), shape((rows, owners * units), LOW)],
        in_specs=[VMEM] * 3,
        out_specs=[VMEM] * 2,
        compiler_params=pltpu.CompilerParams(vmem_limit_bytes=32 * 1024 * 1024),
        name="pick_weights",
    )(attend_in, attend_out, expand)


def sum_owners(number, value, name):
    if not fast():
        return lax.psum(value, "fsdp")

    def kernel(src, out, boxes, *sems):
        owner = lax.axis_index("fsdp")
        greet(True, False)
        sends = Sends()
        boxes[owner] = src[...]
        swap_start(sends, lambda to: src, boxes, *sems)
        swap_wait(boxes, sems[1])
        total = boxes[0]
        for of in range(1, 8):
            total = total + boxes[of]
        out[...] = total
        sends.finish()

    block = jnp.full((8, 128), value, F32)
    total = call(
        kernel, number, (block,), [VMEM], shape((8, 128), F32), VMEM, [pltpu.VMEM((8, 8, 128), F32)] + SWAP_SEMS, name, 4
    )
    return total[0, 0]


def attend(query, keys, values):
    score_scale = 1.0 / math.sqrt(keys.shape[-1])
    scores = mixed_dot("qhd,khd->hqk", query, keys) * score_scale
    top = jnp.max(scores, axis=-1, keepdims=True)
    expo = jnp.exp(scores - top)
    total = jnp.sum(expo, axis=-1, keepdims=True)
    probs = (expo / total).astype(LOW)
    mixed = mixed_dot("hqk,khd->qhd", probs, values)
    return mixed.astype(LOW), (top + jnp.log(total))[..., 0]


def attend_back(query, keys, values, d_mixed, log_total):
    length, heads_here, head_dim = query.shape
    block = min(512, length)
    count = length // block
    score_scale = 1.0 / math.sqrt(head_dim)

    def back_block(carry, pieces):
        d_keys, d_values = carry
        query_block, d_block, log_block = pieces
        scores = mixed_dot("qhd,khd->hqk", query_block, keys) * score_scale
        probs = jnp.exp(scores - log_block[..., None])
        d_probs = mixed_dot("qhd,khd->hqk", d_block, values)
        delta = jnp.sum(probs * d_probs, axis=-1, keepdims=True)
        d_scores = (probs * (d_probs - delta)).astype(LOW)
        d_query = mixed_dot("hqk,khd->qhd", d_scores, keys) * score_scale
        d_keys = d_keys + mixed_dot("hqk,qhd->khd", d_scores, query_block) * score_scale
        d_values = d_values + mixed_dot("hqk,qhd->khd", probs.astype(LOW), d_block)
        return ((d_keys, d_values), d_query)

    empty = jnp.zeros((length, heads_here, head_dim), jnp.float32)
    blocked = (count, block, heads_here, head_dim)
    logs = log_total.reshape(heads_here, count, block).transpose(1, 0, 2)
    (d_keys, d_values), d_query = lax.scan(
        back_block, (empty, empty), (query.reshape(blocked), d_mixed.reshape(blocked), logs)
    )
    flat = (length, heads_here * head_dim)
    return jnp.concatenate(
        [d_query.reshape(flat), d_keys.reshape(flat), d_values.reshape(flat)], axis=1
    ).astype(LOW)


def adam_step(weight, moment, square, gradient, factor):
    clipped = gradient * factor
    moment_next = beta_one * moment + (1.0 - beta_one) * clipped
    square_next = beta_two * square + (1.0 - beta_two) * clipped * clipped
    moment_hat = moment_next / (1.0 - beta_one**STEP)
    square_hat = square_next / (1.0 - beta_two**STEP)
    master = weight - learn_rate * (
        moment_hat / (jnp.sqrt(square_hat) + adam_eps) + weight_decay * weight
    )
    return (master, moment_next, square_next)


def condition_start(latent_tokens, w_io, biases, timesteps, labels, time_first, time_second, class_table, modulation):
    owners, owner = lax.axis_size("fsdp"), lax.axis_index("fsdp")
    share = biases.shape[0]
    width = time_first.shape[1]
    first, second = time_first.astype(LOW), time_second.astype(LOW)
    table, modulation_low = class_table.astype(LOW), modulation.astype(LOW)
    units = first.shape[0]
    bias_low = biases.astype(LOW).astype(F32)
    features = time_features(timesteps).astype(LOW)
    if fast():
        note = jnp.concatenate(
            [
                jnp.broadcast_to(bias_low, (owners, share)),
                features.astype(F32).reshape(owners, units),
                jnp.broadcast_to(labels.astype(F32), (owners, 1)),
                jnp.zeros((owners, 127 - units), F32),
            ],
            axis=1,
        )[:, None]
        w_io_all, tokens, notes, act, slope, cond_cut, cond, mod = forward_first(
            w_io, latent_tokens, note, first, second, table.T, modulation_low.T
        )
        notes = notes[:, 0]
        all_bias = notes[:, :share].reshape(owners * share)
        my_features = notes[:, share : share + units]
        all_labels = notes[:, share + units]
        mod_values = mod.reshape(owners * mod.shape[2])
        state = (first, second, modulation_low, my_features, all_labels, act, slope, cond_cut, cond)
        return w_io_all, tokens, all_bias, mod_values, state
    w_io_all = lax.all_gather(w_io, "fsdp", axis=0)
    tokens = lax.all_gather(latent_tokens, "seq", axis=0)
    note = jnp.concatenate([bias_low, features[0].astype(F32), labels.astype(F32)])
    notes = lax.all_gather(note, "fsdp", axis=0)
    all_bias = notes[:, :share].reshape(owners * share)
    my_features = mine(notes[:, share:-1], 1, owners, owner)
    all_labels = notes[:, -1]
    hidden_time = lax.psum(mixed_dot("bf,fd->bd", my_features.astype(LOW), first), "fsdp") + all_bias[:width]
    act, slope = silu_parts(mine(hidden_time, 1, owners, owner))
    act = act.astype(LOW)
    onehot = (all_labels[:, None] == jnp.arange(NCLS, dtype=F32)[None, :]).astype(LOW)
    cond_part = mixed_dot("bd,de->be", act, second)
    class_part = mixed_dot("bc,cd->bd", onehot, table)
    class_wide = lax.dynamic_update_slice(jnp.zeros_like(cond_part), class_part, (0, owner * class_part.shape[1]))
    cond = lax.psum(cond_part + class_wide, "fsdp") + all_bias[width : 2 * width]
    mod_part = mixed_dot("bd,de->be", silu_parts(cond)[0].astype(LOW), modulation_low)
    mod_values = pick(lax.all_gather(mod_part, "fsdp", axis=0), owner, 1).reshape(owners * mod_part.shape[1])
    state = (first, second, modulation_low, my_features, all_labels, act.astype(F32), slope, None, cond)
    return w_io_all, tokens, all_bias, mod_values, state


def owner_sums(blocks):
    summed = [lax.psum_scatter(block.astype(F32), "fsdp", scatter_dimension=0, tiled=False) for block in blocks]
    return [lax.all_gather(block.astype(LOW), "seq", axis=0) for block in summed]


def condition_end(state, h_attn, d_qkv, mixed, d_part, d_tokens, tokens, scale1, d_middle, d_mod_rest, tail, share):
    first, second, modulation_low, my_features, all_labels, act, slope, cond_cut, cond = state
    owners, owner, rank = lax.axis_size("fsdp"), lax.axis_index("fsdp"), lax.axis_index("seq")
    wide, width = modulation_low.shape[1], cond.shape[1]
    blank = jnp.zeros((2 * width,), F32)
    if fast():
        pad = -wide % 128
        tails = jnp.concatenate([jnp.zeros((owners * share - tail.shape[0],), F32), tail]).reshape(owners, share)
        news = jnp.concatenate(
            [jnp.concatenate([blank, d_mod_rest]).reshape(owners, wide), jnp.zeros((owners, pad), F32), tails], axis=1
        )[:, None]
        grad_in, grad_out, input_gradient, by_latent, d_cond, d_hid, sums, *squares = backward_last(
            h_attn, d_qkv, mixed, d_part, d_tokens, tokens, scale1, d_middle, news, second, modulation_low.T, cond_cut, slope
        )
        d_mod = by_latent[:, 0, :wide]
        my_tail = jnp.sum(by_latent[:, 0, wide + pad :], axis=0)
        d_hidden = d_hid.transpose(1, 0, 2).reshape(owners, width)
        front = jnp.concatenate([jnp.sum(d_hidden, axis=0), jnp.sum(d_cond, axis=0), sums.reshape(owners * wide)])
        count = front.shape[0] // share
        grad_bias = jnp.where(
            owner < count, pick(front.reshape(count, share), jnp.minimum(owner, count - 1)), my_tail
        )
    else:
        (d_hattn,) = rank_sums(6, [d_tokens], "sums")
        norm, inverse = layer_norm(tokens.astype(F32))
        input_gradient = d_middle + layer_norm_back(norm, inverse, d_hattn * (1.0 + scale1))
        my_d_mod = jnp.concatenate([jnp.sum(d_hattn, axis=0), jnp.sum(d_hattn * norm, axis=0), d_mod_rest])
        by_owner = lambda block: block.astype(LOW).reshape((owners, -1) + block.shape[1:])
        grad_in, grad_out = owner_sums(
            [by_owner(mixed_dot("td,te->de", h_attn, d_qkv)), by_owner(mixed_dot("td,te->de", mixed, d_part))]
        )
        rows, span = grad_out.shape[1], grad_out.shape[2]
        grad_in = grad_in.reshape(4, rows, 3, span).transpose(1, 2, 0, 3).reshape(rows, 12 * span)
        grad_out = grad_out.transpose(1, 0, 2).reshape(rows, 4 * span)
        squares = [grad.astype(F32) * grad.astype(F32) for grad in (grad_in, grad_out)]
        all_d_mod = lax.all_gather(lax.psum(my_d_mod, "seq"), "fsdp", axis=0)
        d_mod = mine(all_d_mod, 1, owners, owner)
        part = high_dot(d_mod, modulation_low.astype(F32).T)
        d_cond = lax.psum(part, "fsdp") * silu_parts(cond)[1]
        d_time = high_dot(d_cond, second.astype(F32).T) * slope
        d_hidden = lax.all_gather(d_time, "fsdp", axis=0).transpose(1, 0, 2).reshape(owners, width)
        tail = lax.psum(tail, ("seq", "fsdp"))
        all_bias = jnp.concatenate(
            [jnp.sum(d_hidden, axis=0), jnp.sum(d_cond, axis=0), jnp.sum(all_d_mod, axis=0), tail]
        )
        grad_bias = mine(all_bias, 0, owners, owner)
    onehot = (all_labels[:, None] == jnp.arange(NCLS, dtype=F32)[None, :]).astype(F32)
    cond_act = silu_parts(cond)[0].astype(LOW).astype(F32)
    grad_mod = high_dot(cond_act.T, d_mod)
    grad_class = high_dot(onehot.T, mine(d_cond, 1, owners, owner))
    grad_second = high_dot(act.T, d_cond)
    grad_first = high_dot(my_features.T, d_hidden)
    condition_gradient = lax.dynamic_slice_in_dim(d_cond, owner, 1, 0)
    return grad_in, grad_out, squares, input_gradient, (grad_first, grad_second, grad_class, grad_mod), grad_bias, condition_gradient


def per_device(latents, timesteps, labels, upstream, *state):
    params, moments, squares = state[:9], state[9:18], state[18:]
    time_first, time_second, class_table, modulation, attend_in, attend_out, expand, contract, biases = params
    lat_dev, tok_rows, width = latents.shape
    assert lat_dev == 1
    hidden = expand.shape[1]
    ranks = lax.axis_size("seq")
    owners = lax.axis_size("fsdp")
    rank = lax.axis_index("seq")
    heads_here = H // ranks
    span = heads_here * HD
    length = ranks * tok_rows
    rows = width // owners
    unit = hidden // (owners * ranks)
    hid_here = owners * unit

    my_io, my_up = pick_weights(attend_in, attend_out, expand, rank, span, unit)
    my_down = mine(contract, 0, ranks, rank).astype(LOW)
    w_io, tokens, all_bias, mod_values, kept = condition_start(
        latents[0], my_io, biases, timesteps, labels, time_first, time_second, class_table, modulation
    )
    w_io = w_io.reshape(width, 4 * span)
    w_in = w_io[:, : 3 * span]
    inputs_low = tokens.reshape(length, width)

    b_t1, b_t2, b_mod, b_q, b_v, b_out, b_up, b_down = split_biases(all_bias, width, hidden)
    mod_values = (mod_values + b_mod).reshape(6, 1, width)
    shift1, scale1, gate1, shift2, scale2, gate2 = [mod_values[index] for index in range(6)]

    inputs = inputs_low.astype(F32)
    norm_one, _ = layer_norm(inputs)
    h_attn = (norm_one * (1.0 + scale1) + shift1).astype(LOW)
    my_b_q, my_b_v = mine(b_q, 0, ranks, rank), mine(b_v, 0, ranks, rank)
    qkv_bias = jnp.concatenate([my_b_q, jnp.zeros_like(my_b_q), my_b_v])
    qkv = (mixed_dot("td,de->te", h_attn, w_in) + qkv_bias).astype(LOW)
    head_shape = (length, heads_here, HD)
    if fast():
        w_up, w_down, d_out_low, w_out, mixed, logs = forward_attention(
            qkv, my_up, my_down, upstream[0], w_io
        )
    else:
        query, keys, values = [qkv[:, part * span : (part + 1) * span].reshape(head_shape) for part in range(3)]
        mixed_heads, logs = attend(query, keys, values)
        w_up, w_down, d_out_low, w_out, mixed = gathers(
            2, [my_up, my_down], [upstream[0], w_io[:, 3 * span :], mixed_heads.reshape(length, span)], "gathers"
        )
        w_out = w_out.transpose(1, 0, 2).reshape(width, width)
        mixed = mixed.transpose(1, 0, 2).reshape(length, width)
    w_up, w_down = w_up.reshape(width, hid_here), w_down.reshape(hid_here, width)
    d_out_low = d_out_low.reshape(length, width)
    attn_out = mixed_dot("td,de->te", mixed, w_out) + b_out
    middle = inputs + gate1 * attn_out
    norm_two, inverse_two = layer_norm(middle)
    h_mlp = (norm_two * (1.0 + scale2) + shift2).astype(LOW)

    my_b_up = pick(b_up.reshape(owners, ranks, unit), rank, 1).reshape(hid_here)
    pre_act = mixed_dot("td,df->tf", h_mlp, w_up) + my_b_up
    act_f, gelu_pull = jax.vjp(partial(jax.nn.gelu, approximate=True), pre_act)
    act = act_f.astype(LOW)
    by_rank = (ranks, tok_rows, width)
    by_owner = lambda block: block.astype(LOW).reshape((owners, -1) + block.shape[1:])
    mlp_part = mixed_dot("tf,fd->td", act, w_down).astype(LOW).reshape(by_rank)
    d_out = d_out_low.astype(F32)
    d_mlp = (d_out * gate2).astype(LOW)
    d_act = mixed_dot("td,fd->tf", d_mlp, w_down)
    d_pre = gelu_pull(d_act)[0].astype(LOW)
    d_hmlp_part = mixed_dot("tf,df->td", d_pre, w_up).astype(LOW).reshape(by_rank)
    if fast():
        d_hmlp, g_down, g_up = sum_feed(d_hmlp_part, [(act, d_mlp), (h_mlp, d_pre)])
        g_down, g_up = by_owner(g_down), by_owner(g_up)
    else:
        (d_hmlp,) = rank_sums(4, [d_hmlp_part], "sums")
        g_down = by_owner(mixed_dot("tf,td->fd", act, d_mlp))
        g_up = by_owner(mixed_dot("td,tf->df", h_mlp, d_pre))
    gb_up = jnp.sum(d_pre.astype(F32), axis=0)
    gb_down = jnp.sum(d_mlp.astype(F32), axis=0)

    own = lambda array: mine(array, 0, ranks, rank)
    my_attn_out, my_middle, my_norm_two, my_inverse_two = own(attn_out), own(middle), own(norm_two), own(inverse_two)
    my_d_out = upstream[0].astype(F32)
    d_shift2 = jnp.sum(d_hmlp, axis=0)
    d_scale2 = jnp.sum(d_hmlp * my_norm_two, axis=0)
    d_middle = my_d_out + layer_norm_back(my_norm_two, my_inverse_two, d_hmlp * (1.0 + scale2))
    d_gate1 = jnp.sum(d_middle * my_attn_out, axis=0)
    my_d_attn = (d_middle * gate1).astype(LOW)
    if fast():
        grad_up, grad_down, d_attn, mlp_sum, d_qkv, up_squares = backward_attention(
            g_up, g_down, my_d_attn, mlp_part, qkv, w_out, logs, unit
        )
        d_attn = d_attn.reshape(length, width)
    else:
        (mlp_sum,) = rank_sums(5, [mlp_part], "sums")
        (d_attn,) = gathers(5, [], [my_d_attn], "gathers")
        d_attn = d_attn.reshape(length, width)
        d_mixed = mixed_dot("te,de->td", d_attn, mine(w_out, 0, ranks, rank)).astype(LOW)
        d_qkv = attend_back(query, keys, values, d_mixed.reshape(head_shape), logs)
        grad_up, grad_down = owner_sums([g_up, g_down])
        grad_up = grad_up.reshape(ranks, rows, owners, unit).transpose(1, 2, 0, 3).reshape(rows, hidden)
        up_squares = grad_up.astype(F32) * grad_up.astype(F32)
    mlp_out = mlp_sum + b_down
    output = (my_middle + gate2 * mlp_out).astype(LOW)
    d_gate2 = jnp.sum(my_d_out * mlp_out, axis=0)
    d_part = mine(d_attn, 1, ranks, rank)
    d_hattn_part = mixed_dot("te,de->td", d_qkv, w_in).astype(LOW).reshape(by_rank)
    d_mod_rest = jnp.concatenate([d_gate1, d_shift2, d_scale2, d_gate2])
    gb_qv = jnp.sum(d_qkv.astype(F32), axis=0)
    wide = lambda part, size: lax.dynamic_update_slice(jnp.zeros((size,), F32), part, (rank * part.shape[0],))
    gb_up_wide = lax.dynamic_update_slice(
        jnp.zeros((owners, ranks, unit), F32), gb_up.reshape(owners, 1, unit), (0, rank, 0)
    ).reshape(hidden)
    gb_tail = jnp.concatenate(
        [
            wide(gb_qv[:span], width),
            wide(gb_qv[2 * span :], width),
            jnp.sum(my_d_attn.astype(F32), axis=0),
            gb_up_wide,
            jnp.where(rank == 0, gb_down, 0.0),
        ]
    )
    grad_in, grad_out, squares_io, input_gradient, small_grads, grad_bias, condition_gradient = condition_end(
        kept, h_attn, d_qkv, mixed, d_part, d_hattn_part, latents[0], scale1, d_middle, d_mod_rest, gb_tail, biases.shape[0]
    )
    grad_in, grad_out, grad_up, grad_down = [grad.astype(F32) for grad in (grad_in, grad_out, grad_up, grad_down)]
    grad_down = grad_down.reshape(contract.shape)
    gradients = small_grads + (grad_in, grad_out, grad_up, grad_down, grad_bias)
    local_sum = sum(jnp.sum(gradient * gradient) for gradient in small_grads + (grad_down, grad_bias))
    local_sum = local_sum + sum(jnp.sum(box) for box in [up_squares] + list(squares_io))
    norm_before = jnp.sqrt(sum_owners(7, local_sum, "sum_squares"))
    factor = clip_limit / jnp.maximum(norm_before, clip_limit)
    results = [
        adam_step(params[index], moments[index], squares[index], gradients[index], factor)
        for index in range(9)
    ]
    return (
        (output[None], input_gradient[None], condition_gradient, norm_before)
        + gradients
        + tuple(result[0] for result in results)
        + tuple(result[1] for result in results)
        + tuple(result[2] for result in results)
    )


def solution(mesh):
    tokens = P("fsdp", "seq", None)
    rows, columns = P("fsdp", None), P(None, "fsdp")
    weights = (rows, rows, columns, columns, rows, rows, rows, rows, P("fsdp"))
    return jax.shard_map(
        per_device,
        mesh=mesh,
        in_specs=(tokens, P("fsdp"), P("fsdp"), tokens) + weights * 3,
        out_specs=(tokens, tokens, rows, P()) + weights * 4,
        check_vma=False,
    )
```

```python
from functools import partial
import math

import jax
import jax.numpy as jnp
from jax import lax
from jax.experimental import pallas as pl
from jax.experimental.pallas import tpu as pltpu
from jax.sharding import PartitionSpec as P

H = 16
HD = 72
FREQ = 256
NCLS = 1000
STEP = 10


HIGH = lax.Precision.HIGHEST
LOW = jnp.bfloat16
norm_eps = 1e-06
beta_one = 0.9
beta_two = 0.999
learn_rate = 0.04
weight_decay = 0.01
adam_eps = 1e-08
clip_limit = 1.0


def layer_norm(value):
    centre = value - jnp.mean(value, axis=-1, keepdims=True)
    spread = jnp.mean(centre * centre, axis=-1, keepdims=True)
    inverse = lax.rsqrt(spread + norm_eps)
    return centre * inverse, inverse


def layer_norm_back(norm, inverse, grad):
    first = jnp.mean(grad, axis=-1, keepdims=True)
    second = jnp.mean(grad * norm, axis=-1, keepdims=True)
    return inverse * (grad - first - norm * second)


def silu_parts(value):
    gate = jax.nn.sigmoid(value)
    return value * gate, gate * (1.0 + value * (1.0 - gate))


def time_features(timesteps):
    half = FREQ // 2
    freqs = jnp.exp(-math.log(10000.0) * jnp.arange(half, dtype=jnp.float32) / half)
    angles = timesteps.astype(jnp.float32)[:, None] * freqs[None, :]
    return jnp.concatenate([jnp.cos(angles), jnp.sin(angles)], axis=-1)


def split_biases(biases, width, hidden):
    widths = [width, width, 6 * width, width, width, width, hidden, width]
    pieces = []
    start = 0
    for length in widths:
        pieces.append(biases[start : start + length])
        start = start + length
    return pieces


def high_dot(left, right):
    return jnp.dot(left, right, precision=HIGH, preferred_element_type=jnp.float32)


def mixed_dot(form, left, right):
    return jnp.einsum(form, left, right, preferred_element_type=jnp.float32)


def pick(array, index, axis=0):
    return lax.dynamic_index_in_dim(array, index, axis, keepdims=False)


def mine(array, axis, parts, index):
    size = array.shape[axis] // parts
    return lax.dynamic_slice_in_dim(array, index * size, size, axis)


HBM = pl.BlockSpec(memory_space=pl.ANY)
VMEM = pl.BlockSpec(memory_space=pltpu.VMEM)
DMA = pltpu.SemaphoreType.DMA
F32 = jnp.float32


def fast():
    return lax.axis_size("fsdp") == 8 and lax.axis_size("seq") == 4


def places():
    owner, rank = lax.axis_index("fsdp"), lax.axis_index("seq")
    return owner, rank, lax.div(owner, 2), lax.rem(owner, 2), lax.div(rank, 2), lax.rem(rank, 2)


def remote(src, dst, sent, landed, **where):
    return pltpu.make_async_remote_copy(
        src_ref=src, dst_ref=dst, send_sem=sent, recv_sem=landed, device_id=where, device_id_type=pl.DeviceIdType.MESH
    )


def arrived(dst, landed, **where):
    remote(dst, dst, landed, landed, **where).wait_recv()


def greet(over_owners, over_ranks):
    owner, rank, *_ = places()
    barrier = pltpu.get_barrier_semaphore()
    count = 0
    if over_owners:
        for step in range(1, 8):
            pl.semaphore_signal(
                barrier, inc=1, device_id={"fsdp": lax.rem(owner + step, 8)}, device_id_type=pl.DeviceIdType.MESH
            )
        count += 7
    if over_ranks:
        for step in range(1, 4):
            pl.semaphore_signal(
                barrier, inc=1, device_id={"seq": lax.rem(rank + step, 4)}, device_id_type=pl.DeviceIdType.MESH
            )
        count += 3
    pl.semaphore_wait(barrier, count)


def run_all(parts):
    parts = list(parts)
    while parts:
        for part in list(parts):
            try:
                next(part)
            except StopIteration:
                parts.remove(part)


class Sends:
    def __init__(self):
        self.live = []

    def start(self, copy, when=None):
        self.live.append((copy, when))
        if when is None:
            copy.start()
        else:
            pl.when(when)(copy.start)

    def finish(self):
        for copy, when in self.live:
            wait = copy.wait_send if hasattr(copy, "wait_send") else copy.wait
            if when is None:
                wait()
            else:
                pl.when(when)(wait)


def gather_owners(src, out, sems):
    own_sem, sent, landed = sems
    owner, rank, z, y, x, core = places()
    mate = owner + 1 - 2 * y
    sends = Sends()
    local = pltpu.make_async_copy(src, out.at[owner], own_sem)
    local.start()
    sends.start(remote(src, out.at[owner], sent.at[0, 0], landed.at[owner], fsdp=owner + 2), z < 3)
    sends.start(remote(src, out.at[owner], sent.at[0, 1], landed.at[owner], fsdp=owner - 2), z > 0)
    sends.start(remote(src, out.at[owner], sent.at[0, 2], landed.at[owner], fsdp=mate))
    yield
    for far in (1, 2, 3):
        for sign in (-1, 1):
            block = owner + sign * 2 * far
            here = (z >= far) if sign < 0 else (z + far <= 3)
            on = (z < 3) if sign < 0 else (z > 0)
            at = far if sign < 0 else 3 + far
            pl.when(here)(lambda: arrived(out.at[block], landed.at[block], fsdp=mate))
            sends.start(
                remote(out.at[block], out.at[block], sent.at[at, 0], landed.at[block], fsdp=owner - sign * 2), here & on
            )
            sends.start(remote(out.at[block], out.at[block], sent.at[at, 2], landed.at[block], fsdp=mate), here)
        yield
    for step in range(4):
        block = step * 2 + 1 - y
        arrived(out.at[block], landed.at[block], fsdp=mate)
    local.wait()
    sends.finish()


GATHER_OWNERS_SEMS = [DMA(()), DMA((7, 3)), DMA((8,))]


def gather_ranks(src, out, sems, local_copy=True):
    own_sem, sent, landed = sems
    owner, rank, z, y, x, core = places()
    mate, across, last = x * 2 + 1 - core, (1 - x) * 2 + core, (1 - x) * 2 + 1 - core
    sends = Sends()
    local = None
    if local_copy:
        local = pltpu.make_async_copy(src, out.at[rank], own_sem)
        local.start()
    sends.start(remote(src, out.at[rank], sent.at[0], landed.at[rank], seq=across))
    sends.start(remote(src, out.at[rank], sent.at[1], landed.at[rank], seq=mate))
    yield
    yield
    arrived(out.at[across], landed.at[across], seq=across)
    sends.start(remote(out.at[across], out.at[across], sent.at[2], landed.at[across], seq=mate))
    yield
    arrived(out.at[mate], landed.at[mate], seq=mate)
    arrived(out.at[last], landed.at[last], seq=mate)
    if local is not None:
        local.wait()
    sends.finish()


GATHER_RANKS_SEMS = [DMA(()), DMA((3,)), DMA((4,))]


def by_rows(count, body, step=16):
    def one(index, carry):
        body(pl.ds(pl.multiple_of(index * step, step), step))
        return carry

    lax.fori_loop(0, count // step, one, 0)


def scatter_ranks(parts, out, own, mail, leave, enter, sems):
    own_sem, sent, landed = sems
    owner, rank, z, y, x, core = places()
    mate, across = x * 2 + 1 - core, (1 - x) * 2 + core
    sends = Sends()
    loads = []
    for step in (1, 0):
        to = lax.rem(x + step, 2)
        loads.append(pltpu.make_async_copy(parts.at[to * 2 + core], own.at[step], own_sem.at[step]))
        loads[-1].start()
        sends.start(remote(parts.at[to * 2 + 1 - core], mail.at[step], sent.at[step], landed.at[step], seq=mate))
    yield
    loads[0].wait()
    arrived(mail.at[1], landed.at[1], seq=mate)

    def first(rows):
        leave[rows] = (own[1, rows].astype(F32) + mail[1, rows].astype(F32)).astype(LOW)

    by_rows(out.shape[0], first)
    sends.start(remote(leave, enter, sent.at[2], landed.at[2], seq=across))
    yield
    loads[1].wait()
    arrived(mail.at[0], landed.at[0], seq=mate)
    yield
    arrived(enter, landed.at[2], seq=across)

    def last(rows):
        out[rows] = own[0, rows].astype(F32) + mail[0, rows].astype(F32) + enter[rows].astype(F32)

    by_rows(out.shape[0], last)
    sends.finish()


def scatter_ranks_scratch(rows, columns):
    return [
        pltpu.VMEM((2, rows, columns), LOW),
        pltpu.VMEM((2, rows, columns), LOW),
        pltpu.VMEM((rows, columns), LOW),
        pltpu.VMEM((rows, columns), LOW),
        DMA((2,)),
        DMA((3,)),
        DMA((3,)),
    ]


def scatter_owners(parts, out, own, mail, rise, fall, leave, sems):
    own_sem, y_sent, y_landed, z_sent, up_landed, down_landed = sems[:6]
    owner, rank, z, y, x, core = places()
    mate = owner + 1 - 2 * y
    rows_here = own.shape[1]
    sends = Sends()
    loads = {}
    for to in (3, 0, 2, 1):
        sends.start(remote(parts(to * 2 + 1 - y), mail.at[to], y_sent.at[to], y_landed.at[to], fsdp=mate))
        loads[to] = pltpu.make_async_copy(parts(to * 2 + y), own.at[to], own_sem.at[to])
        loads[to].start()
        yield
    for to, up in ((3, True), (0, False), (2, True), (1, False), (1, True), (2, False)):
        here = (z < to) if up else (z > to)
        more = (z > 0) if up else (z < 3)
        box, box_landed = (rise, up_landed) if up else (fall, down_landed)

        def total(to=to, more=more, box=box, box_landed=box_landed):
            loads[to].wait()
            arrived(mail.at[to], y_landed.at[to], fsdp=mate)

            def start(rows):
                leave[to, rows] = (own[to, rows].astype(F32) + mail[to, rows].astype(F32)).astype(LOW)

            def add(rows):
                leave[to, rows] = (
                    own[to, rows].astype(F32) + mail[to, rows].astype(F32) + box[to, rows].astype(F32)
                ).astype(LOW)

            @pl.when(more)
            def _():
                arrived(box.at[to], box_landed.at[to], fsdp=mate)
                by_rows(rows_here, add)

            @pl.when(jnp.logical_not(more))
            def _():
                by_rows(rows_here, start)

        pl.when(here)(total)
        sends.start(
            remote(
                leave.at[to], box.at[to], z_sent.at[to], box_landed.at[to], fsdp=owner + 2 if up else owner - 2
            ),
            here,
        )
        yield
    for to in range(4):
        at_home = z == to

        @pl.when(at_home)
        def _(to=to):
            loads[to].wait()
            arrived(mail.at[to], y_landed.at[to], fsdp=mate)
            if to > 0:
                arrived(rise.at[to], up_landed.at[to], fsdp=mate)
            if to < 3:
                arrived(fall.at[to], down_landed.at[to], fsdp=mate)

            def end(rows):
                value = own[to, rows].astype(F32) + mail[to, rows].astype(F32)
                if to > 0:
                    value = value + rise[to, rows].astype(F32)
                if to < 3:
                    value = value + fall[to, rows].astype(F32)
                leave[to, rows] = value.astype(LOW)

            by_rows(rows_here, end)

    yield from gather_ranks(leave.at[z], out, sems[6:])
    sends.finish()


def scatter_owners_scratch(rows, columns):
    return [pltpu.VMEM((4, rows, columns), LOW)] * 5 + [DMA((4,))] * 6 + GATHER_RANKS_SEMS


def swap_start(sends, src_of, dst, sent, landed):
    owner = lax.axis_index("fsdp")
    for step in range(1, 8):
        to = lax.rem(owner + step, 8)
        sends.start(remote(src_of(to), dst.at[owner], sent.at[step - 1], landed.at[owner], fsdp=to))


def swap_wait(dst, landed):
    owner = lax.axis_index("fsdp")
    for step in range(1, 8):
        of = lax.rem(owner + step, 8)
        arrived(dst.at[of], landed.at[of], fsdp=of)


SWAP_SEMS = [DMA((7,)), DMA((8,))]


def low_dot(left, right, contract):
    return lax.dot_general(left, right, ((contract[:1], contract[1:]), ((), ())), preferred_element_type=F32)


def fine_dot(left, right, contract):
    high = left.astype(LOW)
    rest = left - high.astype(F32)
    return low_dot(high, right, contract) + low_dot(rest.astype(LOW), right, contract)


def stack_rows(ref):
    return jnp.concatenate([ref[index] for index in range(8)], axis=0)


def condition_forward(note, first, second, table, modulation, outs, scratch, sems):
    notes, act_out, slope_out, cond_cut, cond_out, mod = outs
    send_cut, hid_in, cond_in, bias_cut, mod_cut = scratch
    owner = lax.axis_index("fsdp")
    cut = second.shape[0]
    share = note.shape[2] - 128
    sends = Sends()
    notes[owner] = note[owner]
    swap_start(sends, lambda to: note.at[to], notes, *sems[0:2])
    yield
    swap_wait(notes, sems[1])
    rows = stack_rows(notes)
    feats = rows[:, share : share + first.shape[0]].astype(LOW)
    label = rows[:, share + first.shape[0] : share + first.shape[0] + 1]
    hidden = low_dot(feats, first[...], (1, 0))
    for to in range(8):
        send_cut[0, to] = hidden[:, to * cut : (to + 1) * cut]
        bias_cut[0, to] = rows[0:1, to * cut : (to + 1) * cut]
        bias_cut[1, to] = rows[0:1, (8 + to) * cut : (9 + to) * cut]
    hid_in[owner] = send_cut[0, owner]
    swap_start(sends, lambda to: send_cut.at[0, to], hid_in, *sems[2:4])
    yield
    classes = lax.broadcasted_iota(jnp.int32, (8, table.shape[1]), 1).astype(F32)
    onehot = (label == classes).astype(F32).astype(LOW)
    from_class = low_dot(onehot, table[...], (1, 1))
    swap_wait(hid_in, sems[3])
    hidden_cut = bias_cut[0, owner] + jnp.zeros((8, cut), F32)
    for of in range(8):
        hidden_cut = hidden_cut + hid_in[of]
    act, slope = silu_parts(hidden_cut)
    act = act.astype(LOW)
    act_out[...] = act.astype(F32)
    slope_out[...] = slope
    part = low_dot(act, second[...], (1, 0))
    for to in range(8):
        send_cut[1, to] = part[:, to * cut : (to + 1) * cut]
    cond_in[owner] = send_cut[1, owner]
    swap_start(sends, lambda to: send_cut.at[1, to], cond_in, *sems[4:6])
    yield
    swap_wait(cond_in, sems[5])
    mine_cond = bias_cut[1, owner] + from_class
    for of in range(8):
        mine_cond = mine_cond + cond_in[of]
    cond_cut[owner] = mine_cond
    swap_start(sends, lambda to: cond_cut.at[owner], cond_cut, *sems[6:8])
    yield
    swap_wait(cond_cut, sems[7])
    for of in range(8):
        cond_out[:, of * cut : (of + 1) * cut] = cond_cut[of]
    cond_act = silu_parts(cond_out[...])[0].astype(LOW)
    values = low_dot(cond_act, modulation[...], (1, 1))
    for to in range(8):
        mod_cut[to] = values[to : to + 1]
    mod[owner] = mod_cut[owner]
    swap_start(sends, lambda to: mod_cut.at[to], mod, *sems[8:10])
    yield
    swap_wait(mod, sems[9])
    sends.finish()


def condition_backward(news, second, modulation, cond_cut, time_slope, outs, scratch, sems):
    by_latent, d_cond_out, d_hid_cut, sums = outs
    rank_news, owner_news, d_cut, d_in, d_cond_cut = scratch
    owner, rank, *_ = places()
    cut = second.shape[0]
    wide = modulation.shape[0]
    sends = Sends()
    for step in range(1, 4):
        to = lax.rem(rank + step, 4)
        sends.start(remote(news, rank_news.at[rank], sems[0].at[step - 1], sems[1].at[rank], seq=to))
    yield
    for step in range(1, 4):
        of = lax.rem(rank + step, 4)
        arrived(rank_news.at[of], sems[1].at[of], seq=of)
    rank_news[rank] = news[...]
    for to in range(8):
        owner_news[to] = rank_news[0, to] + rank_news[1, to] + rank_news[2, to] + rank_news[3, to]
    by_latent[owner] = owner_news[owner]
    swap_start(sends, lambda to: owner_news.at[to], by_latent, *sems[2:4])
    yield
    swap_wait(by_latent, sems[3])
    d_mod = stack_rows(by_latent)[:, :wide]
    part = fine_dot(d_mod, modulation[...], (1, 0))
    for to in range(8):
        d_cut[to] = part[:, to * cut : (to + 1) * cut]
    d_in[owner] = d_cut[owner]
    swap_start(sends, lambda to: d_cut.at[to], d_in, *sems[4:6])
    sums[owner] = jnp.sum(d_mod, axis=0, keepdims=True)
    swap_start(sends, lambda to: sums.at[owner], sums, *sems[6:8])
    yield
    swap_wait(d_in, sems[5])
    total = d_in[0]
    for of in range(1, 8):
        total = total + d_in[of]
    d_cond_cut[owner] = total * silu_parts(cond_cut[owner])[1]
    swap_start(sends, lambda to: d_cond_cut.at[owner], d_cond_cut, *sems[8:10])
    yield
    swap_wait(d_cond_cut, sems[9])
    for of in range(8):
        d_cond_out[:, of * cut : (of + 1) * cut] = d_cond_cut[of]
    d_hid_cut[owner] = fine_dot(d_cond_out[...], second[...], (1, 1)) * time_slope[...]
    swap_start(sends, lambda to: d_hid_cut.at[owner], d_hid_cut, *sems[10:12])
    yield
    swap_wait(d_hid_cut, sems[11])
    swap_wait(sums, sems[7])
    sends.finish()


def takes(refs, *counts):
    refs = list(refs)
    groups = []
    for count in counts:
        groups.append(refs[:count])
        refs = refs[count:]
    assert not refs
    return groups


def call(kernel, number, args, in_specs, outs, out_specs, scratch, name, room):
    return pl.pallas_call(
        kernel,
        out_shape=outs,
        in_specs=in_specs,
        out_specs=out_specs,
        scratch_shapes=scratch,
        compiler_params=pltpu.CompilerParams(
            collective_id=number, has_side_effects=True, vmem_limit_bytes=room * 1024 * 1024
        ),
        name=name,
    )(*args)


def shape(dims, kind):
    return jax.ShapeDtypeStruct(tuple(dims), kind)


def forward_first(w_io, tokens, note, first, second, table, modulation):
    rows, width = second.shape
    wide = modulation.shape[0]

    def kernel(*refs):
        args, outs, scratch, cond_sems, io_sems, token_sems = takes(refs, 7, 8, 5, 10, 3, 3)
        greet(True, True)
        run_all(
            [
                condition_forward(args[2], *args[3:7], outs[2:8], scratch, cond_sems),
                gather_ranks(args[1], outs[1], token_sems),
                gather_owners(args[0], outs[0], io_sems),
            ]
        )

    return call(
        kernel,
        1,
        (w_io, tokens, note, first, second, table, modulation),
        [VMEM] * 7,
        [
            shape((8,) + w_io.shape, LOW),
            shape((4,) + tokens.shape, LOW),
            shape(note.shape, F32),
            shape((8, rows), F32),
            shape((8, rows), F32),
            shape((8, 8, rows), F32),
            shape((8, width), F32),
            shape((8, 1, wide), F32),
        ],
        [HBM] * 2 + [VMEM] * 6,
        [
            pltpu.VMEM((2, 8, 8, rows), F32),
            pltpu.VMEM((8, 8, rows), F32),
            pltpu.VMEM((8, 8, rows), F32),
            pltpu.VMEM((2, 8, 1, rows), F32),
            pltpu.VMEM((8, 1, wide), F32),
        ]
        + SWAP_SEMS * 5
        + GATHER_OWNERS_SEMS
        + GATHER_RANKS_SEMS,
        "forward_first",
        20,
    )


QUERIES = 256


def block_of(index, size=QUERIES):
    return pl.ds(pl.multiple_of(index * size, size), size)


def attend_heads(qkv, mixed, logs, head_rows, heads):
    length = qkv.shape[0]
    span = heads * HD
    scale = 1.0 / math.sqrt(HD)
    for head in range(heads):
        for part in range(3):
            start = part * span + head * HD
            head_rows[part] = qkv[:, start : start + HD]

        def block(index, carry):
            query = head_rows[0, block_of(index)]
            scores = low_dot(head_rows[1], query, (1, 1)) * scale
            top = jnp.max(scores, axis=0, keepdims=True)
            expo = jnp.exp(scores - top)
            total = jnp.sum(expo, axis=0, keepdims=True)
            probs = (expo * (1.0 / total)).astype(LOW)
            mixed[block_of(index), head * HD : (head + 1) * HD] = low_dot(head_rows[2], probs, (0, 0)).T.astype(LOW)
            logs[head, index] = top + jnp.log(total)
            return carry

        lax.fori_loop(0, length // QUERIES, block, 0)
        yield


def attend_heads_back(qkv, logs, d_mixed, d_qkv, head_rows, d_head, d_keys, d_values, heads):
    length = qkv.shape[0]
    span = heads * HD
    scale = 1.0 / math.sqrt(HD)
    for head in range(heads):
        lanes = slice(head * HD, (head + 1) * HD)
        for part in range(3):
            start = part * span + head * HD
            head_rows[part] = qkv[:, start : start + HD]
        d_head[...] = d_mixed[:, lanes]
        d_keys[...] = jnp.zeros_like(d_keys)
        d_values[...] = jnp.zeros_like(d_values)

        def block(index, carry):
            query, d_block = head_rows[0, block_of(index)], d_head[block_of(index)]
            scores = low_dot(head_rows[1], query, (1, 1)) * scale
            probs = jnp.exp(scores - logs[head, index])
            d_probs = low_dot(head_rows[2], d_block, (1, 1))
            delta = jnp.sum(probs * d_probs, axis=0, keepdims=True)
            d_scores = (probs * (d_probs - delta)).astype(LOW)
            d_keys[...] += low_dot(d_scores, query, (1, 0))
            d_values[...] += low_dot(probs.astype(LOW), d_block, (1, 0))
            d_query = low_dot(head_rows[1], d_scores, (0, 0)).T * scale
            d_qkv[block_of(index), lanes] = d_query.astype(LOW)
            return carry

        lax.fori_loop(0, length // QUERIES, block, 0)
        d_qkv[:, span + head * HD : span + (head + 1) * HD] = (d_keys[...] * scale).astype(LOW)
        d_qkv[:, 2 * span + head * HD : 2 * span + (head + 1) * HD] = d_values[...].astype(LOW)
        yield


def beside(blocks, out):
    columns = blocks.shape[2]

    def one(at):
        for part in range(4):
            out[at, part * columns : (part + 1) * columns] = blocks[part, at]

    by_rows(out.shape[0], one)


def forward_attention(qkv, w_up, w_down, upstream, w_io):
    length = qkv.shape[0]
    heads = qkv.shape[1] // (3 * HD)
    span = heads * HD
    width = w_io.shape[0]

    def kernel(*refs):
        args, outs, scratch, up_sems, down_sems, token_sems, out_sems, mixed_sems = takes(refs, 5, 6, 5, 3, 3, 3, 3, 3)
        mixed_here, head_rows, mixed_all, out_here, out_all = scratch
        greet(True, True)

        def attention():
            steps = attend_heads(args[0], mixed_here, outs[5], head_rows, heads)
            for index, _ in enumerate(steps):
                if 0 < index < heads - 1:
                    yield
            yield from gather_ranks(mixed_here, mixed_all, mixed_sems)

        def out_weight():
            out_here[...] = args[4][:, 3 * span :]
            yield from gather_ranks(out_here, out_all, out_sems)
            beside(out_all, outs[3])

        run_all(
            [
                gather_owners(args[1], outs[0], up_sems),
                gather_owners(args[2], outs[1], down_sems),
                out_weight(),
                attention(),
                gather_ranks(args[3], outs[2], token_sems),
            ]
        )
        beside(mixed_all, outs[4])

    return call(
        kernel,
        2,
        (qkv, w_up, w_down, upstream, w_io),
        [VMEM] * 5,
        [
            shape((8,) + w_up.shape, LOW),
            shape((8,) + w_down.shape, LOW),
            shape((4,) + upstream.shape, LOW),
            shape((width, 4 * span), LOW),
            shape((length, 4 * span), LOW),
            shape((heads, length // QUERIES, 1, QUERIES), F32),
        ],
        [HBM] * 3 + [VMEM] * 3,
        [
            pltpu.VMEM((length, span), LOW),
            pltpu.VMEM((3, length, HD), LOW),
            pltpu.VMEM((4, length, span), LOW),
            pltpu.VMEM((width, span), LOW),
            pltpu.VMEM((4, width, span), LOW),
        ]
        + GATHER_OWNERS_SEMS * 2
        + GATHER_RANKS_SEMS * 3,
        "forward_attention",
        40,
    )


def gathers(number, by_owner, by_rank, name):
    if not fast():
        return [lax.all_gather(block, "fsdp", axis=0) for block in by_owner] + [
            lax.all_gather(block, "seq", axis=0) for block in by_rank
        ]
    many, few = len(by_owner), len(by_rank)

    def kernel(*refs):
        groups = takes(refs, many + few, many + few, *[3] * (many + few))
        args, outs, sems = groups[0], groups[1], groups[2:]
        greet(many > 0, few > 0)
        run_all(
            [gather_owners(args[at], outs[at], sems[at]) for at in range(many)]
            + [gather_ranks(args[at], outs[at], sems[at]) for at in range(many, many + few)]
        )

    blocks = list(by_owner) + list(by_rank)
    return call(
        kernel,
        number,
        blocks,
        [VMEM] * len(blocks),
        [shape((8 if at < many else 4,) + block.shape, block.dtype) for at, block in enumerate(blocks)],
        [HBM] * len(blocks),
        GATHER_OWNERS_SEMS * many + GATHER_RANKS_SEMS * few,
        name,
        16,
    )


def rank_sums(number, blocks, name):
    if not fast():
        return [lax.psum_scatter(block.astype(F32), "seq", scatter_dimension=0, tiled=False) for block in blocks]
    many = len(blocks)

    def kernel(*refs):
        groups = takes(refs, many, many, *[7] * many)
        greet(False, True)
        run_all(
            [
                scatter_ranks(groups[0][at], groups[1][at], *groups[2 + at][:4], groups[2 + at][4:])
                for at in range(many)
            ]
        )

    scratch = []
    for block in blocks:
        scratch += scatter_ranks_scratch(*block.shape[1:])
    return call(
        kernel,
        number,
        blocks,
        [HBM] * many,
        [shape(block.shape[1:], F32) for block in blocks],
        [VMEM] * many,
        scratch,
        name,
        16,
    )


def columns_product(left, right, out, first=0):
    count = left.shape[1] // 128

    def one(index, carry):
        at = pl.ds(pl.multiple_of(lax.rem(index + first, count) * 128, 128), 128)
        out[at] = low_dot(left[:, at], right[...], (0, 0)).astype(LOW)
        return carry

    lax.fori_loop(0, count, one, 0)


def sum_feed(part, pairs):
    many = len(pairs)

    def kernel(*refs):
        args, outs, scratch = takes(refs, 1 + 2 * many, 1 + many, 7)
        greet(False, True)

        def products():
            for at in range(many):
                columns_product(args[1 + 2 * at], args[2 + 2 * at], outs[1 + at])
                yield

        run_all([scatter_ranks(args[0], outs[0], *scratch[:4], scratch[4:]), products()])

    return call(
        kernel,
        4,
        (part,) + tuple(array for pair in pairs for array in pair),
        [HBM] + [VMEM] * (2 * many),
        [shape(part.shape[1:], F32)] + [shape((left.shape[1], right.shape[1]), LOW) for left, right in pairs],
        [VMEM] * (1 + many),
        scatter_ranks_scratch(*part.shape[1:]),
        "sum_feed",
        36,
    )


def row_cuts(rows, cuts):
    step = (rows // cuts + 15) // 16 * 16
    return [(start, min(step, rows - start)) for start in range(0, rows, step)]


def together(parts, first):
    parts = list(parts)
    for _ in range(first):
        for part in parts:
            next(part)
    yield
    while parts:
        for part in list(parts):
            try:
                next(part)
            except StopIteration:
                parts.remove(part)
        yield


def scatter_items(parts, outs, scratch, cuts):
    items, at = [], 0
    for part, out in zip(parts, outs):
        height = out.shape[1]
        for start, count in row_cuts(height, cuts):
            refs = scratch[at]

            def block(owner, part=part, start=start, count=count):
                if len(part.shape) == 3:
                    return part.at[owner, pl.ds(start, count)]
                return part.at[pl.ds(pl.multiple_of(owner * height + start, 16), count)]

            items.append(scatter_owners(block, out.at[:, pl.ds(start, count)], *refs[:5], refs[5:]))
            at += 1
    return [together(items, 4)]


def scatter_items_scratch(shapes, cuts):
    scratch = []
    for height, columns in shapes:
        for _, count in row_cuts(height, cuts):
            scratch += scatter_owners_scratch(count, columns)
    return scratch


def backward_attention(g_up, g_down, my_d_attn, mlp_part, qkv, w_out, logs, units):
    length = qkv.shape[0]
    heads = qkv.shape[1] // (3 * HD)
    span = heads * HD
    rows, width = my_d_attn.shape

    def kernel(*refs):
        groups = takes(refs, 7, 6, 6, 7, 3, *[14] * 6)
        args, outs, scratch, sum_scratch, token_sems = groups[:5]
        d_mixed, head_rows, d_head, d_keys, d_values, up_all = scratch
        greet(True, True)

        def attention():
            tokens = gather_ranks(args[2], outs[2], token_sems)
            next(tokens)
            yield
            for _ in tokens:
                pass
            w_rows = args[5][pl.ds(pl.multiple_of(lax.axis_index("seq") * span, 16), span)]
            for part in range(4):
                d_mixed[part * rows : (part + 1) * rows] = low_dot(outs[2][part], w_rows, (1, 1)).astype(LOW)
            yield from attend_heads_back(
                args[4], args[6], d_mixed, outs[4], head_rows, d_head, d_keys, d_values, heads
            )

        run_all(
            scatter_items(args[:2], (up_all, outs[1]), groups[5:], 3)
            + [attention(), scatter_ranks(args[3], outs[3], *sum_scratch[:4], sum_scratch[4:])]
        )
        owners = up_all.shape[2] // units
        outs[5][...] = jnp.zeros_like(outs[5])

        def assemble(at):
            for part in range(4):
                for owner in range(owners):
                    to = (owner * 4 + part) * units
                    outs[0][at, to : to + units] = up_all[part, at, owner * units : (owner + 1) * units]
            add_squares(outs[0][at], outs[5])

        by_rows(up_all.shape[1], assemble)

    return call(
        kernel,
        9,
        (g_up, g_down, my_d_attn, mlp_part, qkv, w_out, logs),
        [HBM, HBM, VMEM, HBM, VMEM, VMEM, VMEM],
        [
            shape((g_up.shape[1], 4 * g_up.shape[2]), LOW),
            shape((4,) + g_down.shape[1:], LOW),
            shape((4,) + my_d_attn.shape, LOW),
            shape(my_d_attn.shape, F32),
            shape(qkv.shape, LOW),
            shape((1, 4 * g_up.shape[2]), F32),
        ],
        [VMEM, HBM, VMEM, VMEM, VMEM, VMEM],
        [
            pltpu.VMEM((length, span), LOW),
            pltpu.VMEM((3, length, HD), LOW),
            pltpu.VMEM((length, HD), LOW),
            pltpu.VMEM((length, HD), F32),
            pltpu.VMEM((length, HD), F32),
            pltpu.VMEM((4,) + g_up.shape[1:], LOW),
        ]
        + scatter_ranks_scratch(rows, width)
        + GATHER_RANKS_SEMS
        + scatter_items_scratch([g_up.shape[1:], g_down.shape[1:]], 3),
        "backward_attention",
        50,
    )


def add_squares(values, box):
    values = values.astype(F32)
    box[...] += jnp.sum(values * values, axis=0, keepdims=True)


def backward_last(h_attn, d_qkv, mixed, d_part, d_tokens, tokens, scale, d_middle, news, second, modulation, cond_cut, time_slope):
    rows, width = second.shape
    span = d_part.shape[1]
    tok_rows = tokens.shape[0]
    wide = modulation.shape[0]

    def kernel(*refs):
        groups = takes(refs, 13, 9, 5, 12, 7, 7, *[14] * 6)
        args, outs, scratch, sems, sum_scratch = groups[:5]
        in_all, out_all, d_sum, edge, news_here, g_in, g_out = groups[5]
        squares, outs = outs[7:], outs[:7]
        products, args = args[:4], args[2:]
        greet(True, True)

        def condition():
            yield from scatter_ranks(args[2], d_sum, *sum_scratch[:4], sum_scratch[4:])
            edge[...] = jnp.zeros_like(edge)

            def one(at):
                value = args[3][at].astype(F32)
                norm, inverse = layer_norm(value)
                grad = d_sum[at]
                edge[0] += jnp.sum(grad.reshape(2, 8, width), axis=0)
                edge[1] += jnp.sum((grad * norm).reshape(2, 8, width), axis=0)
                outs[2][at] = args[5][at] + layer_norm_back(norm, inverse, grad * (1.0 + args[4][...]))

            by_rows(tok_rows, one)
            news_here[...] = args[6][...]
            line = jnp.concatenate(
                [jnp.sum(edge[0], axis=0, keepdims=True), jnp.sum(edge[1], axis=0, keepdims=True)], axis=1
            )
            at = 0
            while at * wide < 2 * width:
                end = min((at + 1) * wide, 2 * width)
                news_here[at, :, : end - at * wide] = line[:, at * wide : end]
                at += 1
            yield from condition_backward(news_here, *args[7:], outs[3:], scratch, sems)

        def gradients():
            columns_product(products[2], products[3], g_out, 5)
            yield
            columns_product(products[0], products[1], g_in, 5)
            yield from scatter_items((g_in, g_out), (in_all, out_all), groups[6:], 3)[0]

        run_all([condition(), gradients()])
        for box in squares:
            box[...] = jnp.zeros_like(box)

        def assemble(at):
            for part in range(4):
                for block in range(3):
                    to = (block * 4 + part) * span
                    outs[0][at, to : to + span] = in_all[part, at, block * span : (block + 1) * span]
                outs[1][at, part * span : (part + 1) * span] = out_all[part, at]
            add_squares(outs[0][at], squares[0])
            add_squares(outs[1][at], squares[1])

        by_rows(rows, assemble)

    return call(
        kernel,
        8,
        (h_attn, d_qkv, mixed, d_part, d_tokens, tokens, scale, d_middle, news, second, modulation, cond_cut, time_slope),
        [VMEM] * 4 + [HBM] + [VMEM] * 8,
        [
            shape((rows, 12 * span), LOW),
            shape((rows, 4 * span), LOW),
            shape(tokens.shape, F32),
            shape(news.shape, F32),
            shape((8, width), F32),
            shape((8, 8, rows), F32),
            shape((8, 1, wide), F32),
            shape((1, 12 * span), F32),
            shape((1, 4 * span), F32),
        ],
        [VMEM] * 9,
        [
            pltpu.VMEM((4,) + news.shape, F32),
            pltpu.VMEM(news.shape, F32),
            pltpu.VMEM((8, 8, rows), F32),
            pltpu.VMEM((8, 8, rows), F32),
            pltpu.VMEM((8, 8, rows), F32),
            DMA((3,)),
            DMA((4,)),
        ]
        + SWAP_SEMS * 5
        + scatter_ranks_scratch(tok_rows, width)
        + [
            pltpu.VMEM((4, rows, 3 * span), LOW),
            pltpu.VMEM((4, rows, span), LOW),
            pltpu.VMEM((tok_rows, width), F32),
            pltpu.VMEM((2, 8, width), F32),
            pltpu.VMEM(news.shape, F32),
            pltpu.VMEM((width, 3 * span), LOW),
            pltpu.VMEM((width, span), LOW),
        ]
        + scatter_items_scratch([(rows, 3 * span), (rows, span)], 3),
        "backward_last",
        52,
    )


def pick_weights(attend_in, attend_out, expand, rank, span, units):
    rows = attend_in.shape[0]
    owners = expand.shape[1] // (4 * units)
    if not fast():
        w_in = pick(attend_in.reshape(rows, 3, 4, span), rank, 2).astype(LOW).reshape(rows, 3 * span)
        w_up = pick(expand.reshape(rows, owners, 4, units), rank, 2).astype(LOW).reshape(rows, owners * units)
        return jnp.concatenate([w_in, mine(attend_out, 1, 4, rank).astype(LOW)], axis=1), w_up

    def kernel(in_ref, out_ref, up_ref, io, up):
        here = lax.axis_index("seq")
        for part in range(4):

            @pl.when(here == part)
            def _(part=part):
                def one(at):
                    for block in range(3):
                        start = (block * 4 + part) * span
                        io[at, block * span : (block + 1) * span] = in_ref[at, start : start + span].astype(LOW)
                    io[at, 3 * span :] = out_ref[at, part * span : (part + 1) * span].astype(LOW)
                    for owner in range(owners):
                        start = (owner * 4 + part) * units
                        up[at, owner * units : (owner + 1) * units] = up_ref[at, start : start + units].astype(LOW)

                by_rows(rows, one)

    return pl.pallas_call(
        kernel,
        out_shape=[shape((rows, 4 * span), LOW), shape((rows, owners * units), LOW)],
        in_specs=[VMEM] * 3,
        out_specs=[VMEM] * 2,
        compiler_params=pltpu.CompilerParams(vmem_limit_bytes=32 * 1024 * 1024),
        name="pick_weights",
    )(attend_in, attend_out, expand)


def sum_owners(number, value, name):
    if not fast():
        return lax.psum(value, "fsdp")

    def kernel(src, out, boxes, *sems):
        owner = lax.axis_index("fsdp")
        greet(True, False)
        sends = Sends()
        boxes[owner] = src[...]
        swap_start(sends, lambda to: src, boxes, *sems)
        swap_wait(boxes, sems[1])
        total = boxes[0]
        for of in range(1, 8):
            total = total + boxes[of]
        out[...] = total
        sends.finish()

    block = jnp.full((8, 128), value, F32)
    total = call(
        kernel, number, (block,), [VMEM], shape((8, 128), F32), VMEM, [pltpu.VMEM((8, 8, 128), F32)] + SWAP_SEMS, name, 4
    )
    return total[0, 0]


def attend(query, keys, values):
    score_scale = 1.0 / math.sqrt(keys.shape[-1])
    scores = mixed_dot("qhd,khd->hqk", query, keys) * score_scale
    top = jnp.max(scores, axis=-1, keepdims=True)
    expo = jnp.exp(scores - top)
    total = jnp.sum(expo, axis=-1, keepdims=True)
    probs = (expo / total).astype(LOW)
    mixed = mixed_dot("hqk,khd->qhd", probs, values)
    return mixed.astype(LOW), (top + jnp.log(total))[..., 0]


def attend_back(query, keys, values, d_mixed, log_total):
    length, heads_here, head_dim = query.shape
    block = min(512, length)
    count = length // block
    score_scale = 1.0 / math.sqrt(head_dim)

    def back_block(carry, pieces):
        d_keys, d_values = carry
        query_block, d_block, log_block = pieces
        scores = mixed_dot("qhd,khd->hqk", query_block, keys) * score_scale
        probs = jnp.exp(scores - log_block[..., None])
        d_probs = mixed_dot("qhd,khd->hqk", d_block, values)
        delta = jnp.sum(probs * d_probs, axis=-1, keepdims=True)
        d_scores = (probs * (d_probs - delta)).astype(LOW)
        d_query = mixed_dot("hqk,khd->qhd", d_scores, keys) * score_scale
        d_keys = d_keys + mixed_dot("hqk,qhd->khd", d_scores, query_block) * score_scale
        d_values = d_values + mixed_dot("hqk,qhd->khd", probs.astype(LOW), d_block)
        return ((d_keys, d_values), d_query)

    empty = jnp.zeros((length, heads_here, head_dim), jnp.float32)
    blocked = (count, block, heads_here, head_dim)
    logs = log_total.reshape(heads_here, count, block).transpose(1, 0, 2)
    (d_keys, d_values), d_query = lax.scan(
        back_block, (empty, empty), (query.reshape(blocked), d_mixed.reshape(blocked), logs)
    )
    flat = (length, heads_here * head_dim)
    return jnp.concatenate(
        [d_query.reshape(flat), d_keys.reshape(flat), d_values.reshape(flat)], axis=1
    ).astype(LOW)


def adam_step(weight, moment, square, gradient, factor):
    clipped = gradient * factor
    moment_next = beta_one * moment + (1.0 - beta_one) * clipped
    square_next = beta_two * square + (1.0 - beta_two) * clipped * clipped
    moment_hat = moment_next / (1.0 - beta_one**STEP)
    square_hat = square_next / (1.0 - beta_two**STEP)
    master = weight - learn_rate * (
        moment_hat / (jnp.sqrt(square_hat) + adam_eps) + weight_decay * weight
    )
    return (master, moment_next, square_next)


def condition_start(latent_tokens, w_io, biases, timesteps, labels, time_first, time_second, class_table, modulation):
    owners, owner = lax.axis_size("fsdp"), lax.axis_index("fsdp")
    share = biases.shape[0]
    width = time_first.shape[1]
    first, second = time_first.astype(LOW), time_second.astype(LOW)
    table, modulation_low = class_table.astype(LOW), modulation.astype(LOW)
    units = first.shape[0]
    bias_low = biases.astype(LOW).astype(F32)
    features = time_features(timesteps).astype(LOW)
    if fast():
        note = jnp.concatenate(
            [
                jnp.broadcast_to(bias_low, (owners, share)),
                features.astype(F32).reshape(owners, units),
                jnp.broadcast_to(labels.astype(F32), (owners, 1)),
                jnp.zeros((owners, 127 - units), F32),
            ],
            axis=1,
        )[:, None]
        w_io_all, tokens, notes, act, slope, cond_cut, cond, mod = forward_first(
            w_io, latent_tokens, note, first, second, table.T, modulation_low.T
        )
        notes = notes[:, 0]
        all_bias = notes[:, :share].reshape(owners * share)
        my_features = notes[:, share : share + units]
        all_labels = notes[:, share + units]
        mod_values = mod.reshape(owners * mod.shape[2])
        state = (first, second, modulation_low, my_features, all_labels, act, slope, cond_cut, cond)
        return w_io_all, tokens, all_bias, mod_values, state
    w_io_all = lax.all_gather(w_io, "fsdp", axis=0)
    tokens = lax.all_gather(latent_tokens, "seq", axis=0)
    note = jnp.concatenate([bias_low, features[0].astype(F32), labels.astype(F32)])
    notes = lax.all_gather(note, "fsdp", axis=0)
    all_bias = notes[:, :share].reshape(owners * share)
    my_features = mine(notes[:, share:-1], 1, owners, owner)
    all_labels = notes[:, -1]
    hidden_time = lax.psum(mixed_dot("bf,fd->bd", my_features.astype(LOW), first), "fsdp") + all_bias[:width]
    act, slope = silu_parts(mine(hidden_time, 1, owners, owner))
    act = act.astype(LOW)
    onehot = (all_labels[:, None] == jnp.arange(NCLS, dtype=F32)[None, :]).astype(LOW)
    cond_part = mixed_dot("bd,de->be", act, second)
    class_part = mixed_dot("bc,cd->bd", onehot, table)
    class_wide = lax.dynamic_update_slice(jnp.zeros_like(cond_part), class_part, (0, owner * class_part.shape[1]))
    cond = lax.psum(cond_part + class_wide, "fsdp") + all_bias[width : 2 * width]
    mod_part = mixed_dot("bd,de->be", silu_parts(cond)[0].astype(LOW), modulation_low)
    mod_values = pick(lax.all_gather(mod_part, "fsdp", axis=0), owner, 1).reshape(owners * mod_part.shape[1])
    state = (first, second, modulation_low, my_features, all_labels, act.astype(F32), slope, None, cond)
    return w_io_all, tokens, all_bias, mod_values, state


def owner_sums(blocks):
    summed = [lax.psum_scatter(block.astype(F32), "fsdp", scatter_dimension=0, tiled=False) for block in blocks]
    return [lax.all_gather(block.astype(LOW), "seq", axis=0) for block in summed]


def condition_end(state, h_attn, d_qkv, mixed, d_part, d_tokens, tokens, scale1, d_middle, d_mod_rest, tail, share):
    first, second, modulation_low, my_features, all_labels, act, slope, cond_cut, cond = state
    owners, owner, rank = lax.axis_size("fsdp"), lax.axis_index("fsdp"), lax.axis_index("seq")
    wide, width = modulation_low.shape[1], cond.shape[1]
    blank = jnp.zeros((2 * width,), F32)
    if fast():
        pad = -wide % 128
        tails = jnp.concatenate([jnp.zeros((owners * share - tail.shape[0],), F32), tail]).reshape(owners, share)
        news = jnp.concatenate(
            [jnp.concatenate([blank, d_mod_rest]).reshape(owners, wide), jnp.zeros((owners, pad), F32), tails], axis=1
        )[:, None]
        grad_in, grad_out, input_gradient, by_latent, d_cond, d_hid, sums, *squares = backward_last(
            h_attn, d_qkv, mixed, d_part, d_tokens, tokens, scale1, d_middle, news, second, modulation_low.T, cond_cut, slope
        )
        d_mod = by_latent[:, 0, :wide]
        my_tail = jnp.sum(by_latent[:, 0, wide + pad :], axis=0)
        d_hidden = d_hid.transpose(1, 0, 2).reshape(owners, width)
        front = jnp.concatenate([jnp.sum(d_hidden, axis=0), jnp.sum(d_cond, axis=0), sums.reshape(owners * wide)])
        count = front.shape[0] // share
        grad_bias = jnp.where(
            owner < count, pick(front.reshape(count, share), jnp.minimum(owner, count - 1)), my_tail
        )
    else:
        (d_hattn,) = rank_sums(6, [d_tokens], "sums")
        norm, inverse = layer_norm(tokens.astype(F32))
        input_gradient = d_middle + layer_norm_back(norm, inverse, d_hattn * (1.0 + scale1))
        my_d_mod = jnp.concatenate([jnp.sum(d_hattn, axis=0), jnp.sum(d_hattn * norm, axis=0), d_mod_rest])
        by_owner = lambda block: block.astype(LOW).reshape((owners, -1) + block.shape[1:])
        grad_in, grad_out = owner_sums(
            [by_owner(mixed_dot("td,te->de", h_attn, d_qkv)), by_owner(mixed_dot("td,te->de", mixed, d_part))]
        )
        rows, span = grad_out.shape[1], grad_out.shape[2]
        grad_in = grad_in.reshape(4, rows, 3, span).transpose(1, 2, 0, 3).reshape(rows, 12 * span)
        grad_out = grad_out.transpose(1, 0, 2).reshape(rows, 4 * span)
        squares = [grad.astype(F32) * grad.astype(F32) for grad in (grad_in, grad_out)]
        all_d_mod = lax.all_gather(lax.psum(my_d_mod, "seq"), "fsdp", axis=0)
        d_mod = mine(all_d_mod, 1, owners, owner)
        part = high_dot(d_mod, modulation_low.astype(F32).T)
        d_cond = lax.psum(part, "fsdp") * silu_parts(cond)[1]
        d_time = high_dot(d_cond, second.astype(F32).T) * slope
        d_hidden = lax.all_gather(d_time, "fsdp", axis=0).transpose(1, 0, 2).reshape(owners, width)
        tail = lax.psum(tail, ("seq", "fsdp"))
        all_bias = jnp.concatenate(
            [jnp.sum(d_hidden, axis=0), jnp.sum(d_cond, axis=0), jnp.sum(all_d_mod, axis=0), tail]
        )
        grad_bias = mine(all_bias, 0, owners, owner)
    onehot = (all_labels[:, None] == jnp.arange(NCLS, dtype=F32)[None, :]).astype(F32)
    cond_act = silu_parts(cond)[0].astype(LOW).astype(F32)
    grad_mod = high_dot(cond_act.T, d_mod)
    grad_class = high_dot(onehot.T, mine(d_cond, 1, owners, owner))
    grad_second = high_dot(act.T, d_cond)
    grad_first = high_dot(my_features.T, d_hidden)
    condition_gradient = lax.dynamic_slice_in_dim(d_cond, owner, 1, 0)
    return grad_in, grad_out, squares, input_gradient, (grad_first, grad_second, grad_class, grad_mod), grad_bias, condition_gradient


def per_device(latents, timesteps, labels, upstream, *state):
    params, moments, squares = state[:9], state[9:18], state[18:]
    time_first, time_second, class_table, modulation, attend_in, attend_out, expand, contract, biases = params
    lat_dev, tok_rows, width = latents.shape
    assert lat_dev == 1
    hidden = expand.shape[1]
    ranks = lax.axis_size("seq")
    owners = lax.axis_size("fsdp")
    rank = lax.axis_index("seq")
    heads_here = H // ranks
    span = heads_here * HD
    length = ranks * tok_rows
    rows = width // owners
    unit = hidden // (owners * ranks)
    hid_here = owners * unit

    my_io, my_up = pick_weights(attend_in, attend_out, expand, rank, span, unit)
    my_down = mine(contract, 0, ranks, rank).astype(LOW)
    w_io, tokens, all_bias, mod_values, kept = condition_start(
        latents[0], my_io, biases, timesteps, labels, time_first, time_second, class_table, modulation
    )
    w_io = w_io.reshape(width, 4 * span)
    w_in = w_io[:, : 3 * span]
    inputs_low = tokens.reshape(length, width)

    b_t1, b_t2, b_mod, b_q, b_v, b_out, b_up, b_down = split_biases(all_bias, width, hidden)
    mod_values = (mod_values + b_mod).reshape(6, 1, width)
    shift1, scale1, gate1, shift2, scale2, gate2 = [mod_values[index] for index in range(6)]

    inputs = inputs_low.astype(F32)
    norm_one, _ = layer_norm(inputs)
    h_attn = (norm_one * (1.0 + scale1) + shift1).astype(LOW)
    my_b_q, my_b_v = mine(b_q, 0, ranks, rank), mine(b_v, 0, ranks, rank)
    qkv_bias = jnp.concatenate([my_b_q, jnp.zeros_like(my_b_q), my_b_v])
    qkv = (mixed_dot("td,de->te", h_attn, w_in) + qkv_bias).astype(LOW)
    head_shape = (length, heads_here, HD)
    if fast():
        w_up, w_down, d_out_low, w_out, mixed, logs = forward_attention(
            qkv, my_up, my_down, upstream[0], w_io
        )
    else:
        query, keys, values = [qkv[:, part * span : (part + 1) * span].reshape(head_shape) for part in range(3)]
        mixed_heads, logs = attend(query, keys, values)
        w_up, w_down, d_out_low, w_out, mixed = gathers(
            2, [my_up, my_down], [upstream[0], w_io[:, 3 * span :], mixed_heads.reshape(length, span)], "gathers"
        )
        w_out = w_out.transpose(1, 0, 2).reshape(width, width)
        mixed = mixed.transpose(1, 0, 2).reshape(length, width)
    w_up, w_down = w_up.reshape(width, hid_here), w_down.reshape(hid_here, width)
    d_out_low = d_out_low.reshape(length, width)
    attn_out = mixed_dot("td,de->te", mixed, w_out) + b_out
    middle = inputs + gate1 * attn_out
    norm_two, inverse_two = layer_norm(middle)
    h_mlp = (norm_two * (1.0 + scale2) + shift2).astype(LOW)

    my_b_up = pick(b_up.reshape(owners, ranks, unit), rank, 1).reshape(hid_here)
    pre_act = mixed_dot("td,df->tf", h_mlp, w_up) + my_b_up
    act_f, gelu_pull = jax.vjp(partial(jax.nn.gelu, approximate=True), pre_act)
    act = act_f.astype(LOW)
    by_rank = (ranks, tok_rows, width)
    by_owner = lambda block: block.astype(LOW).reshape((owners, -1) + block.shape[1:])
    mlp_part = mixed_dot("tf,fd->td", act, w_down).astype(LOW).reshape(by_rank)
    d_out = d_out_low.astype(F32)
    d_mlp = (d_out * gate2).astype(LOW)
    d_act = mixed_dot("td,fd->tf", d_mlp, w_down)
    d_pre = gelu_pull(d_act)[0].astype(LOW)
    d_hmlp_part = mixed_dot("tf,df->td", d_pre, w_up).astype(LOW).reshape(by_rank)
    if fast():
        d_hmlp, g_down, g_up = sum_feed(d_hmlp_part, [(act, d_mlp), (h_mlp, d_pre)])
        g_down, g_up = by_owner(g_down), by_owner(g_up)
    else:
        (d_hmlp,) = rank_sums(4, [d_hmlp_part], "sums")
        g_down = by_owner(mixed_dot("tf,td->fd", act, d_mlp))
        g_up = by_owner(mixed_dot("td,tf->df", h_mlp, d_pre))
    gb_up = jnp.sum(d_pre.astype(F32), axis=0)
    gb_down = jnp.sum(d_mlp.astype(F32), axis=0)

    own = lambda array: mine(array, 0, ranks, rank)
    my_attn_out, my_middle, my_norm_two, my_inverse_two = own(attn_out), own(middle), own(norm_two), own(inverse_two)
    my_d_out = upstream[0].astype(F32)
    d_shift2 = jnp.sum(d_hmlp, axis=0)
    d_scale2 = jnp.sum(d_hmlp * my_norm_two, axis=0)
    d_middle = my_d_out + layer_norm_back(my_norm_two, my_inverse_two, d_hmlp * (1.0 + scale2))
    d_gate1 = jnp.sum(d_middle * my_attn_out, axis=0)
    my_d_attn = (d_middle * gate1).astype(LOW)
    if fast():
        grad_up, grad_down, d_attn, mlp_sum, d_qkv, up_squares = backward_attention(
            g_up, g_down, my_d_attn, mlp_part, qkv, w_out, logs, unit
        )
        d_attn = d_attn.reshape(length, width)
    else:
        (mlp_sum,) = rank_sums(5, [mlp_part], "sums")
        (d_attn,) = gathers(5, [], [my_d_attn], "gathers")
        d_attn = d_attn.reshape(length, width)
        d_mixed = mixed_dot("te,de->td", d_attn, mine(w_out, 0, ranks, rank)).astype(LOW)
        d_qkv = attend_back(query, keys, values, d_mixed.reshape(head_shape), logs)
        grad_up, grad_down = owner_sums([g_up, g_down])
        grad_up = grad_up.reshape(ranks, rows, owners, unit).transpose(1, 2, 0, 3).reshape(rows, hidden)
        up_squares = grad_up.astype(F32) * grad_up.astype(F32)
    mlp_out = mlp_sum + b_down
    output = (my_middle + gate2 * mlp_out).astype(LOW)
    d_gate2 = jnp.sum(my_d_out * mlp_out, axis=0)
    d_part = mine(d_attn, 1, ranks, rank)
    d_hattn_part = mixed_dot("te,de->td", d_qkv, w_in).astype(LOW).reshape(by_rank)
    d_mod_rest = jnp.concatenate([d_gate1, d_shift2, d_scale2, d_gate2])
    gb_qv = jnp.sum(d_qkv.astype(F32), axis=0)
    wide = lambda part, size: lax.dynamic_update_slice(jnp.zeros((size,), F32), part, (rank * part.shape[0],))
    gb_up_wide = lax.dynamic_update_slice(
        jnp.zeros((owners, ranks, unit), F32), gb_up.reshape(owners, 1, unit), (0, rank, 0)
    ).reshape(hidden)
    gb_tail = jnp.concatenate(
        [
            wide(gb_qv[:span], width),
            wide(gb_qv[2 * span :], width),
            jnp.sum(my_d_attn.astype(F32), axis=0),
            gb_up_wide,
            jnp.where(rank == 0, gb_down, 0.0),
        ]
    )
    grad_in, grad_out, squares_io, input_gradient, small_grads, grad_bias, condition_gradient = condition_end(
        kept, h_attn, d_qkv, mixed, d_part, d_hattn_part, latents[0], scale1, d_middle, d_mod_rest, gb_tail, biases.shape[0]
    )
    grad_in, grad_out, grad_up, grad_down = [grad.astype(F32) for grad in (grad_in, grad_out, grad_up, grad_down)]
    grad_down = grad_down.reshape(contract.shape)
    gradients = small_grads + (grad_in, grad_out, grad_up, grad_down, grad_bias)
    local_sum = sum(jnp.sum(gradient * gradient) for gradient in small_grads + (grad_down, grad_bias))
    local_sum = local_sum + sum(jnp.sum(box) for box in [up_squares] + list(squares_io))
    norm_before = jnp.sqrt(sum_owners(7, local_sum, "sum_squares"))
    factor = clip_limit / jnp.maximum(norm_before, clip_limit)
    results = [
        adam_step(params[index], moments[index], squares[index], gradients[index], factor)
        for index in range(9)
    ]
    return (
        (output[None], input_gradient[None], condition_gradient, norm_before)
        + gradients
        + tuple(result[0] for result in results)
        + tuple(result[1] for result in results)
        + tuple(result[2] for result in results)
    )


def solution(mesh):
    tokens = P("fsdp", "seq", None)
    rows, columns = P("fsdp", None), P(None, "fsdp")
    weights = (rows, rows, columns, columns, rows, rows, rows, rows, P("fsdp"))
    return jax.shard_map(
        per_device,
        mesh=mesh,
        in_specs=(tokens, P("fsdp"), P("fsdp"), tokens) + weights * 3,
        out_specs=(tokens, tokens, rows, P()) + weights * 4,
        check_vma=False,
    )
```
